256 devices in a mesh: dom: 8 (over y, x_lo), sub: 32 (over z, x_hi, core).
Axes of the slice: x: 4 (x_hi: 2, x_lo: 2; x = x_hi * 2 + x_lo), y: 4, z: 8, core: 2. Of those that a mesh axis runs over, the one named last changes fastest.
Arguments:
- fine_residual: float32 [3, 1048576], P(None, ('dom', 'sub')), may hold values from -6 to 6
- bonds: bfloat16 [32, 3, 3, 1048576], P(None, None, None, ('dom', 'sub')), may hold values from -0.3125 to 0.3125
- bond_col: int32 [32, 1048576], P(None, ('dom', 'sub')), may hold values from 0 to 5119, as said below
- ghost_points: int32 [256, 2, 512], P(('dom', 'sub')), may hold values from -1 to 4095, as said below
- fine_dinv: float32 [3, 3, 1048576], P(None, None, ('dom', 'sub')), may hold values from -0.2 to 1.6
- aggregate: int32 [1048576], P(('dom', 'sub')), may hold values from 0 to 131071, as said below
- coarse_dinv: float32 [3, 3, 131072], P(None, None, 'sub'), may hold values from -0.071 to 0.566
- coarse_couple: float32 [4, 131072], P(None, 'sub'), may hold values from 0.08 to 0.24
Outputs:
- preconditioned: float32 [3, 1048576], P(None, ('dom', 'sub'))
The draws below stay inside these ranges and needn't reach their ends.
Inputs may be any that keep to these rules, and one draw needn't show every extreme that they name: ghost_points[r, 0, :] lists distinct local points of the previous run of r, ghost_points[r, 1, :] of the next run; each list holds 128 to 512 entries, followed by -1; in every draw some run has both lists full. bond_col[0, i] is i's own local index; a column below 4096 is a local point of the run, 4096 + s names slot s from the previous run and 4608 + s slot s from the next run; only slots that hold a point are named. A point of a run with sub-partition index s lies in an aggregate s * 4096 to (s + 1) * 4096 - 1.
All inputs are finite; a program needn't handle non-finite values.
Results may differ from the reference program's by a relative error of at most 0.0014.
Values may be sent and summed in bfloat16 or wider, within the bound.
No kernel may reach another device: no remote copies, remote signals or barrier semaphores. Data moves between devices by JAX's collectives and lax.ppermute only.
A program may use at most 64 MiB of HBM per device.

```python
import math
import jax
import jax.numpy as jnp
from jax import lax

PTS_DEV = 4096
K = 32
AGG = 8
SWEEPS = 3
JAC = 6
PARTS_SIZE = 8
SUBS = 32
RUNS = 256
GCAP = 512
NPTS = 1048576
CPD = 4096
NC = 131072


def ghost_layout(key):
    base_key = jax.random.fold_in(key, 11)
    key_counts, key_full, key_perm, key_cols = jax.random.split(base_key, 4)
    lowest = max(GCAP // 4, 1)
    counts = jax.random.randint(key_counts, (RUNS, 2), lowest, GCAP + 1)
    full_run = jax.random.randint(key_full, (), 0, RUNS)
    counts = counts.at[full_run].set(GCAP)
    perm_keys = jax.random.split(key_perm, RUNS * 2)
    perms = jax.vmap(lambda one_key: jax.random.permutation(one_key, PTS_DEV))(perm_keys)
    perms = perms.reshape(RUNS, 2, PTS_DEV)[:, :, :GCAP]
    slots = jnp.arange(GCAP)
    ghosts = jnp.where(slots[None, None, :] < counts[:, :, None], perms, -1).astype(jnp.int32)
    points = jnp.arange(NPTS)
    run_of = points // PTS_DEV
    local_of = points % PTS_DEV
    count_prev = counts[run_of, 0]
    count_next = counts[run_of, 1]
    span = PTS_DEV + count_prev + count_next
    raw = jax.random.randint(key_cols, (K - 1, NPTS), 0, 1 << 24) % span[None, :]
    mapped = jnp.where(raw < PTS_DEV + count_prev[None, :], raw, raw - count_prev[None, :] + GCAP)
    columns = jnp.concatenate([local_of[None, :], mapped], axis=0)
    columns = columns.at[K - 1, full_run * PTS_DEV].set(PTS_DEV + 2 * GCAP - 1)
    return (ghosts, columns.astype(jnp.int32))


def draw_ghost_points(key, part):
    return ghost_layout(key)[0]


def draw_bond_col(key, part):
    return ghost_layout(key)[1]


def draw_aggregate(key, part):
    inner = jax.random.fold_in(key, 23)
    points = jnp.arange(NPTS)
    group = points // PTS_DEV % SUBS
    local_ids = jax.random.randint(inner, (NPTS,), 0, CPD)
    result = group * CPD + local_ids
    result = result.at[0].set(0)
    result = result.at[NPTS - 1].set(NC - 1)
    return result.astype(jnp.int32)


def block_scaling(key, count, scale):
    key_diag, key_off = jax.random.split(key)
    diagonal = jnp.exp(jax.random.uniform(key_diag, (3, count), jnp.float32, jnp.log(0.6), jnp.log(1.6)))
    offdiag = jax.random.uniform(key_off, (3, 3, count), jnp.float32, -0.2, 0.2)
    identity = jnp.eye(3, dtype=jnp.float32)[:, :, None]
    return scale * (identity * diagonal[None, :, :] + (1.0 - identity) * offdiag)


def draw_fine_dinv(key, part):
    return block_scaling(jax.random.fold_in(key, 31), NPTS, 1.0)


def draw_coarse_dinv(key, part):
    return block_scaling(jax.random.fold_in(key, 37), NC, 1.0 / AGG ** 0.5)


def block_scale(own_key, extent, cuts, least, largest):
    factor_of, own = 1.0, jax.random.fold_in(own_key, 6)
    for position, shards_of in cuts:
        draws = jnp.exp(jax.random.uniform(jax.random.fold_in(own, position), (shards_of,), jnp.float32, least / len(cuts), largest / len(cuts)))
        factor_of = factor_of * jnp.repeat(draws, extent[position] // shards_of).reshape([-1 if axis == position else 1 for axis in range(len(extent))])
    return factor_of


def scatter_about(rng, shape, deviation, limit, cuts=(), kind=jnp.bfloat16):
    level = block_scale(rng, shape, cuts, -0.22, 0.18) if cuts else 1.0
    values = jax.random.normal(rng, shape, jnp.float32) * deviation * level
    return jnp.minimum(jnp.maximum(values, -limit), limit).astype(kind)


def setup_inputs(seed: int = 0) -> dict:
    arg_keys = jax.random.split(jax.random.key(seed), 9)
    return {
        "fine_residual": scatter_about(arg_keys[0], (3, NPTS), 1.0, 6.0, ((1, 256),), jnp.float32),
        "bonds": scatter_about(arg_keys[1], (K, 3, 3, NPTS), (12 * K) ** -0.5, 0.3125, ((3, 256),)),
        "bond_col": draw_bond_col(jax.random.fold_in(arg_keys[8], 71), 0),
        "ghost_points": draw_ghost_points(jax.random.fold_in(arg_keys[8], 71), 0),
        "fine_dinv": draw_fine_dinv(jax.random.fold_in(arg_keys[8], 71), 0),
        "aggregate": draw_aggregate(jax.random.fold_in(arg_keys[8], 71), 0),
        "coarse_dinv": draw_coarse_dinv(jax.random.fold_in(arg_keys[8], 71), 0),
        "coarse_couple": jnp.clip(jnp.exp(math.log(0.24) - 1.0986123 * jax.random.uniform(arg_keys[7], (4, NC), jnp.float32) ** block_scale(arg_keys[7], (4, NC), ((1, 32),), -0.2, 0.2)), 0.08, 0.24),
    }


LOW_EIG = 0.3
HIGH_EIG = 2.2


def point_solve(matrix, vector):
    return jnp.sum(matrix * vector[None, :, :], axis=1)


def bond_apply(field_in, bonds, bond_col, ghost_points):
    rounded = field_in.astype(jnp.bfloat16)
    blocked = rounded.reshape(3, PARTS_SIZE, SUBS, PTS_DEV).transpose(1, 2, 0, 3)
    previous = jnp.roll(blocked, 1, axis=1)
    following = jnp.roll(blocked, -1, axis=1)
    requested = ghost_points.reshape(PARTS_SIZE, SUBS, 2, GCAP)

    def choose_points(source, wanted):
        clamped = jnp.maximum(wanted, 0).astype(jnp.int32)
        picked = jnp.take_along_axis(source, clamped[:, :, None, :], axis=3)
        return jnp.where(wanted[:, :, None, :] >= 0, picked, jnp.zeros_like(picked))

    extended = jnp.concatenate([blocked, choose_points(previous, requested[:, :, 0]), choose_points(following, requested[:, :, 1])], axis=3)
    extended = extended.reshape(RUNS, 3, PTS_DEV + 2 * GCAP)

    def one_run(run_index):
        start = (run_index * PTS_DEV).astype(jnp.int32)
        columns = lax.dynamic_slice_in_dim(bond_col, start, PTS_DEV, 1)
        blocks = lax.dynamic_slice_in_dim(bonds, start, PTS_DEV, 3).astype(jnp.float32)
        gathered = extended[run_index][:, columns].astype(jnp.float32)
        return jnp.einsum("kcep,ekp->cp", blocks, gathered)

    result = lax.map(one_run, jnp.arange(RUNS, dtype=jnp.int32))
    return result.transpose(1, 0, 2).reshape(3, NPTS)


def reference(fine_residual, bonds, bond_col, ghost_points, fine_dinv, aggregate, coarse_dinv, coarse_couple):
    center_eig = (HIGH_EIG + LOW_EIG) / 2.0
    half_range = (HIGH_EIG - LOW_EIG) / 2.0
    factor = half_range / center_eig
    update = point_solve(fine_dinv, fine_residual) / center_eig
    smoothed = update
    for iteration in range(SWEEPS):
        remainder = fine_residual - smoothed - bond_apply(smoothed, bonds, bond_col, ghost_points)
        factor_new = 1.0 / (2.0 * center_eig / half_range - factor)
        update = (factor_new * factor) * update + (2.0 * factor_new / half_range) * point_solve(fine_dinv, remainder)
        smoothed = smoothed + update
        factor = factor_new
    coarse_rhs = jax.vmap(lambda component: jax.ops.segment_sum(component, aggregate, num_segments=NC))(fine_residual)
    coarse_base = point_solve(coarse_dinv, coarse_rhs)
    coarse = coarse_base
    couple_grid = coarse_couple.reshape(4, SUBS, CPD)
    for iteration in range(JAC - 1):
        coarse_grid = coarse.reshape(3, SUBS, CPD)
        zero_row = jnp.zeros((3, 1, CPD), jnp.float32)
        zero_col = jnp.zeros((3, SUBS, 1), jnp.float32)
        below = jnp.concatenate([zero_row, coarse_grid[:, :-1]], axis=1)
        above = jnp.concatenate([coarse_grid[:, 1:], zero_row], axis=1)
        before = jnp.concatenate([zero_col, coarse_grid[:, :, :-1]], axis=2)
        after = jnp.concatenate([coarse_grid[:, :, 1:], zero_col], axis=2)
        coupled = couple_grid[0] * below + couple_grid[1] * above + couple_grid[2] * before + couple_grid[3] * after
        coarse = coarse_base + coupled.reshape(3, NC)
    return smoothed + coarse[:, aggregate]
```

```python
import functools

import jax
import jax.numpy as jnp
from jax import lax
from jax.experimental import pallas as pl
from jax.experimental.pallas import tpu as pltpu
from jax.sharding import PartitionSpec as P

SWEEPS = 3
JAC = 6
LOW_EIG = 0.3
HIGH_EIG = 2.2
CENTER = (HIGH_EIG + LOW_EIG) / 2.0
HALF = (HIGH_EIG - LOW_EIG) / 2.0
LANES = 128
F32 = jnp.float32
BF16 = jnp.bfloat16
VMEM = pltpu.VMEM


def lane_gather(rows, index):
    numbers = lax.GatherDimensionNumbers(
        offset_dims=(),
        collapsed_slice_dims=(1,),
        start_index_map=(1,),
        operand_batching_dims=(0,),
        start_indices_batching_dims=(0,),
    )
    return lax.gather(
        rows,
        index[..., None],
        numbers,
        (1, 1),
        mode=lax.GatherScatterMode.PROMISE_IN_BOUNDS,
    )


def call(kernel, out, inputs, scratch=(), us=1.0, smem=()):
    specs = [
        pl.BlockSpec(memory_space=pltpu.SMEM if i in smem else VMEM) for i in range(len(inputs))
    ]
    return pl.pallas_call(
        kernel,
        out_shape=out,
        in_specs=specs,
        out_specs=jax.tree.map(lambda _: pl.BlockSpec(memory_space=VMEM), out),
        scratch_shapes=list(scratch),
        cost_estimate=pl.CostEstimate(
            flops=int(us * 1.0e9), transcendentals=0, bytes_accessed=int(us * 1.0e6)
        ),
    )(*inputs)


def point_solve(matrix_ref, vector):
    return [jnp.sum(matrix_ref[c] * vector, axis=0, keepdims=True) for c in range(3)]


def first_kernel(dinv, residual, smooth, packed):
    solved = point_solve(dinv, residual[...])
    for c in range(3):
        row = solved[c] * (1.0 / CENTER)
        smooth[c : c + 1, :] = row
        packed[c : c + 1, :] = row.astype(BF16)


def restrict_kernel(residual, local_agg, out):
    points = residual.shape[1]
    groups = out.shape[1]
    agg = local_agg[...]
    low = (agg & (LANES - 1)).astype(jnp.int16)
    high = (agg >> 7).astype(jnp.int16)
    width = 512
    total = [jnp.zeros((2 * groups, LANES), F32) for c in range(3)]
    lane_ids = lax.broadcasted_iota(jnp.int16, (LANES, width), 0)
    group_ids = lax.broadcasted_iota(jnp.int16, (groups, width), 0)
    for block in range(points // width):
        part = slice(block * width, (block + 1) * width)
        onehot = jnp.where(
            jnp.broadcast_to(low[:, part], (LANES, width)) == lane_ids,
            jnp.ones((), BF16),
            jnp.zeros((), BF16),
        )
        chosen = jnp.broadcast_to(high[:, part], (groups, width)) == group_ids
        for c in range(3):
            value = residual[c : c + 1, part]
            upper = value.astype(BF16)
            lower = (value - upper.astype(F32)).astype(BF16)
            zero = jnp.zeros((), BF16)
            both = jnp.concatenate(
                [
                    jnp.where(chosen, jnp.broadcast_to(upper, (groups, width)), zero),
                    jnp.where(chosen, jnp.broadcast_to(lower, (groups, width)), zero),
                ],
                axis=0,
            )
            total[c] = total[c] + lax.dot_general(
                both, onehot, (((1,), (1,)), ((), ())), preferred_element_type=F32
            )
    for c in range(3):
        out[c] = total[c][:groups] + total[c][groups:]


def base_kernel(rhs, dinv, base, packed):
    groups = rhs.shape[1]
    for g in range(groups):
        lanes = slice(g * LANES, (g + 1) * LANES)
        vector = jnp.concatenate([rhs[e, g : g + 1, :] for e in range(3)], axis=0)
        for c in range(3):
            base[c, g : g + 1, :] = jnp.sum(dinv[c, :, lanes] * vector, axis=0, keepdims=True)
    for c in range(3):
        packed[c] = base[c].astype(BF16)


def fill_table(table, source, groups):
    for e in range(3):
        for g in range(groups):
            row = source[e, g : g + 1, :]
            table[e, g] = jnp.broadcast_to(row, (16, LANES)).astype(BF16)


def pick(table, index, groups, first, starts):
    low = (index & (LANES - 1)).astype(jnp.int16)
    high = (index >> 7).astype(jnp.int16)
    picked = list(starts)
    for g in range(groups):
        chosen = high == (first + g)
        for e in range(3):
            value = lane_gather(table[e, g], low)
            picked[e] = jnp.where(chosen, value, picked[e])
    return picked


def local_kernel(smooth, col, out, table, *, first, tiles):
    groups = smooth.shape[1] // LANES
    for e in range(3):
        for g in range(groups):
            row = smooth[e : e + 1, g * LANES : (g + 1) * LANES]
            table[e, g] = jnp.broadcast_to(row, (16, LANES)).astype(BF16)
    bonds_of = col.shape[0]
    zero = jnp.zeros((16, LANES), BF16)

    def one_tile(t, carry):
        source = pl.multiple_of((first + t) * LANES, LANES)
        target = pl.multiple_of(t * LANES, LANES)
        for h in range(bonds_of // 16):
            index = col[pl.ds(h * 16, 16), pl.ds(source, LANES)]
            picked = pick(table, index, groups, 0, [zero] * 3)
            for e in range(3):
                out[e, pl.ds(h * 16, 16), pl.ds(target, LANES)] = picked[e]
        return carry

    lax.fori_loop(0, tiles, one_tile, 0)


def halo_kernel(*refs, pieces, scale_old, scale_new):
    (col, ghost, prev, follow, residual, dinv, smooth, update, bonds) = refs[:9]
    picked_refs = refs[9 : 9 + pieces]
    new_smooth, new_update, packed = refs[9 + pieces : 12 + pieces]
    slots, table, applied = refs[12 + pieces :]
    points = smooth.shape[1]
    groups = points // LANES
    wanted = ghost[...]
    half = wanted.shape[0] // 2
    low = wanted & (LANES - 1)
    high = wanted >> 7
    upper = lax.broadcasted_iota(jnp.int32, wanted.shape, 0) < half
    found = [jnp.zeros(wanted.shape, F32)] * 3
    for g in range(groups):
        lanes = slice(g * LANES, (g + 1) * LANES)
        chosen = high == g
        for e in range(3):
            rows = jnp.where(
                upper,
                jnp.broadcast_to(prev[e : e + 1, lanes].astype(F32), wanted.shape),
                jnp.broadcast_to(follow[e : e + 1, lanes].astype(F32), wanted.shape),
            )
            found[e] = jnp.where(chosen, lane_gather(rows, low), found[e])
    for e in range(3):
        slots[e] = found[e]
    halo_groups = wanted.shape[0]
    fill_table(table, slots, halo_groups)
    bonds_of = col.shape[0]
    tiles_of = groups // pieces

    for piece in range(pieces):

        def one_tile(t, carry, piece=piece):
            here = pl.multiple_of((piece * tiles_of + t) * LANES, LANES)
            there = pl.multiple_of(t * LANES, LANES)
            total = [jnp.zeros((16, LANES), F32)] * 3
            for h in range(bonds_of // 16):
                rows = pl.ds(h * 16, 16)
                index = col[rows, pl.ds(here, LANES)]
                starts = [picked_refs[piece][e, rows, pl.ds(there, LANES)] for e in range(3)]
                picked = pick(table, index, halo_groups, groups, starts)
                wide = [value.astype(F32) for value in picked]
                for c in range(3):
                    for e in range(3):
                        total[c] = (
                            total[c] + bonds[c, e, rows, pl.ds(here, LANES)].astype(F32) * wide[e]
                        )
            for c in range(3):
                applied[c : c + 1, pl.ds(here, LANES)] = jnp.sum(total[c], axis=0, keepdims=True)
            return carry

        lax.fori_loop(0, tiles_of, one_tile, 0)
    remainder = residual[...] - smooth[...] - applied[...]
    solved = point_solve(dinv, remainder)
    for c in range(3):
        row = scale_old * update[c : c + 1, :] + scale_new * solved[c]
        new_update[c : c + 1, :] = row
        total = smooth[c : c + 1, :] + row
        new_smooth[c : c + 1, :] = total
        packed[c : c + 1, :] = total.astype(BF16)


def coarse_kernel(place, base, bases, own_couple, couples, local_agg, smooth, out, field, links):
    subs, me = place[0], place[1]
    groups = base.shape[1]
    steps = JAC - 1

    def valid(row):
        inside = jnp.logical_and(me + row >= 0, me + row < subs)
        return jnp.where(inside, 1.0, 0.0).astype(F32)

    def base_of(row, c):
        if row == 0:
            return base[c]
        slot = row + steps if row < 0 else row + steps - 1
        return bases[slot * 3 + c].astype(F32) * valid(row)

    for k in range(4):
        for g in range(groups):
            links[steps - 1, k, g : g + 1, :] = own_couple[
                k : k + 1, g * LANES : (g + 1) * LANES
            ]
    reach = steps - 1
    for row in range(-reach, reach + 1):
        if row == 0:
            continue
        slot = row + reach if row < 0 else row + reach - 1
        for k in range(4):
            links[row + reach, k] = couples[slot * 4 + k].astype(F32) * valid(row)
    for row in range(-steps, steps + 1):
        for c in range(3):
            field[0, row + steps, c] = base_of(row, c)
    lane = lax.broadcasted_iota(jnp.int32, (groups, LANES), 1)
    line = lax.broadcasted_iota(jnp.int32, (groups, LANES), 0)
    for step in range(steps):
        old, new = step % 2, (step + 1) % 2
        reach = steps - 1 - step
        for row in range(-reach, reach + 1):
            spot = row + steps
            weights = [links[row + steps - 1, k] for k in range(4)]
            for c in range(3):
                x = field[old, spot, c]
                right = pltpu.roll(x, 1, 1)
                right = jnp.where(lane == 0, pltpu.roll(right, 1, 0), right)
                right = jnp.where(jnp.logical_and(lane == 0, line == 0), 0.0, right)
                left = pltpu.roll(x, LANES - 1, 1)
                left = jnp.where(lane == LANES - 1, pltpu.roll(left, groups - 1, 0), left)
                left = jnp.where(
                    jnp.logical_and(lane == LANES - 1, line == groups - 1), 0.0, left
                )
                field[new, spot, c] = base_of(row, c) + (
                    weights[0] * field[old, spot - 1, c]
                    + weights[1] * field[old, spot + 1, c]
                    + weights[2] * right
                    + weights[3] * left
                )
    final = steps % 2
    agg = local_agg[...]
    for block in range(agg.shape[0] // 8):
        index = agg[block * 8 : (block + 1) * 8]
        low = index & (LANES - 1)
        high = index >> 7
        found = [jnp.zeros((8, LANES), F32)] * 3
        for g in range(groups):
            chosen = high == g
            for c in range(3):
                rows = jnp.broadcast_to(field[final, steps, c, g : g + 1, :], (8, LANES))
                found[c] = jnp.where(chosen, lane_gather(rows, low), found[c])
        for c in range(3):
            for r in range(8):
                lanes = slice((block * 8 + r) * LANES, (block * 8 + r + 1) * LANES)
                out[c : c + 1, lanes] = smooth[c : c + 1, lanes] + found[c][r : r + 1]


def shifted(value, steps):
    count = lax.axis_size("sub")
    return lax.ppermute(value, "sub", [(i, (i + steps) % count) for i in range(count)])


def body(
    fine_residual, bonds, bond_col, ghost_points, fine_dinv, aggregate, coarse_dinv, coarse_couple
):
    points = fine_residual.shape[1]
    groups = points // LANES
    bonds_of = bond_col.shape[0]
    per_group = coarse_dinv.shape[2]
    coarse_groups = per_group // LANES
    sub = lax.axis_index("sub")
    ghost = ghost_points.reshape(-1, LANES)
    sds = jax.ShapeDtypeStruct
    field = sds((3, points), F32)
    packed_field = sds((3, points), BF16)

    smooth, packed = call(first_kernel, (field, packed_field), (fine_dinv, fine_residual), us=0.5)
    update = smooth
    local_agg = aggregate - sub * per_group
    couple_rows = coarse_couple.astype(BF16).reshape(4, coarse_groups, LANES)
    message = jnp.concatenate([packed.reshape(3, groups, LANES), couple_rows], axis=0)
    after = shifted(message, 1)
    before = shifted(message, -1)

    rhs = call(
        restrict_kernel,
        sds((3, coarse_groups, LANES), F32),
        (fine_residual, local_agg.reshape(1, points)),
        us=1.5,
    )
    relaid = bonds.transpose(1, 2, 0, 3)
    doms = lax.axis_size("dom")
    step = 1
    while step < doms:
        rhs = rhs + lax.ppermute(rhs, "dom", [(i, i ^ step) for i in range(doms)])
        step *= 2
    coarse_field = sds((3, coarse_groups, LANES), F32)
    base, packed_base = call(
        base_kernel,
        (coarse_field, sds(coarse_field.shape, BF16)),
        (rhs, coarse_dinv),
        us=0.5,
    )

    def gather_local(smooth, pieces):
        tiles = groups // pieces
        return [
            call(
                functools.partial(local_kernel, first=piece * tiles, tiles=tiles),
                sds((3, bonds_of, tiles * LANES), BF16),
                (smooth, bond_col),
                scratch=[VMEM((3, groups, 16, LANES), BF16)],
                us=8.0 / pieces,
            )
            for piece in range(pieces)
        ]

    factor = HALF / CENTER
    base_rows = {0: packed_base}
    link_rows = {0: couple_rows, -1: after[3:], 1: before[3:]}
    for sweep, pieces in enumerate((4, 2, 2)):
        factor_new = 1.0 / (2.0 * CENTER / HALF - factor)
        parts = gather_local(smooth, pieces)
        smooth, update, packed = call(
            functools.partial(
                halo_kernel,
                pieces=pieces,
                scale_old=factor_new * factor,
                scale_new=2.0 * factor_new / HALF,
            ),
            (field, field, packed_field),
            (
                bond_col,
                ghost,
                after[:3].reshape(3, points),
                before[:3].reshape(3, points),
                fine_residual,
                fine_dinv,
                smooth,
                update,
                relaid,
                *parts,
            ),
            scratch=[
                VMEM((3,) + ghost.shape, F32),
                VMEM((3, ghost.shape[0], 16, LANES), BF16),
                VMEM((3, points), F32),
            ],
            us=4.0,
        )
        factor = factor_new
        shaped = packed.reshape(3, groups, LANES)
        if sweep == 0:
            after = shifted(jnp.concatenate([shaped, base_rows[0], link_rows[-1]], axis=0), 1)
            before = shifted(jnp.concatenate([shaped, base_rows[0], link_rows[1]], axis=0), -1)
            base_rows[-1], base_rows[1] = after[3:6], before[3:6]
            link_rows[-2], link_rows[2] = after[6:], before[6:]
        elif sweep == 1:
            after = shifted(jnp.concatenate([shaped, base_rows[-1]], axis=0), 1)
            before = shifted(jnp.concatenate([shaped, base_rows[1]], axis=0), -1)
            base_rows[-2], base_rows[2] = after[3:6], before[3:6]
            far_after = shifted(
                jnp.concatenate(
                    [base_rows[-2], base_rows[-1], base_rows[0], link_rows[-1], link_rows[0]],
                    axis=0,
                ),
                3,
            )
            far_before = shifted(
                jnp.concatenate(
                    [base_rows[0], base_rows[1], base_rows[2], link_rows[0], link_rows[1]],
                    axis=0,
                ),
                -3,
            )
    bases = jnp.concatenate(
        [far_after[:9], base_rows[-2], base_rows[-1], base_rows[1], base_rows[2], far_before[:9]],
        axis=0,
    )
    couples = jnp.concatenate(
        [
            far_after[9:],
            link_rows[-2],
            link_rows[-1],
            link_rows[1],
            link_rows[2],
            far_before[9:],
        ],
        axis=0,
    )
    place = jnp.stack([jnp.int32(lax.axis_size("sub")), sub.astype(jnp.int32)])
    steps = JAC - 1
    return call(
        coarse_kernel,
        field,
        (
            place,
            base,
            bases,
            coarse_couple,
            couples,
            local_agg.reshape(groups, LANES),
            smooth,
        ),
        scratch=[
            VMEM((2, 2 * steps + 1, 3, coarse_groups, LANES), F32),
            VMEM((2 * steps - 1, 4, coarse_groups, LANES), F32),
        ],
        us=2.0,
        smem=(0,),
    )


def solution(mesh):
    placed = (
        P(None, ("dom", "sub")),
        P(None, None, None, ("dom", "sub")),
        P(None, ("dom", "sub")),
        P(("dom", "sub"), None, None),
        P(None, None, ("dom", "sub")),
        P(("dom", "sub")),
        P(None, None, "sub"),
        P(None, "sub"),
    )
    return jax.shard_map(
        body, mesh=mesh, in_specs=placed, out_specs=P(None, ("dom", "sub")), check_vma=False
    )
```

```python
import functools

import jax
import jax.numpy as jnp
from jax import lax
from jax.experimental import pallas as pl
from jax.experimental.pallas import tpu as pltpu
from jax.sharding import PartitionSpec as P

SWEEPS = 3
STEPS = 5
LOW_EIG = 0.3
HIGH_EIG = 2.2
CENTER = (HIGH_EIG + LOW_EIG) / 2.0
HALF = (HIGH_EIG - LOW_EIG) / 2.0
LANES = 128
PACK = 16
F32 = jnp.float32
BF16 = jnp.bfloat16
VMEM = pltpu.VMEM


def lane_gather(rows, index):
    numbers = lax.GatherDimensionNumbers(
        offset_dims=(),
        collapsed_slice_dims=(1,),
        start_index_map=(1,),
        operand_batching_dims=(0,),
        start_indices_batching_dims=(0,),
    )
    return lax.gather(
        rows,
        index[..., None],
        numbers,
        (1, 1),
        mode=lax.GatherScatterMode.PROMISE_IN_BOUNDS,
    )


def call(kernel, out, inputs, scratch=(), us=1.0, spaces={}, limit=16):
    return pl.pallas_call(
        kernel,
        out_shape=out,
        in_specs=[
            pl.BlockSpec(memory_space=spaces.get(i, VMEM)) for i in range(len(inputs))
        ],
        out_specs=jax.tree.map(lambda _: pl.BlockSpec(memory_space=VMEM), out),
        scratch_shapes=list(scratch),
        cost_estimate=pl.CostEstimate(
            flops=int(us * 1.0e9), transcendentals=0, bytes_accessed=int(us * 1.0e6)
        ),
        compiler_params=pltpu.CompilerParams(vmem_limit_bytes=limit * 1024 * 1024),
    )(*inputs)


def rows_of(ref, lead, group):
    return ref[lead + (slice(group * LANES, (group + 1) * LANES),)]


def first_kernel(dinv, residual, couple, dense_dinv, dense_residual, smooth, message):
    groups = smooth.shape[1]
    coarse_groups = message.shape[1]
    for g in range(groups):
        lanes = slice(g * LANES, (g + 1) * LANES)
        for e in range(3):
            dense_residual[e, g : g + 1, :] = residual[e : e + 1, lanes]
            for c in range(3):
                dense_dinv[c, e, g : g + 1, :] = dinv[c, e : e + 1, lanes]
    for g in range(coarse_groups):
        lanes = slice(g * LANES, (g + 1) * LANES)
        for k in range(4):
            message[3 + k, g : g + 1, :] = couple[k : k + 1, lanes].astype(BF16)
    for c in range(3):
        total = dense_dinv[c, 0] * dense_residual[0]
        for e in range(1, 3):
            total = total + dense_dinv[c, e] * dense_residual[e]
        total = total * (1.0 / CENTER)
        smooth[c] = total
        message[c] = total.astype(BF16)


def restrict_kernel(residual, aggregate, out):
    groups = residual.shape[1]
    bins = out.shape[1]
    agg = aggregate[...] & (bins * LANES - 1)
    low = agg & (LANES - 1)
    high = agg >> 7
    batch = 4
    total = [jnp.zeros((2 * bins, LANES), F32) for c in range(3)]
    lane_ids = lax.broadcasted_iota(jnp.int32, (LANES, LANES), 0)
    bin_ids = lax.broadcasted_iota(jnp.int32, (bins, LANES), 0)
    for block in range(groups // batch):
        onehot = []
        spread = [[] for c in range(3)]
        for g in range(block * batch, (block + 1) * batch):
            same = jnp.broadcast_to(low[g : g + 1], (LANES, LANES)) == lane_ids
            onehot.append(jnp.where(same, 1.0, 0.0).astype(BF16))
            chosen = jnp.broadcast_to(high[g : g + 1], (bins, LANES)) == bin_ids
            for c in range(3):
                value = residual[c, g : g + 1, :]
                upper = value.astype(BF16).astype(F32)
                lower = value - upper
                spread[c].append(
                    jnp.concatenate(
                        [
                            jnp.where(chosen, jnp.broadcast_to(part, (bins, LANES)), 0.0)
                            for part in (upper, lower)
                        ],
                        axis=0,
                    ).astype(BF16)
                )
        onehot = jnp.concatenate(onehot, axis=1)
        for c in range(3):
            total[c] = total[c] + lax.dot_general(
                jnp.concatenate(spread[c], axis=1),
                onehot,
                (((1,), (1,)), ((), ())),
                preferred_element_type=F32,
            )
    for c in range(3):
        out[c] = total[c][:bins] + total[c][bins:]


def fill_table(table, source, groups):
    for e in range(3):
        for g in range(groups):
            row = source[e, g : g + 1, :]
            table[e, g] = jnp.broadcast_to(row, (PACK, LANES)).astype(BF16)


def pick(table, index, groups, first, starts):
    low = (index & (LANES - 1)).astype(jnp.int16)
    high = (index >> 7).astype(jnp.int16)
    picked = list(starts)
    for g in range(groups):
        chosen = high == (first + g)
        for e in range(3):
            value = lane_gather(table[e, g], low)
            picked[e] = jnp.where(chosen, value, picked[e])
    return picked


def local_kernel(smooth, col, out, table, *, first, tiles, unroll=4):
    groups = smooth.shape[1]
    fill_table(table, smooth, groups)
    bonds_of = col.shape[0]
    zero = jnp.zeros((PACK, LANES), BF16)

    def some_tiles(t, carry):
        for u in range(unroll):
            source = pl.multiple_of((first + t * unroll + u) * LANES, LANES)
            target = pl.multiple_of((t * unroll + u) * LANES, LANES)
            for h in range(bonds_of // PACK):
                rows = pl.ds(h * PACK, PACK)
                picked = pick(table, col[rows, pl.ds(source, LANES)], groups, 0, [zero] * 3)
                for e in range(3):
                    out[e, rows, pl.ds(target, LANES)] = picked[e]
        return carry

    lax.fori_loop(0, tiles // unroll, some_tiles, 0)


def dense_solve(matrix, vector):
    solved = []
    for c in range(3):
        total = matrix[c, 0] * vector[0]
        for e in range(1, 3):
            total = total + matrix[c, e] * vector[e]
        solved.append(total)
    return solved


def halo_kernel(*refs, sizes, stage, scale_old, scale_new, unroll=4):
    pieces = len(sizes)
    (col, ghost, after, before, residual, dinv, smooth, update, bonds) = refs[:9]
    picked_refs = refs[9 : 9 + pieces]
    refs = refs[9 + pieces :]
    if stage == 0:
        rhs, arrived, coarse_dinv = refs[:3]
        new_smooth, new_update, base, to_next, to_prev = refs[3:8]
        refs = refs[8:]
    elif stage == 1:
        first_after, first_before, base, couple_own = refs[:4]
        new_smooth, new_update, to_next, to_prev, far_next, far_prev = refs[4:10]
        refs = refs[10:]
    else:
        (new_smooth,) = refs[:1]
        refs = refs[1:]
    slots, table, applied = refs
    groups = smooth.shape[1]
    if stage == 0:
        vector = [rhs[e] + arrived[e] for e in range(3)]
        coarse_groups = base.shape[1]
        for c in range(3):
            for g in range(coarse_groups):
                lanes = slice(g * LANES, (g + 1) * LANES)
                total = coarse_dinv[c, 0:1, lanes] * vector[0][g : g + 1]
                for e in range(1, 3):
                    total = total + coarse_dinv[c, e : e + 1, lanes] * vector[e][g : g + 1]
                base[c, g : g + 1, :] = total
        for c in range(3):
            row = base[c].astype(BF16)
            to_next[3 + c] = row
            to_prev[3 + c] = row
        to_next[6:10] = after[3:7]
        to_prev[6:10] = before[3:7]
    elif stage == 1:
        own = base[...].astype(BF16)
        to_next[3:6] = after[3:6]
        to_prev[3:6] = before[3:6]
        for message in (far_next, far_prev):
            message[0:3] = after[3:6]
            message[3:6] = own
            message[6:9] = before[3:6]
        far_next[9:13] = couple_own[3:7]
        far_next[13:17] = first_before[3:7]
        far_prev[9:13] = first_after[3:7]
        far_prev[13:17] = couple_own[3:7]
    wanted = ghost[...]
    half = wanted.shape[0] // 2
    low = wanted & (LANES - 1)
    high = wanted >> 7
    upper = lax.broadcasted_iota(jnp.int32, wanted.shape, 0) < half
    found = [jnp.zeros(wanted.shape, F32)] * 3
    for e in range(3):
        applied[e] = after[e].astype(F32)
        new_smooth[e] = before[e].astype(F32)
    for g in range(groups):
        chosen = high == g
        for e in range(3):
            rows = jnp.where(
                upper,
                jnp.broadcast_to(applied[e, g : g + 1, :], wanted.shape),
                jnp.broadcast_to(new_smooth[e, g : g + 1, :], wanted.shape),
            )
            found[e] = jnp.where(chosen, lane_gather(rows, low), found[e])
    for e in range(3):
        slots[e] = found[e]
    halo_groups = wanted.shape[0]
    fill_table(table, slots, halo_groups)
    bonds_of = col.shape[0]

    for piece in range(pieces):
        start = sum(sizes[:piece])

        def some_tiles(t, carry, piece=piece, start=start):
            for u in range(unroll):
                tile = start + t * unroll + u
                here = pl.ds(pl.multiple_of(tile * LANES, LANES), LANES)
                there = pl.ds(pl.multiple_of((t * unroll + u) * LANES, LANES), LANES)
                total = [jnp.zeros((PACK, LANES), F32)] * 3
                for h in range(bonds_of // PACK):
                    rows = pl.ds(h * PACK, PACK)
                    starts = [picked_refs[piece][e, rows, there] for e in range(3)]
                    picked = pick(table, col[rows, here], halo_groups, groups, starts)
                    wide = [value.astype(F32) for value in picked]
                    for c in range(3):
                        for e in range(3):
                            total[c] = (
                                total[c] + bonds[c, e, rows, here].astype(F32) * wide[e]
                            )
                for c in range(3):
                    applied[c, pl.ds(tile, 1), :] = jnp.sum(total[c], axis=0, keepdims=True)
            return carry

        lax.fori_loop(0, sizes[piece] // unroll, some_tiles, 0)
    remainder = [residual[e] - smooth[e] - applied[e] for e in range(3)]
    solved = dense_solve(dinv, remainder)
    for c in range(3):
        change = scale_old * update[c] + scale_new * solved[c]
        total = smooth[c] + change
        new_smooth[c] = total
        if stage < SWEEPS - 1:
            new_update[c] = change
            to_next[c] = total.astype(BF16)
            to_prev[c] = total.astype(BF16)


def coarse_kernel(*refs):
    (place, base, own_couple, first_after, first_before, second_after, second_before) = refs[:7]
    (third_after, third_before, far_after, far_before, aggregate, smooth) = refs[7:13]
    out, field, links = refs[13:]
    subs, me = place[0], place[1]
    groups = base.shape[1]

    def valid(row):
        inside = jnp.logical_and(me + row >= 0, me + row < subs)
        return jnp.where(inside, 1.0, 0.0).astype(F32)

    base_rows = {
        -5: (far_after, 0),
        -4: (far_after, 3),
        -3: (far_after, 6),
        -2: (third_after, 3),
        -1: (second_after, 3),
        1: (second_before, 3),
        2: (third_before, 3),
        3: (far_before, 0),
        4: (far_before, 3),
        5: (far_before, 6),
    }
    link_rows = {
        -4: (far_after, 9),
        -3: (far_after, 13),
        -2: (second_after, 6),
        -1: (first_after, 3),
        1: (first_before, 3),
        2: (second_before, 6),
        3: (far_before, 9),
        4: (far_before, 13),
    }

    def base_of(row, c):
        if row == 0:
            return base[c]
        ref, start = base_rows[row]
        return ref[start + c].astype(F32) * valid(row)

    for k in range(4):
        for g in range(groups):
            links[STEPS - 1, k, g : g + 1, :] = own_couple[
                k : k + 1, g * LANES : (g + 1) * LANES
            ]
    for row, (ref, start) in link_rows.items():
        for k in range(4):
            links[row + STEPS - 1, k] = ref[start + k].astype(F32) * valid(row)
    for row in range(-STEPS, STEPS + 1):
        for c in range(3):
            field[0, row + STEPS, c] = base_of(row, c)
    lane = lax.broadcasted_iota(jnp.int32, (groups, LANES), 1)
    line = lax.broadcasted_iota(jnp.int32, (groups, LANES), 0)
    for step in range(STEPS):
        old, new = step % 2, (step + 1) % 2
        reach = STEPS - 1 - step
        for row in range(-reach, reach + 1):
            spot = row + STEPS
            weights = [links[row + STEPS - 1, k] for k in range(4)]
            for c in range(3):
                x = field[old, spot, c]
                right = pltpu.roll(x, 1, 1)
                right = jnp.where(lane == 0, pltpu.roll(right, 1, 0), right)
                right = jnp.where(jnp.logical_and(lane == 0, line == 0), 0.0, right)
                left = pltpu.roll(x, LANES - 1, 1)
                left = jnp.where(lane == LANES - 1, pltpu.roll(left, groups - 1, 0), left)
                left = jnp.where(
                    jnp.logical_and(lane == LANES - 1, line == groups - 1), 0.0, left
                )
                field[new, spot, c] = base_of(row, c) + (
                    weights[0] * field[old, spot - 1, c]
                    + weights[1] * field[old, spot + 1, c]
                    + weights[2] * right
                    + weights[3] * left
                )
    final = STEPS % 2
    agg = aggregate[...] & (groups * LANES - 1)
    for block in range(agg.shape[0] // 8):
        index = agg[block * 8 : (block + 1) * 8]
        low = index & (LANES - 1)
        high = index >> 7
        found = [jnp.zeros((8, LANES), F32)] * 3
        for g in range(groups):
            chosen = high == g
            for c in range(3):
                rows = jnp.broadcast_to(field[final, STEPS, c, g : g + 1, :], (8, LANES))
                found[c] = jnp.where(chosen, lane_gather(rows, low), found[c])
        for c in range(3):
            result = smooth[c, block * 8 : (block + 1) * 8, :] + found[c]
            for r in range(8):
                lanes = slice((block * 8 + r) * LANES, (block * 8 + r + 1) * LANES)
                out[c : c + 1, lanes] = result[r : r + 1]


def shifted(value, steps):
    count = lax.axis_size("sub")
    return lax.ppermute(value, "sub", [(i, (i + steps) % count) for i in range(count)])


def body(
    fine_residual, bonds, bond_col, ghost_points, fine_dinv, aggregate, coarse_dinv, coarse_couple
):
    points = fine_residual.shape[1]
    groups = points // LANES
    bonds_of = bond_col.shape[0]
    per_group = coarse_dinv.shape[2]
    coarse_groups = per_group // LANES
    assert per_group & (per_group - 1) == 0
    sub = lax.axis_index("sub")
    doms = lax.axis_size("dom")
    ghost = ghost_points.reshape(-1, LANES)
    agg = aggregate.reshape(groups, LANES)
    relaid = bonds.transpose(1, 2, 0, 3)
    sds = jax.ShapeDtypeStruct
    field = sds((3, groups, LANES), F32)
    coarse_field = sds((3, coarse_groups, LANES), F32)

    def message(rows):
        return sds((rows, groups, LANES), BF16)

    dinv, residual, smooth, packed = call(
        first_kernel,
        (sds((3, 3, groups, LANES), F32), field, field, message(7)),
        (fine_dinv, fine_residual, coarse_couple),
        us=2.0,
    )
    update = smooth
    own_packed = packed
    after = shifted(packed, 1)
    before = shifted(packed, -1)
    first_after, first_before = after, before
    rhs = call(restrict_kernel, coarse_field, (residual, agg), us=2.5)

    def local(smooth, first, tiles):
        return call(
            functools.partial(local_kernel, first=first, tiles=tiles),
            sds((3, bonds_of, tiles * LANES), BF16),
            (smooth, bond_col),
            scratch=[VMEM((3, groups, PACK, LANES), BF16)],
            us=7.5 * tiles / groups,
        )

    def exchanged(value, step):
        return lax.ppermute(value, "dom", [(i, i ^ step) for i in range(doms)])

    sizes = (12, 12, 8)
    parts = []
    arrived = exchanged(rhs, 1)
    parts.append(local(smooth, 0, sizes[0]))
    rhs = rhs + arrived
    arrived = exchanged(rhs, 2)
    later, rhs, parts[0] = lax.optimization_barrier((smooth, rhs, parts[0]))
    parts.append(local(later, sizes[0], sizes[1]))
    rhs = rhs + arrived
    arrived = exchanged(rhs, 4)
    later, rhs, parts[1] = lax.optimization_barrier((smooth, rhs, parts[1]))
    parts.append(local(later, sizes[0] + sizes[1], sizes[2]))

    factor = HALF / CENTER
    for stage in range(SWEEPS):
        factor_new = 1.0 / (2.0 * CENTER / HALF - factor)
        if stage:
            sizes = (groups,)
            parts = [local(smooth, 0, groups)]
        inputs = [bond_col, ghost, after, before, residual, dinv, smooth, update, relaid]
        inputs += parts
        if stage == 0:
            inputs += [rhs, arrived, coarse_dinv]
            outs = (field, field, coarse_field, message(10), message(10))
        elif stage == 1:
            inputs += [first_after, first_before, base, own_packed]
            outs = (field, field, message(6), message(6), message(17), message(17))
        else:
            outs = (field,)
        result = call(
            functools.partial(
                halo_kernel,
                sizes=sizes,
                stage=stage,
                scale_old=factor_new * factor,
                scale_new=2.0 * factor_new / HALF,
            ),
            outs,
            inputs,
            scratch=[
                VMEM((3,) + ghost.shape, F32),
                VMEM((3, ghost.shape[0], PACK, LANES), BF16),
                VMEM((3, groups, LANES), F32),
            ],
            us=4.0,
        )
        factor = factor_new
        if stage == 0:
            smooth, update, base, to_next, to_prev = result
            after = second_after = shifted(to_next, 1)
            before = second_before = shifted(to_prev, -1)
        elif stage == 1:
            smooth, update, to_next, to_prev, far_next, far_prev = result
            after = third_after = shifted(to_next, 1)
            before = third_before = shifted(to_prev, -1)
            far_after = shifted(far_next, 4)
            far_before = shifted(far_prev, -4)
        else:
            (smooth,) = result
    place = jnp.stack([jnp.int32(lax.axis_size("sub")), sub.astype(jnp.int32)])
    return call(
        coarse_kernel,
        sds((3, points), F32),
        (
            place,
            base,
            coarse_couple,
            first_after,
            first_before,
            second_after,
            second_before,
            third_after,
            third_before,
            far_after,
            far_before,
            agg,
            smooth,
        ),
        scratch=[
            VMEM((2, 2 * STEPS + 1, 3, coarse_groups, LANES), F32),
            VMEM((2 * STEPS - 1, 4, coarse_groups, LANES), F32),
        ],
        us=2.0,
        spaces={0: pltpu.SMEM},
    )


def solution(mesh):
    placed = (
        P(None, ("dom", "sub")),
        P(None, None, None, ("dom", "sub")),
        P(None, ("dom", "sub")),
        P(("dom", "sub"), None, None),
        P(None, None, ("dom", "sub")),
        P(("dom", "sub")),
        P(None, None, "sub"),
        P(None, "sub"),
    )
    return jax.shard_map(
        body, mesh=mesh, in_specs=placed, out_specs=P(None, ("dom", "sub")), check_vma=False
    )
```

```python
import functools

import jax
import jax.numpy as jnp
from jax import lax
from jax.experimental import pallas as pl
from jax.experimental.pallas import tpu as pltpu
from jax.sharding import PartitionSpec as P

SWEEPS = 3
STEPS = 5
LOW_EIG = 0.3
HIGH_EIG = 2.2
CENTER = (HIGH_EIG + LOW_EIG) / 2.0
HALF = (HIGH_EIG - LOW_EIG) / 2.0
LANES = 128
PACK = 16
F32 = jnp.float32
BF16 = jnp.bfloat16
VMEM = pltpu.VMEM


def lane_gather(rows, index):
    numbers = lax.GatherDimensionNumbers(
        offset_dims=(),
        collapsed_slice_dims=(1,),
        start_index_map=(1,),
        operand_batching_dims=(0,),
        start_indices_batching_dims=(0,),
    )
    return lax.gather(
        rows,
        index[..., None],
        numbers,
        (1, 1),
        mode=lax.GatherScatterMode.PROMISE_IN_BOUNDS,
    )


def call(kernel, out, inputs, scratch=(), us=1.0, spaces={}, limit=16):
    return pl.pallas_call(
        kernel,
        out_shape=out,
        in_specs=[
            pl.BlockSpec(memory_space=spaces.get(i, VMEM)) for i in range(len(inputs))
        ],
        out_specs=jax.tree.map(lambda _: pl.BlockSpec(memory_space=VMEM), out),
        scratch_shapes=list(scratch),
        cost_estimate=pl.CostEstimate(
            flops=int(us * 1.0e9), transcendentals=0, bytes_accessed=int(us * 1.0e6)
        ),
        compiler_params=pltpu.CompilerParams(vmem_limit_bytes=limit * 1024 * 1024),
    )(*inputs)


def rows_of(ref, lead, group):
    return ref[lead + (slice(group * LANES, (group + 1) * LANES),)]


def first_kernel(*refs):
    sources = refs[:3]
    dense_dinv, dense_residual, smooth, message = refs[3:7]
    dinv, residual, couple, semaphores = refs[7:]
    copies = [
        pltpu.make_async_copy(source, target, semaphores.at[i])
        for i, (source, target) in enumerate(zip(sources, (dinv, residual, couple)))
    ]
    for copy in copies:
        copy.start()
    for copy in copies:
        copy.wait()
    groups = smooth.shape[1]
    coarse_groups = message.shape[1]
    for g in range(groups):
        lanes = slice(g * LANES, (g + 1) * LANES)
        for e in range(3):
            dense_residual[e, g : g + 1, :] = residual[e : e + 1, lanes]
            for c in range(3):
                dense_dinv[c, e, g : g + 1, :] = dinv[c, e : e + 1, lanes]
    for g in range(coarse_groups):
        lanes = slice(g * LANES, (g + 1) * LANES)
        for k in range(4):
            message[3 + k, g : g + 1, :] = couple[k : k + 1, lanes].astype(BF16)
    for c in range(3):
        total = dense_dinv[c, 0] * dense_residual[0]
        for e in range(1, 3):
            total = total + dense_dinv[c, e] * dense_residual[e]
        total = total * (1.0 / CENTER)
        smooth[c] = total
        message[c] = total.astype(BF16)


def restrict_kernel(residual, aggregate, out):
    groups = residual.shape[1]
    bins = out.shape[1]
    agg = aggregate[...] & (bins * LANES - 1)
    low = agg & (LANES - 1)
    high = agg >> 7
    batch = 4
    total = [jnp.zeros((2 * bins, LANES), F32) for c in range(3)]
    lane_ids = lax.broadcasted_iota(jnp.int32, (LANES, LANES), 0)
    bin_ids = lax.broadcasted_iota(jnp.int32, (bins, LANES), 0)
    for block in range(groups // batch):
        onehot = []
        spread = [[] for c in range(3)]
        for g in range(block * batch, (block + 1) * batch):
            same = jnp.broadcast_to(low[g : g + 1], (LANES, LANES)) == lane_ids
            onehot.append(jnp.where(same, 1.0, 0.0).astype(BF16))
            chosen = jnp.broadcast_to(high[g : g + 1], (bins, LANES)) == bin_ids
            for c in range(3):
                value = residual[c, g : g + 1, :]
                upper = value.astype(BF16).astype(F32)
                lower = value - upper
                spread[c].append(
                    jnp.concatenate(
                        [
                            jnp.where(chosen, jnp.broadcast_to(part, (bins, LANES)), 0.0)
                            for part in (upper, lower)
                        ],
                        axis=0,
                    ).astype(BF16)
                )
        onehot = jnp.concatenate(onehot, axis=1)
        for c in range(3):
            total[c] = total[c] + lax.dot_general(
                jnp.concatenate(spread[c], axis=1),
                onehot,
                (((1,), (1,)), ((), ())),
                preferred_element_type=F32,
            )
    for c in range(3):
        out[c] = total[c][:bins] + total[c][bins:]


def fill_table(table, source, groups):
    for e in range(3):
        for g in range(groups):
            row = source[e, g : g + 1, :]
            table[e, g] = jnp.broadcast_to(row, (PACK, LANES)).astype(BF16)


def pick(table, index, groups, first, starts):
    low = (index & (LANES - 1)).astype(jnp.int16)
    high = (index >> 7).astype(jnp.int16)
    picked = list(starts)
    for g in range(groups):
        chosen = high == (first + g)
        for e in range(3):
            value = lane_gather(table[e, g], low)
            picked[e] = jnp.where(chosen, value, picked[e])
    return picked


def local_kernel(smooth, col, out, table, *, first, tiles, unroll=4):
    groups = smooth.shape[1]
    fill_table(table, smooth, groups)
    bonds_of = col.shape[0]
    zero = jnp.zeros((PACK, LANES), BF16)

    def some_tiles(t, carry):
        for u in range(unroll):
            source = pl.multiple_of((first + t * unroll + u) * LANES, LANES)
            target = pl.multiple_of((t * unroll + u) * LANES, LANES)
            for h in range(bonds_of // PACK):
                rows = pl.ds(h * PACK, PACK)
                picked = pick(table, col[rows, pl.ds(source, LANES)], groups, 0, [zero] * 3)
                for e in range(3):
                    out[e, rows, pl.ds(target, LANES)] = picked[e]
        return carry

    lax.fori_loop(0, tiles // unroll, some_tiles, 0)


def dense_solve(matrix, vector):
    solved = []
    for c in range(3):
        total = matrix[c, 0] * vector[0]
        for e in range(1, 3):
            total = total + matrix[c, e] * vector[e]
        solved.append(total)
    return solved


def sort_sides(even, outer, inner, after, before):
    @pl.when(even)
    def _():
        after[...] = outer[...]
        before[...] = inner[...]

    @pl.when(jnp.logical_not(even))
    def _():
        after[...] = inner[...]
        before[...] = outer[...]


def put_sides(even, outer, inner, rows, to_next, to_prev):
    @pl.when(even)
    def _():
        outer[rows] = to_prev
        inner[rows] = to_next

    @pl.when(jnp.logical_not(even))
    def _():
        outer[rows] = to_next
        inner[rows] = to_prev


def halo_kernel(*refs, sizes, stage, scale_old, scale_new, unroll=4):
    pieces = len(sizes)
    (place, col, ghost, outer, inner, residual, dinv, smooth, update, bonds) = refs[:10]
    picked_refs = refs[10 : 10 + pieces]
    refs = refs[10 + pieces :]
    even = (place[1] & 1) == 0
    if stage == 0:
        rhs, arrived, coarse_dinv = refs[:3]
        new_smooth, new_update, base, out_outer, out_inner = refs[3:8]
        refs = refs[8:]
    elif stage == 1:
        first_outer, first_inner, base, couple_own = refs[:4]
        new_smooth, new_update, out_outer, out_inner, far_next, far_prev = refs[4:10]
        refs = refs[10:]
    else:
        (new_smooth,) = refs[:1]
        refs = refs[1:]
    slots, table, applied, after, before = refs[:5]
    sort_sides(even, outer, inner, after, before)
    groups = smooth.shape[1]
    if stage == 0:
        vector = [rhs[e] + arrived[e] for e in range(3)]
        coarse_groups = base.shape[1]
        for c in range(3):
            for g in range(coarse_groups):
                lanes = slice(g * LANES, (g + 1) * LANES)
                total = coarse_dinv[c, 0:1, lanes] * vector[0][g : g + 1]
                for e in range(1, 3):
                    total = total + coarse_dinv[c, e : e + 1, lanes] * vector[e][g : g + 1]
                base[c, g : g + 1, :] = total
        for c in range(3):
            row = base[c].astype(BF16)
            out_outer[3 + c] = row
            out_inner[3 + c] = row
        put_sides(even, out_outer, out_inner, slice(6, 10), after[3:7], before[3:7])
    elif stage == 1:
        first_after, first_before = refs[5:7]
        sort_sides(even, first_outer, first_inner, first_after, first_before)
        own = base[...].astype(BF16)
        put_sides(even, out_outer, out_inner, slice(3, 6), after[3:6], before[3:6])
        for message in (far_next, far_prev):
            message[0:3] = after[3:6]
            message[3:6] = own
            message[6:9] = before[3:6]
        far_next[9:13] = couple_own[3:7]
        far_next[13:17] = first_before[3:7]
        far_prev[9:13] = first_after[3:7]
        far_prev[13:17] = couple_own[3:7]
    wanted = ghost[...]
    half = wanted.shape[0] // 2
    low = wanted & (LANES - 1)
    high = wanted >> 7
    upper = lax.broadcasted_iota(jnp.int32, wanted.shape, 0) < half
    found = [jnp.zeros(wanted.shape, F32)] * 3
    for e in range(3):
        applied[e] = after[e].astype(F32)
        new_smooth[e] = before[e].astype(F32)
    for g in range(groups):
        chosen = high == g
        for e in range(3):
            rows = jnp.where(
                upper,
                jnp.broadcast_to(applied[e, g : g + 1, :], wanted.shape),
                jnp.broadcast_to(new_smooth[e, g : g + 1, :], wanted.shape),
            )
            found[e] = jnp.where(chosen, lane_gather(rows, low), found[e])
    for e in range(3):
        slots[e] = found[e]
    halo_groups = wanted.shape[0]
    fill_table(table, slots, halo_groups)
    bonds_of = col.shape[0]

    for piece in range(pieces):
        start = sum(sizes[:piece])

        def some_tiles(t, carry, piece=piece, start=start):
            for u in range(unroll):
                tile = start + t * unroll + u
                here = pl.ds(pl.multiple_of(tile * LANES, LANES), LANES)
                there = pl.ds(pl.multiple_of((t * unroll + u) * LANES, LANES), LANES)
                total = [jnp.zeros((PACK, LANES), F32)] * 3
                for h in range(bonds_of // PACK):
                    rows = pl.ds(h * PACK, PACK)
                    starts = [picked_refs[piece][e, rows, there] for e in range(3)]
                    picked = pick(table, col[rows, here], halo_groups, groups, starts)
                    wide = [value.astype(F32) for value in picked]
                    for c in range(3):
                        for e in range(3):
                            total[c] = (
                                total[c] + bonds[c, e, rows, here].astype(F32) * wide[e]
                            )
                for c in range(3):
                    applied[c, pl.ds(tile, 1), :] = jnp.sum(total[c], axis=0, keepdims=True)
            return carry

        lax.fori_loop(0, sizes[piece] // unroll, some_tiles, 0)
    remainder = [residual[e] - smooth[e] - applied[e] for e in range(3)]
    solved = dense_solve(dinv, remainder)
    for c in range(3):
        change = scale_old * update[c] + scale_new * solved[c]
        total = smooth[c] + change
        new_smooth[c] = total
        if stage < SWEEPS - 1:
            new_update[c] = change
            out_outer[c] = total.astype(BF16)
            out_inner[c] = total.astype(BF16)


def coarse_kernel(*refs):
    (place, base, own_couple) = refs[:3]
    first, second, third = refs[3:5], refs[5:7], refs[7:9]
    far_after, far_before, aggregate, smooth = refs[9:13]
    out, field, links, kept = refs[13:]
    subs, me = place[0], place[1]
    groups = base.shape[1]
    even = (me & 1) == 0

    def valid(row):
        inside = jnp.logical_and(me + row >= 0, me + row < subs)
        return jnp.where(inside, 1.0, 0.0).astype(F32)

    def from_after(pair):
        return lambda i: jnp.where(even, pair[0][i].astype(F32), pair[1][i].astype(F32))

    def from_before(pair):
        return lambda i: jnp.where(even, pair[1][i].astype(F32), pair[0][i].astype(F32))

    def plain(ref):
        return lambda i: ref[i].astype(F32)

    base_rows = {
        -5: (plain(far_after), 0),
        -4: (plain(far_after), 3),
        -3: (plain(far_after), 6),
        -2: (from_after(third), 3),
        -1: (from_after(second), 3),
        1: (from_before(second), 3),
        2: (from_before(third), 3),
        3: (plain(far_before), 0),
        4: (plain(far_before), 3),
        5: (plain(far_before), 6),
    }
    link_rows = {
        -4: (plain(far_after), 9),
        -3: (plain(far_after), 13),
        -2: (from_after(second), 6),
        -1: (from_after(first), 3),
        1: (from_before(first), 3),
        2: (from_before(second), 6),
        3: (plain(far_before), 9),
        4: (plain(far_before), 13),
    }

    def base_of(row, c):
        if row == 0:
            return base[c]
        ref, start = base_rows[row]
        return ref(start + c) * valid(row)

    for k in range(4):
        for g in range(groups):
            links[STEPS - 1, k, g : g + 1, :] = own_couple[
                k : k + 1, g * LANES : (g + 1) * LANES
            ]
    for row, (ref, start) in link_rows.items():
        for k in range(4):
            links[row + STEPS - 1, k] = ref(start + k) * valid(row)
    for row in range(-STEPS, STEPS + 1):
        for c in range(3):
            value = base_of(row, c)
            kept[row + STEPS, c] = value
            field[0, row + STEPS, c] = value
    lane = lax.broadcasted_iota(jnp.int32, (groups, LANES), 1)
    line = lax.broadcasted_iota(jnp.int32, (groups, LANES), 0)
    for step in range(STEPS):
        old, new = step % 2, (step + 1) % 2
        reach = STEPS - 1 - step
        for row in range(-reach, reach + 1):
            spot = row + STEPS
            weights = [links[row + STEPS - 1, k] for k in range(4)]
            for c in range(3):
                x = field[old, spot, c]
                right = pltpu.roll(x, 1, 1)
                right = jnp.where(lane == 0, pltpu.roll(right, 1, 0), right)
                right = jnp.where(jnp.logical_and(lane == 0, line == 0), 0.0, right)
                left = pltpu.roll(x, LANES - 1, 1)
                left = jnp.where(lane == LANES - 1, pltpu.roll(left, groups - 1, 0), left)
                left = jnp.where(
                    jnp.logical_and(lane == LANES - 1, line == groups - 1), 0.0, left
                )
                field[new, spot, c] = kept[spot, c] + (
                    weights[0] * field[old, spot - 1, c]
                    + weights[1] * field[old, spot + 1, c]
                    + weights[2] * right
                    + weights[3] * left
                )
    final = STEPS % 2
    agg = aggregate[...] & (groups * LANES - 1)
    for block in range(agg.shape[0] // 8):
        index = agg[block * 8 : (block + 1) * 8]
        low = index & (LANES - 1)
        high = index >> 7
        found = [jnp.zeros((8, LANES), F32)] * 3
        for g in range(groups):
            chosen = high == g
            for c in range(3):
                rows = jnp.broadcast_to(field[final, STEPS, c, g : g + 1, :], (8, LANES))
                found[c] = jnp.where(chosen, lane_gather(rows, low), found[c])
        for c in range(3):
            result = smooth[c, block * 8 : (block + 1) * 8, :] + found[c]
            for r in range(8):
                lanes = slice((block * 8 + r) * LANES, (block * 8 + r + 1) * LANES)
                out[c : c + 1, lanes] = result[r : r + 1]


def shifted(value, steps):
    count = lax.axis_size("sub")
    return lax.ppermute(value, "sub", [(i, (i + steps) % count) for i in range(count)])


def exchanged_by_pairs(outer, inner):
    count = lax.axis_size("sub")
    across = [(i, (i + 1) % count) for i in range(1, count, 2)]
    within = [(i, i + 1) for i in range(0, count, 2)]
    outer = lax.ppermute(outer, "sub", across + [(j, i) for i, j in across])
    inner = lax.ppermute(inner, "sub", within + [(j, i) for i, j in within])
    return outer, inner


def body(
    fine_residual, bonds, bond_col, ghost_points, fine_dinv, aggregate, coarse_dinv, coarse_couple
):
    points = fine_residual.shape[1]
    groups = points // LANES
    bonds_of = bond_col.shape[0]
    per_group = coarse_dinv.shape[2]
    coarse_groups = per_group // LANES
    assert per_group & (per_group - 1) == 0
    sub = lax.axis_index("sub")
    doms = lax.axis_size("dom")
    ghost = ghost_points.reshape(-1, LANES)
    agg = aggregate.reshape(groups, LANES)
    relaid = bonds.transpose(1, 2, 0, 3)
    sds = jax.ShapeDtypeStruct
    field = sds((3, groups, LANES), F32)
    coarse_field = sds((3, coarse_groups, LANES), F32)

    def message(rows):
        return sds((rows, groups, LANES), BF16)

    dinv, residual, smooth, packed = call(
        first_kernel,
        (sds((3, 3, groups, LANES), F32), field, field, message(7)),
        tuple(
            pltpu.with_memory_space_constraint(x, pltpu.HBM)
            for x in (fine_dinv, fine_residual, coarse_couple)
        ),
        scratch=[
            VMEM(fine_dinv.shape, F32),
            VMEM(fine_residual.shape, F32),
            VMEM(coarse_couple.shape, F32),
            pltpu.SemaphoreType.DMA((3,)),
        ],
        us=2.0,
        spaces={i: pltpu.HBM for i in range(3)},
    )
    update = smooth
    own_packed = packed
    place = jnp.stack([jnp.int32(lax.axis_size("sub")), sub.astype(jnp.int32)])
    first = arrived_sides = exchanged_by_pairs(packed, packed)
    rhs = call(restrict_kernel, coarse_field, (residual, agg), us=2.5)

    def local(smooth, first, tiles):
        return call(
            functools.partial(local_kernel, first=first, tiles=tiles),
            sds((3, bonds_of, tiles * LANES), BF16),
            (smooth, bond_col),
            scratch=[VMEM((3, groups, PACK, LANES), BF16)],
            us=7.5 * tiles / groups,
        )

    def exchanged(value, step):
        return lax.ppermute(value, "dom", [(i, i ^ step) for i in range(doms)])

    sizes = (12, 12, 8)
    parts = []
    arrived = exchanged(rhs, 1)
    parts.append(local(smooth, 0, sizes[0]))
    rhs = rhs + arrived
    arrived = exchanged(rhs, 2)
    later, rhs, parts[0] = lax.optimization_barrier((smooth, rhs, parts[0]))
    parts.append(local(later, sizes[0], sizes[1]))
    rhs = rhs + arrived
    arrived = exchanged(rhs, 4)
    later, rhs, parts[1] = lax.optimization_barrier((smooth, rhs, parts[1]))
    parts.append(local(later, sizes[0] + sizes[1], sizes[2]))

    factor = HALF / CENTER
    for stage in range(SWEEPS):
        factor_new = 1.0 / (2.0 * CENTER / HALF - factor)
        if stage:
            sizes = (groups,)
            parts = [local(smooth, 0, groups)]
        if stage == SWEEPS - 1:
            parts[0], far_after, far_before = lax.optimization_barrier(
                (parts[0], far_after, far_before)
            )
        inputs = [place, bond_col, ghost, *arrived_sides]
        inputs += [residual, dinv, smooth, update, relaid]
        inputs += parts
        if stage == 0:
            inputs += [rhs, arrived, coarse_dinv]
            outs = (field, field, coarse_field, message(10), message(10))
        elif stage == 1:
            inputs += [*first, base, own_packed]
            outs = (field, field, message(6), message(6), message(17), message(17))
        else:
            outs = (field,)
        result = call(
            functools.partial(
                halo_kernel,
                sizes=sizes,
                stage=stage,
                scale_old=factor_new * factor,
                scale_new=2.0 * factor_new / HALF,
            ),
            outs,
            inputs,
            scratch=[
                VMEM((3,) + ghost.shape, F32),
                VMEM((3, ghost.shape[0], PACK, LANES), BF16),
                VMEM((3, groups, LANES), F32),
                VMEM(arrived_sides[0].shape, BF16),
                VMEM(arrived_sides[0].shape, BF16),
            ]
            + [VMEM(first[0].shape, BF16)] * (2 if stage == 1 else 0),
            us=4.0,
            spaces={0: pltpu.SMEM},
        )
        factor = factor_new
        if stage == 0:
            smooth, update, base, outer, inner = result
            second = arrived_sides = exchanged_by_pairs(outer, inner)
        elif stage == 1:
            smooth, update, outer, inner, far_next, far_prev = result
            third = arrived_sides = exchanged_by_pairs(outer, inner)
            far_after = shifted(far_next, 4)
            far_before = shifted(far_prev, -4)
        else:
            (smooth,) = result
    return call(
        coarse_kernel,
        sds((3, points), F32),
        (
            place,
            base,
            coarse_couple,
            *first,
            *second,
            *third,
            far_after,
            far_before,
            agg,
            smooth,
        ),
        scratch=[
            VMEM((2, 2 * STEPS + 1, 3, coarse_groups, LANES), F32),
            VMEM((2 * STEPS - 1, 4, coarse_groups, LANES), F32),
            VMEM((2 * STEPS + 1, 3, coarse_groups, LANES), F32),
        ],
        us=2.0,
        spaces={0: pltpu.SMEM},
    )


def solution(mesh):
    placed = (
        P(None, ("dom", "sub")),
        P(None, None, None, ("dom", "sub")),
        P(None, ("dom", "sub")),
        P(("dom", "sub"), None, None),
        P(None, None, ("dom", "sub")),
        P(("dom", "sub")),
        P(None, None, "sub"),
        P(None, "sub"),
    )
    return jax.shard_map(
        body, mesh=mesh, in_specs=placed, out_specs=P(None, ("dom", "sub")), check_vma=False
    )
```

```python
import functools

import jax
import jax.numpy as jnp
from jax import lax
from jax.experimental import pallas as pl
from jax.experimental.pallas import tpu as pltpu
from jax.sharding import PartitionSpec as P

SWEEPS = 3
STEPS = 5
LOW_EIG = 0.3
HIGH_EIG = 2.2
CENTER = (HIGH_EIG + LOW_EIG) / 2.0
HALF = (HIGH_EIG - LOW_EIG) / 2.0
LANES = 128
PACK = 16
F32 = jnp.float32
BF16 = jnp.bfloat16
VMEM = pltpu.VMEM


def gather(rows, index, axis):
    numbers = lax.GatherDimensionNumbers(
        offset_dims=(),
        collapsed_slice_dims=(axis,),
        start_index_map=(axis,),
        operand_batching_dims=(1 - axis,),
        start_indices_batching_dims=(1 - axis,),
    )
    return lax.gather(
        rows,
        index[..., None],
        numbers,
        (1, 1),
        mode=lax.GatherScatterMode.PROMISE_IN_BOUNDS,
    )


def lane_gather(rows, index):
    return gather(rows, index, 1)


def row_gather(rows, index):
    return gather(rows, index, 0)


def sorting_network(count):
    pairs = []
    span = 1
    while span < count:
        gap = span
        while gap >= 1:
            for j in range(gap % span, count - gap, 2 * gap):
                for i in range(min(gap, count - j - gap)):
                    if (i + j) // (2 * span) == (i + j + gap) // (2 * span):
                        pairs.append((i + j, i + j + gap))
            gap //= 2
        span *= 2
    return pairs


def sort_planes(planes):
    planes = list(planes)
    for i, j in sorting_network(len(planes)):
        planes[i], planes[j] = (
            jnp.minimum(planes[i], planes[j]),
            jnp.maximum(planes[i], planes[j]),
        )
    return planes


def call(kernel, out, inputs, scratch=(), us=1.0, spaces={}, limit=16):
    return pl.pallas_call(
        kernel,
        out_shape=out,
        in_specs=[
            pl.BlockSpec(memory_space=spaces.get(i, VMEM)) for i in range(len(inputs))
        ],
        out_specs=jax.tree.map(
            lambda x: pl.BlockSpec(memory_space=pltpu.SMEM if x.shape == (2,) else VMEM), out
        ),
        scratch_shapes=list(scratch),
        cost_estimate=pl.CostEstimate(
            flops=int(us * 1.0e9), transcendentals=0, bytes_accessed=int(us * 1.0e6)
        ),
        compiler_params=pltpu.CompilerParams(vmem_limit_bytes=limit * 1024 * 1024),
    )(*inputs)


def rows_of(ref, lead, group):
    return ref[lead + (slice(group * LANES, (group + 1) * LANES),)]


def first_kernel(*refs):
    sources = refs[:3]
    dense_dinv, dense_residual, smooth, message = refs[3:7]
    dinv, residual, couple, semaphores = refs[7:]
    copies = [
        pltpu.make_async_copy(source, target, semaphores.at[i])
        for i, (source, target) in enumerate(zip(sources, (dinv, residual, couple)))
    ]
    for copy in copies:
        copy.start()
    for copy in copies:
        copy.wait()
    groups = smooth.shape[1]
    coarse_groups = message.shape[1]
    for g in range(groups):
        lanes = slice(g * LANES, (g + 1) * LANES)
        for e in range(3):
            dense_residual[e, g : g + 1, :] = residual[e : e + 1, lanes]
            for c in range(3):
                dense_dinv[c, e, g : g + 1, :] = dinv[c, e : e + 1, lanes]
    for g in range(coarse_groups):
        lanes = slice(g * LANES, (g + 1) * LANES)
        for k in range(4):
            message[3 + k, g : g + 1, :] = couple[k : k + 1, lanes].astype(BF16)
    for c in range(3):
        total = dense_dinv[c, 0] * dense_residual[0]
        for e in range(1, 3):
            total = total + dense_dinv[c, e] * dense_residual[e]
        total = total * (1.0 / CENTER)
        smooth[c] = total
        message[c] = total.astype(BF16)


def restrict_kernel(residual, aggregate, out):
    groups = residual.shape[1]
    bins = out.shape[1]
    agg = aggregate[...] & (bins * LANES - 1)
    low = agg & (LANES - 1)
    high = agg >> 7
    batch = 4
    total = [jnp.zeros((2 * bins, LANES), F32) for c in range(3)]
    lane_ids = lax.broadcasted_iota(jnp.int32, (LANES, LANES), 0)
    bin_ids = lax.broadcasted_iota(jnp.int32, (bins, LANES), 0)
    for block in range(groups // batch):
        onehot = []
        spread = [[] for c in range(3)]
        for g in range(block * batch, (block + 1) * batch):
            same = jnp.broadcast_to(low[g : g + 1], (LANES, LANES)) == lane_ids
            onehot.append(jnp.where(same, 1.0, 0.0).astype(BF16))
            chosen = jnp.broadcast_to(high[g : g + 1], (bins, LANES)) == bin_ids
            for c in range(3):
                value = residual[c, g : g + 1, :]
                upper = value.astype(BF16).astype(F32)
                lower = value - upper
                spread[c].append(
                    jnp.concatenate(
                        [
                            jnp.where(chosen, jnp.broadcast_to(part, (bins, LANES)), 0.0)
                            for part in (upper, lower)
                        ],
                        axis=0,
                    ).astype(BF16)
                )
        onehot = jnp.concatenate(onehot, axis=1)
        for c in range(3):
            total[c] = total[c] + lax.dot_general(
                jnp.concatenate(spread[c], axis=1),
                onehot,
                (((1,), (1,)), ((), ())),
                preferred_element_type=F32,
            )
    for c in range(3):
        out[c] = total[c][:bins] + total[c][bins:]


def prepare_kernel(col, picks, start, halo_start, spot, rank, most, flip):
    bonds_of = col.shape[0]
    groups = col.shape[1] // LANES
    stride = bonds_of + 1

    def eight_tiles(block, carry):
        best, halo_best = carry

        def lanes_of(t):
            return pl.ds(pl.multiple_of((block * 8 + t) * LANES, LANES), LANES)

        for t in range(8):
            flip[pl.ds(t * stride, bonds_of), :] = col[:, lanes_of(t)]
        keys = []
        for k in range(bonds_of):
            c = flip[pl.ds(k, 8, stride=stride), :]
            keys.append(((c >> 8) << 13) | (k << 8) | (c & 255))
        keys = sort_planes(keys)
        pairs = [key >> 13 for key in keys]
        ranks = [jnp.zeros((8, LANES), jnp.int32)]
        for k in range(1, bonds_of):
            ranks.append(jnp.where(pairs[k] == pairs[k - 1], ranks[k - 1] + 1, 0))
        back = []
        for k in range(bonds_of):
            local = pairs[k] < PACK
            best = jnp.maximum(best, jnp.where(local, ranks[k], 0))
            halo_best = jnp.maximum(halo_best, jnp.where(local, 0, ranks[k]))
            code = jnp.where(
                local,
                (ranks[k] << 4) | pairs[k],
                ((ranks[k] >> 2) << 4) | ((ranks[k] & 3) << 2) | ((pairs[k] - PACK) + (32 << 4)),
            )
            back.append((((keys[k] >> 8) & 31) << 10) | code)
            flip[pl.ds(k, 8, stride=stride), :] = keys[k]
        row = lax.broadcasted_iota(jnp.int32, (PACK, LANES), 0)
        for t in range(8):
            halves = [flip[pl.ds(t * stride + h * PACK, PACK), :] for h in range(2)]
            for h in range(2):
                picks[h * PACK : (h + 1) * PACK, lanes_of(t)] = (halves[h] & 255).astype(jnp.int16)
            first, second = [(x >> 13).astype(jnp.int16) for x in halves]
            for target, pair, extra in (
                (start, row.astype(jnp.int16), None),
                (halo_start, (PACK + (row & 3)).astype(jnp.int16), (row >> 2).astype(jnp.int16)),
            ):
                place = jnp.zeros((PACK, LANES), jnp.int16)
                for step in (16, 8, 4, 2, 1, 1):
                    probe = place + jnp.int16(step - 1)
                    inner = probe & jnp.int16(PACK - 1)
                    value = jnp.where(
                        probe < PACK, row_gather(first, inner), row_gather(second, inner)
                    )
                    place = jnp.where(value < pair, place + jnp.int16(step), place)
                target[:, lanes_of(t)] = place if extra is None else place + extra
        back = sort_planes(back)
        for k in range(bonds_of):
            flip[pl.ds(k, 8, stride=stride), :] = back[k] & 1023
        for t in range(8):
            for h in range(2):
                code = flip[pl.ds(t * stride + h * PACK, PACK), :]
                rows = slice(h * PACK, (h + 1) * PACK)
                spot[rows, lanes_of(t)] = (code & 15).astype(jnp.int16)
                rank[rows, lanes_of(t)] = (code >> 4).astype(jnp.int16)
        return best, halo_best

    zero = jnp.zeros((8, LANES), jnp.int32)
    best, halo_best = lax.fori_loop(0, groups // 8, eight_tiles, (zero, zero))
    most[0] = jnp.max(best)
    most[1] = jnp.max(halo_best) >> 2


def layer(place, picks, even, odd):
    inner = place & jnp.int16(PACK - 1)
    pick = jnp.where(
        place < PACK, row_gather(picks[0], inner), row_gather(picks[1], inner)
    )
    lane = pick & jnp.int16(LANES - 1)
    second = pick >= LANES
    return [
        jnp.where(second, lane_gather(odd[e], lane), lane_gather(even[e], lane))
        for e in range(3)
    ]


def put_back(values, number, spots, ranks, out):
    for h in range(2):
        hit = ranks[h] == number
        for e in range(3):
            out[h][e] = jnp.where(hit, row_gather(values[e], spots[h]), out[h][e])


def halves_of(ref, lanes):
    return [ref[h * PACK : (h + 1) * PACK, lanes] for h in range(2)]


def splat(number):
    return jnp.full((PACK, LANES), number, jnp.int32).astype(jnp.int16)


LAYERS = 10
HALO_LAYERS = 3


def local_kernel(smooth, picks, start, spot, rank, most, out, *, first, tiles, unroll=4):
    even = [smooth[e, pl.ds(0, PACK, stride=2), :].astype(BF16) for e in range(3)]
    odd = [smooth[e, pl.ds(1, PACK, stride=2), :].astype(BF16) for e in range(3)]

    def some_tiles(t, carry):
        for u in range(unroll):
            source = pl.ds(pl.multiple_of((first + t * unroll + u) * LANES, LANES), LANES)
            target = pl.ds(pl.multiple_of((t * unroll + u) * LANES, LANES), LANES)
            place = start[:, source]
            chosen = halves_of(picks, source)
            spots, ranks = halves_of(spot, source), halves_of(rank, source)
            found = [[jnp.zeros((PACK, LANES), BF16)] * 3 for h in range(2)]
            for m in range(LAYERS):
                values = layer(place + jnp.int16(m), chosen, even, odd)
                put_back(values, jnp.int16(m), spots, ranks, found)
            for h in range(2):
                for e in range(3):
                    out[e, h * PACK : (h + 1) * PACK, target] = found[h][e]
        return carry

    lax.fori_loop(0, tiles // unroll, some_tiles, 0)

    def more(m, carry):
        number = splat(m)
        for t in range(tiles):
            source = slice((first + t) * LANES, (first + t + 1) * LANES)
            target = slice(t * LANES, (t + 1) * LANES)
            found = [
                [out[e, h * PACK : (h + 1) * PACK, target] for e in range(3)] for h in range(2)
            ]
            values = layer(start[:, source] + number, halves_of(picks, source), even, odd)
            put_back(values, number, halves_of(spot, source), halves_of(rank, source), found)
            for h in range(2):
                for e in range(3):
                    out[e, h * PACK : (h + 1) * PACK, target] = found[h][e]
        return carry

    lax.fori_loop(LAYERS, most[0] + 1, more, 0)


def dense_solve(matrix, vector):
    solved = []
    for c in range(3):
        total = matrix[c, 0] * vector[0]
        for e in range(1, 3):
            total = total + matrix[c, e] * vector[e]
        solved.append(total)
    return solved


def halo_kernel(*refs, stage, scale_old, scale_new, unroll=4):
    (place, most, picks, halo_start, spot, rank, ghost, outer, inner) = refs[:9]
    (residual, dinv, smooth, update, bonds, local_found) = refs[9:15]
    refs = refs[15:]
    if stage == 0:
        rhs, arrived, coarse_dinv = refs[:3]
        new_smooth, new_update, base, out_outer, out_inner = refs[3:8]
        refs = refs[8:]
    elif stage == 1:
        first_outer, first_inner, base, couple_own = refs[:4]
        new_smooth, new_update, out_outer, out_inner, far = refs[4:9]
        refs = refs[9:]
    else:
        (new_smooth,) = refs[:1]
        refs = refs[1:]
    applied, other = refs
    groups = smooth.shape[1]
    if stage == 0:
        vector = [rhs[e] + arrived[e] for e in range(3)]
        coarse_groups = base.shape[1]
        for c in range(3):
            for g in range(coarse_groups):
                lanes = slice(g * LANES, (g + 1) * LANES)
                total = coarse_dinv[c, 0:1, lanes] * vector[0][g : g + 1]
                for e in range(1, 3):
                    total = total + coarse_dinv[c, e : e + 1, lanes] * vector[e][g : g + 1]
                base[c, g : g + 1, :] = total
        for c in range(3):
            row = base[c].astype(BF16)
            out_outer[3 + c] = row
            out_inner[3 + c] = row
        out_outer[6:10] = inner[3:7]
        out_inner[6:10] = outer[3:7]
    elif stage == 1:
        out_outer[3:6] = inner[3:6]
        out_inner[3:6] = outer[3:6]
        far[0:3] = outer[3:6]
        far[3:6] = base[...].astype(BF16)
        far[6:9] = inner[3:6]
        far[9:13] = couple_own[3:7]
        far[13:17] = first_outer[3:7]
        far[17:21] = first_inner[3:7]
    wanted = ghost[...]
    half = wanted.shape[0] // 2
    low = wanted & (LANES - 1)
    high = wanted >> 7
    upper = jnp.where(lax.broadcasted_iota(jnp.int32, wanted.shape, 0) < half, 1, 0)
    from_outer = (upper ^ (place[1] & 1)) == 1
    found = [jnp.zeros(wanted.shape, F32)] * 3
    for e in range(3):
        applied[e] = outer[e].astype(F32)
        other[e] = inner[e].astype(F32)
    for g in range(groups):
        chosen = high == g
        for e in range(3):
            rows = jnp.where(
                from_outer,
                jnp.broadcast_to(applied[e, g : g + 1, :], wanted.shape),
                jnp.broadcast_to(other[e, g : g + 1, :], wanted.shape),
            )
            found[e] = jnp.where(chosen, lane_gather(rows, low), found[e])
    pair = (lax.broadcasted_iota(jnp.int32, wanted.shape, 0) & 3) * 2

    def four_times(rows):
        return jnp.concatenate([rows, rows], axis=0).astype(BF16)

    even = [four_times(row_gather(found[e], pair)) for e in range(3)]
    odd = [four_times(row_gather(found[e], pair + 1)) for e in range(3)]

    def apply_tile(tile, values):
        here = pl.ds(pl.multiple_of(tile * LANES, LANES), LANES)
        totals = []
        for c in range(3):
            total = jnp.zeros((PACK, LANES), F32)
            for h in range(2):
                for e in range(3):
                    block = bonds[c, e, h * PACK : (h + 1) * PACK, here].astype(F32)
                    total = total + block * values[h][e].astype(F32)
            totals.append(jnp.sum(total, axis=0, keepdims=True))
        return totals

    def some_tiles(t, carry):
        for u in range(unroll):
            tile = t * unroll + u
            here = pl.ds(pl.multiple_of(tile * LANES, LANES), LANES)
            chosen = halves_of(picks, here)
            spots, ranks = halves_of(spot, here), halves_of(rank, here)
            values = [
                [local_found[e, h * PACK : (h + 1) * PACK, here] for e in range(3)]
                for h in range(2)
            ]
            for v in range(HALO_LAYERS):
                row = layer(halo_start[:, here] + jnp.int16(4 * v), chosen, even, odd)
                put_back(row, jnp.int16(32 + v), spots, ranks, values)
            totals = apply_tile(tile, values)
            for c in range(3):
                applied[c, pl.ds(tile, 1), :] = totals[c]
        return carry

    lax.fori_loop(0, groups // unroll, some_tiles, 0)

    @pl.when(most[1] >= HALO_LAYERS)
    def _():
        def one_tile(tile, carry):
            here = pl.ds(pl.multiple_of(tile * LANES, LANES), LANES)

            def more(v, flat):
                values = [list(flat[:3]), list(flat[3:])]
                row = layer(halo_start[:, here] + splat(4 * v), halves_of(picks, here), even, odd)
                put_back(row, splat(32 + v), halves_of(spot, here), halves_of(rank, here), values)
                return tuple(values[0] + values[1])

            empty = (jnp.zeros((PACK, LANES), BF16),) * 6
            flat = lax.fori_loop(HALO_LAYERS, most[1] + 1, more, empty)
            totals = apply_tile(tile, [flat[:3], flat[3:]])
            for c in range(3):
                applied[c, pl.ds(tile, 1), :] = applied[c, pl.ds(tile, 1), :] + totals[c]
            return carry

        lax.fori_loop(0, groups, one_tile, 0)

    remainder = [residual[e] - smooth[e] - applied[e] for e in range(3)]
    solved = dense_solve(dinv, remainder)
    for c in range(3):
        change = scale_old * update[c] + scale_new * solved[c]
        total = smooth[c] + change
        new_smooth[c] = total
        if stage < SWEEPS - 1:
            new_update[c] = change
            out_outer[c] = total.astype(BF16)
            out_inner[c] = total.astype(BF16)


def coarse_kernel(*refs):
    (place, base, own_couple) = refs[:3]
    first, second, third = refs[3:5], refs[5:7], refs[7:9]
    far_after, far_before, aggregate, smooth = refs[9:13]
    out, field, links, kept = refs[13:]
    subs, me = place[0], place[1]
    groups = base.shape[1]
    even = (me & 1) == 0

    def valid(row):
        inside = jnp.logical_and(me + row >= 0, me + row < subs)
        return jnp.where(inside, 1.0, 0.0).astype(F32)

    def from_after(pair, start):
        return lambda i: jnp.where(
            even, pair[0][start + i].astype(F32), pair[1][start + i].astype(F32)
        )

    def from_before(pair, start):
        return from_after((pair[1], pair[0]), start)

    def plain(ref, start):
        return lambda i: ref[start + i].astype(F32)

    def either(ref, when_even, when_odd):
        return lambda i: jnp.where(
            even, ref[when_even + i].astype(F32), ref[when_odd + i].astype(F32)
        )

    base_rows = {
        -5: either(far_after, 0, 6),
        -4: plain(far_after, 3),
        -3: either(far_after, 6, 0),
        -2: from_after(third, 3),
        -1: from_after(second, 3),
        1: from_before(second, 3),
        2: from_before(third, 3),
        3: either(far_before, 0, 6),
        4: plain(far_before, 3),
        5: either(far_before, 6, 0),
    }
    link_rows = {
        -4: plain(far_after, 9),
        -3: either(far_after, 17, 13),
        -2: from_after(second, 6),
        -1: from_after(first, 3),
        1: from_before(first, 3),
        2: from_before(second, 6),
        3: either(far_before, 13, 17),
        4: plain(far_before, 9),
    }

    def base_of(row, c):
        if row == 0:
            return base[c]
        return base_rows[row](c) * valid(row)

    for k in range(4):
        for g in range(groups):
            links[STEPS - 1, k, g : g + 1, :] = own_couple[
                k : k + 1, g * LANES : (g + 1) * LANES
            ]
    for row, read in link_rows.items():
        for k in range(4):
            links[row + STEPS - 1, k] = read(k) * valid(row)
    for row in range(-STEPS, STEPS + 1):
        for c in range(3):
            value = base_of(row, c)
            kept[row + STEPS, c] = value
            field[0, row + STEPS, c] = value
    lane = lax.broadcasted_iota(jnp.int32, (groups, LANES), 1)
    line = lax.broadcasted_iota(jnp.int32, (groups, LANES), 0)
    for step in range(STEPS):
        old, new = step % 2, (step + 1) % 2
        reach = STEPS - 1 - step
        for row in range(-reach, reach + 1):
            spot = row + STEPS
            weights = [links[row + STEPS - 1, k] for k in range(4)]
            for c in range(3):
                x = field[old, spot, c]
                right = pltpu.roll(x, 1, 1)
                right = jnp.where(lane == 0, pltpu.roll(right, 1, 0), right)
                right = jnp.where(jnp.logical_and(lane == 0, line == 0), 0.0, right)
                left = pltpu.roll(x, LANES - 1, 1)
                left = jnp.where(lane == LANES - 1, pltpu.roll(left, groups - 1, 0), left)
                left = jnp.where(
                    jnp.logical_and(lane == LANES - 1, line == groups - 1), 0.0, left
                )
                field[new, spot, c] = kept[spot, c] + (
                    weights[0] * field[old, spot - 1, c]
                    + weights[1] * field[old, spot + 1, c]
                    + weights[2] * right
                    + weights[3] * left
                )
    final = STEPS % 2
    agg = aggregate[...] & (groups * LANES - 1)
    for block in range(agg.shape[0] // 8):
        index = agg[block * 8 : (block + 1) * 8]
        low = index & (LANES - 1)
        high = index >> 7
        found = [jnp.zeros((8, LANES), F32)] * 3
        for g in range(groups):
            chosen = high == g
            for c in range(3):
                rows = jnp.broadcast_to(field[final, STEPS, c, g : g + 1, :], (8, LANES))
                found[c] = jnp.where(chosen, lane_gather(rows, low), found[c])
        for c in range(3):
            result = smooth[c, block * 8 : (block + 1) * 8, :] + found[c]
            for r in range(8):
                lanes = slice((block * 8 + r) * LANES, (block * 8 + r + 1) * LANES)
                out[c : c + 1, lanes] = result[r : r + 1]


def shifted(value, steps):
    count = lax.axis_size("sub")
    return lax.ppermute(value, "sub", [(i, (i + steps) % count) for i in range(count)])


def exchanged_by_pairs(outer, inner):
    count = lax.axis_size("sub")
    across = [(i, (i + 1) % count) for i in range(1, count, 2)]
    within = [(i, i + 1) for i in range(0, count, 2)]
    outer = lax.ppermute(outer, "sub", across + [(j, i) for i, j in across])
    inner = lax.ppermute(inner, "sub", within + [(j, i) for i, j in within])
    return outer, inner


def body(
    fine_residual, bonds, bond_col, ghost_points, fine_dinv, aggregate, coarse_dinv, coarse_couple
):
    points = fine_residual.shape[1]
    groups = points // LANES
    bonds_of = bond_col.shape[0]
    per_group = coarse_dinv.shape[2]
    coarse_groups = per_group // LANES
    assert per_group & (per_group - 1) == 0
    sub = lax.axis_index("sub")
    doms = lax.axis_size("dom")
    ghost = ghost_points.reshape(-1, LANES)
    agg = aggregate.reshape(groups, LANES)
    relaid = bonds.transpose(1, 2, 0, 3)
    sds = jax.ShapeDtypeStruct
    field = sds((3, groups, LANES), F32)
    coarse_field = sds((3, coarse_groups, LANES), F32)

    def message(rows):
        return sds((rows, groups, LANES), BF16)

    dinv, residual, smooth, packed = call(
        first_kernel,
        (sds((3, 3, groups, LANES), F32), field, field, message(7)),
        tuple(
            pltpu.with_memory_space_constraint(x, pltpu.HBM)
            for x in (fine_dinv, fine_residual, coarse_couple)
        ),
        scratch=[
            VMEM(fine_dinv.shape, F32),
            VMEM(fine_residual.shape, F32),
            VMEM(coarse_couple.shape, F32),
            pltpu.SemaphoreType.DMA((3,)),
        ],
        us=2.0,
        spaces={i: pltpu.HBM for i in range(3)},
    )
    update = smooth
    own_packed = packed
    place = jnp.stack([jnp.int32(lax.axis_size("sub")), sub.astype(jnp.int32)])
    rhs = call(restrict_kernel, coarse_field, (residual, agg), us=1.2)

    def exchanged(value, step):
        return lax.ppermute(value, "dom", [(i, i ^ step) for i in range(doms)])

    rhs, packed = lax.optimization_barrier((rhs, packed))
    arrived = exchanged(rhs, 1)
    first = arrived_sides = exchanged_by_pairs(packed, packed)
    rhs = rhs + arrived
    arrived = exchanged(rhs, 2)
    columns, rhs = lax.optimization_barrier((bond_col, rhs))

    def shorts(rows):
        return sds((rows, points), jnp.int16)

    picks, start, halo_start, spot, rank, most = call(
        prepare_kernel,
        (
            shorts(bonds_of),
            shorts(PACK),
            shorts(PACK),
            shorts(bonds_of),
            shorts(bonds_of),
            sds((2,), jnp.int32),
        ),
        (columns,),
        scratch=[VMEM((8 * (bonds_of + 2), LANES), jnp.int32)],
        us=2.5,
    )
    rhs = rhs + arrived
    arrived = exchanged(rhs, 4)
    start, rhs = lax.optimization_barrier((start, rhs))

    factor = HALF / CENTER
    for stage in range(SWEEPS):
        factor_new = 1.0 / (2.0 * CENTER / HALF - factor)
        found = call(
            functools.partial(local_kernel, first=0, tiles=groups),
            sds((3, bonds_of, points), BF16),
            (smooth, picks, start, spot, rank, most),
            us=3.5,
            spaces={5: pltpu.SMEM},
        )
        if stage == SWEEPS - 1:
            found, far_after, far_before = lax.optimization_barrier(
                (found, far_after, far_before)
            )
        inputs = [place, most, picks, halo_start, spot, rank, ghost, *arrived_sides]
        inputs += [residual, dinv, smooth, update, relaid, found]
        if stage == 0:
            inputs += [rhs, arrived, coarse_dinv]
            outs = (field, field, coarse_field, message(10), message(10))
        elif stage == 1:
            inputs += [*first, base, own_packed]
            outs = (field, field, message(6), message(6), message(21))
        else:
            outs = (field,)
        result = call(
            functools.partial(
                halo_kernel,
                stage=stage,
                scale_old=factor_new * factor,
                scale_new=2.0 * factor_new / HALF,
            ),
            outs,
            inputs,
            scratch=[VMEM((3, groups, LANES), F32), VMEM((3, groups, LANES), F32)],
            us=2.5,
            spaces={0: pltpu.SMEM, 1: pltpu.SMEM},
        )
        factor = factor_new
        if stage == 0:
            smooth, update, base, outer, inner = result
            second = arrived_sides = exchanged_by_pairs(outer, inner)
        elif stage == 1:
            smooth, update, outer, inner, far = result
            third = arrived_sides = exchanged_by_pairs(outer, inner)
            far_after = shifted(far, 4)
            far_before = shifted(far, -4)
        else:
            (smooth,) = result
    return call(
        coarse_kernel,
        sds((3, points), F32),
        (
            place,
            base,
            coarse_couple,
            *first,
            *second,
            *third,
            far_after,
            far_before,
            agg,
            smooth,
        ),
        scratch=[
            VMEM((2, 2 * STEPS + 1, 3, coarse_groups, LANES), F32),
            VMEM((2 * STEPS - 1, 4, coarse_groups, LANES), F32),
            VMEM((2 * STEPS + 1, 3, coarse_groups, LANES), F32),
        ],
        us=2.0,
        spaces={0: pltpu.SMEM},
    )


def solution(mesh):
    placed = (
        P(None, ("dom", "sub")),
        P(None, None, None, ("dom", "sub")),
        P(None, ("dom", "sub")),
        P(("dom", "sub"), None, None),
        P(None, None, ("dom", "sub")),
        P(("dom", "sub")),
        P(None, None, "sub"),
        P(None, "sub"),
    )
    return jax.shard_map(
        body, mesh=mesh, in_specs=placed, out_specs=P(None, ("dom", "sub")), check_vma=False
    )
```

```python
import functools

import jax
import jax.numpy as jnp
from jax import lax
from jax.experimental import pallas as pl
from jax.experimental.pallas import tpu as pltpu
from jax.sharding import PartitionSpec as P

SWEEPS = 3
STEPS = 5
LOW_EIG = 0.3
HIGH_EIG = 2.2
CENTER = (HIGH_EIG + LOW_EIG) / 2.0
HALF = (HIGH_EIG - LOW_EIG) / 2.0
LANES = 128
PACK = 16
F32 = jnp.float32
BF16 = jnp.bfloat16
VMEM = pltpu.VMEM


def gather(rows, index, axis):
    numbers = lax.GatherDimensionNumbers(
        offset_dims=(),
        collapsed_slice_dims=(axis,),
        start_index_map=(axis,),
        operand_batching_dims=(1 - axis,),
        start_indices_batching_dims=(1 - axis,),
    )
    return lax.gather(
        rows,
        index[..., None],
        numbers,
        (1, 1),
        mode=lax.GatherScatterMode.PROMISE_IN_BOUNDS,
    )


def lane_gather(rows, index):
    return gather(rows, index, 1)


def row_gather(rows, index):
    return gather(rows, index, 0)


def sorting_network(count):
    pairs = []
    span = 1
    while span < count:
        gap = span
        while gap >= 1:
            for j in range(gap % span, count - gap, 2 * gap):
                for i in range(min(gap, count - j - gap)):
                    if (i + j) // (2 * span) == (i + j + gap) // (2 * span):
                        pairs.append((i + j, i + j + gap))
            gap //= 2
        span *= 2
    return pairs


def sort_planes(planes):
    planes = list(planes)
    for i, j in sorting_network(len(planes)):
        planes[i], planes[j] = (
            jnp.minimum(planes[i], planes[j]),
            jnp.maximum(planes[i], planes[j]),
        )
    return planes


def call(kernel, out, inputs, scratch=(), us=1.0, spaces={}, limit=16):
    return pl.pallas_call(
        kernel,
        out_shape=out,
        in_specs=[
            pl.BlockSpec(memory_space=spaces.get(i, VMEM)) for i in range(len(inputs))
        ],
        out_specs=jax.tree.map(
            lambda x: pl.BlockSpec(memory_space=pltpu.SMEM if x.shape == (2,) else VMEM), out
        ),
        scratch_shapes=list(scratch),
        cost_estimate=pl.CostEstimate(
            flops=int(us * 1.0e9), transcendentals=0, bytes_accessed=int(us * 1.0e6)
        ),
        compiler_params=pltpu.CompilerParams(vmem_limit_bytes=limit * 1024 * 1024),
    )(*inputs)


def rows_of(ref, lead, group):
    return ref[lead + (slice(group * LANES, (group + 1) * LANES),)]


def first_kernel(*refs):
    sources = refs[:4]
    dense_dinv, dense_residual, smooth, message, rhs = refs[4:9]
    residual, aggregate, dinv, couple, semaphores = refs[9:]
    copies = [
        pltpu.make_async_copy(source, target, semaphores.at[i])
        for i, (source, target) in enumerate(zip(sources, (residual, aggregate, dinv, couple)))
    ]
    for copy in copies:
        copy.start()
    groups = smooth.shape[1]
    copies[0].wait()
    for g in range(groups):
        for e in range(3):
            dense_residual[e, g : g + 1, :] = residual[
                e : e + 1, g * LANES : (g + 1) * LANES
            ]
    copies[1].wait()
    restrict(dense_residual, aggregate, rhs)
    copies[2].wait()
    copies[3].wait()
    coarse_groups = message.shape[1]
    for g in range(groups):
        lanes = slice(g * LANES, (g + 1) * LANES)
        for e in range(3):
            for c in range(3):
                dense_dinv[c, e, g : g + 1, :] = dinv[c, e : e + 1, lanes]
    for g in range(coarse_groups):
        lanes = slice(g * LANES, (g + 1) * LANES)
        for k in range(4):
            message[3 + k, g : g + 1, :] = couple[k : k + 1, lanes].astype(BF16)
    for c in range(3):
        total = dense_dinv[c, 0] * dense_residual[0]
        for e in range(1, 3):
            total = total + dense_dinv[c, e] * dense_residual[e]
        total = total * (1.0 / CENTER)
        smooth[c] = total
        message[c] = total.astype(BF16)


def restrict(residual, aggregate, out):
    groups = residual.shape[1]
    bins = out.shape[1]
    agg = aggregate[...] & (bins * LANES - 1)
    low = agg & (LANES - 1)
    high = agg >> 7
    batch = 4
    total = [jnp.zeros((2 * bins, LANES), F32) for c in range(3)]
    lane_ids = lax.broadcasted_iota(jnp.int32, (LANES, LANES), 0)
    bin_ids = lax.broadcasted_iota(jnp.int32, (bins, LANES), 0)
    for block in range(groups // batch):
        onehot = []
        spread = [[] for c in range(3)]
        for g in range(block * batch, (block + 1) * batch):
            same = jnp.broadcast_to(low[g : g + 1], (LANES, LANES)) == lane_ids
            onehot.append(jnp.where(same, 1.0, 0.0).astype(BF16))
            chosen = jnp.broadcast_to(high[g : g + 1], (bins, LANES)) == bin_ids
            for c in range(3):
                value = residual[c, g : g + 1, :]
                upper = value.astype(BF16).astype(F32)
                lower = value - upper
                spread[c].append(
                    jnp.concatenate(
                        [
                            jnp.where(chosen, jnp.broadcast_to(part, (bins, LANES)), 0.0)
                            for part in (upper, lower)
                        ],
                        axis=0,
                    ).astype(BF16)
                )
        onehot = jnp.concatenate(onehot, axis=1)
        for c in range(3):
            total[c] = total[c] + lax.dot_general(
                jnp.concatenate(spread[c], axis=1),
                onehot,
                (((1,), (1,)), ((), ())),
                preferred_element_type=F32,
            )
    for c in range(3):
        out[c] = total[c][:bins] + total[c][bins:]


def prepare_kernel(col, picks, start, halo_start, spot, rank, most, flip):
    bonds_of = col.shape[0]
    groups = col.shape[1] // LANES
    stride = bonds_of + 1

    def eight_tiles(block, carry):
        best, halo_best = carry

        def lanes_of(t):
            return pl.ds(pl.multiple_of((block * 8 + t) * LANES, LANES), LANES)

        for t in range(8):
            flip[pl.ds(t * stride, bonds_of), :] = col[:, lanes_of(t)]
        keys = []
        for k in range(bonds_of):
            c = flip[pl.ds(k, 8, stride=stride), :]
            keys.append(((c >> 8) << 13) | (k << 8) | (c & 255))
        keys = sort_planes(keys)
        pairs = [key >> 13 for key in keys]
        ranks = [jnp.zeros((8, LANES), jnp.int32)]
        for k in range(1, bonds_of):
            ranks.append(jnp.where(pairs[k] == pairs[k - 1], ranks[k - 1] + 1, 0))
        back = []
        for k in range(bonds_of):
            local = pairs[k] < PACK
            best = jnp.maximum(best, jnp.where(local, ranks[k], 0))
            halo_best = jnp.maximum(halo_best, jnp.where(local, 0, ranks[k]))
            code = jnp.where(
                local,
                (ranks[k] << 4) | pairs[k],
                ((ranks[k] >> 2) << 4) | ((ranks[k] & 3) << 2) | ((pairs[k] - PACK) + (32 << 4)),
            )
            back.append((((keys[k] >> 8) & 31) << 10) | code)
            flip[pl.ds(k, 8, stride=stride), :] = keys[k]
        row = lax.broadcasted_iota(jnp.int32, (PACK, LANES), 0)
        for t in range(8):
            halves = [flip[pl.ds(t * stride + h * PACK, PACK), :] for h in range(2)]
            for h in range(2):
                picks[h * PACK : (h + 1) * PACK, lanes_of(t)] = (halves[h] & 255).astype(jnp.int16)
            first, second = [(x >> 13).astype(jnp.int16) for x in halves]
            for target, pair, extra in (
                (start, row.astype(jnp.int16), None),
                (halo_start, (PACK + (row & 3)).astype(jnp.int16), (row >> 2).astype(jnp.int16)),
            ):
                place = jnp.zeros((PACK, LANES), jnp.int16)
                for step in (16, 8, 4, 2, 1, 1):
                    probe = place + jnp.int16(step - 1)
                    inner = probe & jnp.int16(PACK - 1)
                    value = jnp.where(
                        probe < PACK, row_gather(first, inner), row_gather(second, inner)
                    )
                    place = jnp.where(value < pair, place + jnp.int16(step), place)
                target[:, lanes_of(t)] = place if extra is None else place + extra
        back = sort_planes(back)
        for k in range(bonds_of):
            flip[pl.ds(k, 8, stride=stride), :] = back[k] & 1023
        for t in range(8):
            for h in range(2):
                code = flip[pl.ds(t * stride + h * PACK, PACK), :]
                rows = slice(h * PACK, (h + 1) * PACK)
                spot[rows, lanes_of(t)] = (code & 15).astype(jnp.int16)
                rank[rows, lanes_of(t)] = (code >> 4).astype(jnp.int16)
        return best, halo_best

    zero = jnp.zeros((8, LANES), jnp.int32)
    best, halo_best = lax.fori_loop(0, groups // 8, eight_tiles, (zero, zero))
    most[0] = jnp.max(best)
    most[1] = jnp.max(halo_best) >> 2


def layer(place, picks, even, odd):
    inner = place & jnp.int16(PACK - 1)
    pick = jnp.where(
        place < PACK, row_gather(picks[0], inner), row_gather(picks[1], inner)
    )
    lane = pick & jnp.int16(LANES - 1)
    second = pick >= LANES
    return [
        jnp.where(second, lane_gather(odd[e], lane), lane_gather(even[e], lane))
        for e in range(3)
    ]


def put_back(values, number, spots, ranks, out):
    for h in range(2):
        hit = ranks[h] == number
        for e in range(3):
            out[h][e] = jnp.where(hit, row_gather(values[e], spots[h]), out[h][e])


def halves_of(ref, lanes):
    return [ref[h * PACK : (h + 1) * PACK, lanes] for h in range(2)]


def splat(number):
    return jnp.full((PACK, LANES), number, jnp.int32).astype(jnp.int16)


LAYERS = 10
HALO_LAYERS = 3


def local_kernel(smooth, picks, start, spot, rank, most, out, *, first, tiles, unroll=8):
    even = [smooth[e, pl.ds(0, PACK, stride=2), :].astype(BF16) for e in range(3)]
    odd = [smooth[e, pl.ds(1, PACK, stride=2), :].astype(BF16) for e in range(3)]

    def some_tiles(t, carry):
        for u in range(unroll):
            source = pl.ds(pl.multiple_of((first + t * unroll + u) * LANES, LANES), LANES)
            target = pl.ds(pl.multiple_of((t * unroll + u) * LANES, LANES), LANES)
            place = start[:, source]
            chosen = halves_of(picks, source)
            spots, ranks = halves_of(spot, source), halves_of(rank, source)
            found = [[jnp.zeros((PACK, LANES), BF16)] * 3 for h in range(2)]
            for m in range(LAYERS):
                values = layer(place + jnp.int16(m), chosen, even, odd)
                put_back(values, jnp.int16(m), spots, ranks, found)
            for h in range(2):
                for e in range(3):
                    out[e, h * PACK : (h + 1) * PACK, target] = found[h][e]
        return carry

    lax.fori_loop(0, tiles // unroll, some_tiles, 0)

    def more(m, carry):
        number = splat(m)
        for t in range(tiles):
            source = slice((first + t) * LANES, (first + t + 1) * LANES)
            target = slice(t * LANES, (t + 1) * LANES)
            found = [
                [out[e, h * PACK : (h + 1) * PACK, target] for e in range(3)] for h in range(2)
            ]
            values = layer(start[:, source] + number, halves_of(picks, source), even, odd)
            put_back(values, number, halves_of(spot, source), halves_of(rank, source), found)
            for h in range(2):
                for e in range(3):
                    out[e, h * PACK : (h + 1) * PACK, target] = found[h][e]
        return carry

    lax.fori_loop(LAYERS, most[0] + 1, more, 0)


def dense_solve(matrix, vector):
    solved = []
    for c in range(3):
        total = matrix[c, 0] * vector[0]
        for e in range(1, 3):
            total = total + matrix[c, e] * vector[e]
        solved.append(total)
    return solved


def halo_kernel(*refs, stage, scale_old, scale_new, unroll=8):
    (place, most, picks, halo_start, spot, rank, ghost, outer, inner) = refs[:9]
    (residual, dinv, smooth, update, bonds, local_found) = refs[9:15]
    refs = refs[15:]
    if stage == 0:
        rhs, arrived, coarse_dinv = refs[:3]
        new_smooth, new_update, base, out_outer, out_inner = refs[3:8]
        refs = refs[8:]
    elif stage == 1:
        first_outer, first_inner, base, couple_own = refs[:4]
        new_smooth, new_update, out_outer, out_inner, far = refs[4:9]
        refs = refs[9:]
    else:
        (new_smooth,) = refs[:1]
        refs = refs[1:]
    applied, other, partial = refs
    groups = smooth.shape[1]
    if stage == 0:
        vector = [rhs[e] + arrived[e] for e in range(3)]
        coarse_groups = base.shape[1]
        for c in range(3):
            for g in range(coarse_groups):
                lanes = slice(g * LANES, (g + 1) * LANES)
                total = coarse_dinv[c, 0:1, lanes] * vector[0][g : g + 1]
                for e in range(1, 3):
                    total = total + coarse_dinv[c, e : e + 1, lanes] * vector[e][g : g + 1]
                base[c, g : g + 1, :] = total
        for c in range(3):
            row = base[c].astype(BF16)
            out_outer[3 + c] = row
            out_inner[3 + c] = row
        out_outer[6:10] = inner[3:7]
        out_inner[6:10] = outer[3:7]
    elif stage == 1:
        out_outer[3:6] = inner[3:6]
        out_inner[3:6] = outer[3:6]
        far[0:3] = outer[3:6]
        far[3:6] = base[...].astype(BF16)
        far[6:9] = inner[3:6]
        far[9:13] = couple_own[3:7]
        far[13:17] = first_outer[3:7]
        far[17:21] = first_inner[3:7]
    wanted = ghost[...]
    half = wanted.shape[0] // 2
    low = wanted & (LANES - 1)
    high = wanted >> 7
    upper = jnp.where(lax.broadcasted_iota(jnp.int32, wanted.shape, 0) < half, 1, 0)
    from_outer = (upper ^ (place[1] & 1)) == 1
    found = [jnp.zeros(wanted.shape, F32)] * 3
    for e in range(3):
        applied[e] = outer[e].astype(F32)
        other[e] = inner[e].astype(F32)
    for g in range(groups):
        chosen = high == g
        for e in range(3):
            rows = jnp.where(
                from_outer,
                jnp.broadcast_to(applied[e, g : g + 1, :], wanted.shape),
                jnp.broadcast_to(other[e, g : g + 1, :], wanted.shape),
            )
            found[e] = jnp.where(chosen, lane_gather(rows, low), found[e])
    pair = (lax.broadcasted_iota(jnp.int32, wanted.shape, 0) & 3) * 2

    def four_times(rows):
        return jnp.concatenate([rows, rows], axis=0).astype(BF16)

    even = [four_times(row_gather(found[e], pair)) for e in range(3)]
    odd = [four_times(row_gather(found[e], pair + 1)) for e in range(3)]

    def apply_tile(tile, values):
        here = pl.ds(pl.multiple_of(tile * LANES, LANES), LANES)
        totals = []
        for c in range(3):
            total = jnp.zeros((PACK, LANES), F32)
            for h in range(2):
                for e in range(3):
                    block = bonds[c, e, h * PACK : (h + 1) * PACK, here].astype(F32)
                    total = total + block * values[h][e].astype(F32)
            totals.append(total[:8] + total[8:])
        return totals

    def some_tiles(t, carry):
        for u in range(unroll):
            tile = t * unroll + u
            here = pl.ds(pl.multiple_of(tile * LANES, LANES), LANES)
            chosen = halves_of(picks, here)
            spots, ranks = halves_of(spot, here), halves_of(rank, here)
            values = [
                [local_found[e, h * PACK : (h + 1) * PACK, here] for e in range(3)]
                for h in range(2)
            ]
            for v in range(HALO_LAYERS):
                row = layer(halo_start[:, here] + jnp.int16(4 * v), chosen, even, odd)
                put_back(row, jnp.int16(32 + v), spots, ranks, values)
            totals = apply_tile(tile, values)
            for c in range(3):
                partial[c, pl.ds(pl.multiple_of(tile * 8, 8), 8), :] = totals[c]
        return carry

    lax.fori_loop(0, groups // unroll, some_tiles, 0)

    @pl.when(most[1] >= HALO_LAYERS)
    def _():
        def one_tile(tile, carry):
            here = pl.ds(pl.multiple_of(tile * LANES, LANES), LANES)

            def more(v, flat):
                values = [list(flat[:3]), list(flat[3:])]
                row = layer(halo_start[:, here] + splat(4 * v), halves_of(picks, here), even, odd)
                put_back(row, splat(32 + v), halves_of(spot, here), halves_of(rank, here), values)
                return tuple(values[0] + values[1])

            empty = (jnp.zeros((PACK, LANES), BF16),) * 6
            flat = lax.fori_loop(HALO_LAYERS, most[1] + 1, more, empty)
            totals = apply_tile(tile, [flat[:3], flat[3:]])
            for c in range(3):
                rows = pl.ds(pl.multiple_of(tile * 8, 8), 8)
                partial[c, rows, :] = partial[c, rows, :] + totals[c]
            return carry

        lax.fori_loop(0, groups, one_tile, 0)

    remainder = []
    for e in range(3):
        total = partial[e, pl.ds(0, groups, stride=8), :]
        for row in range(1, 8):
            total = total + partial[e, pl.ds(row, groups, stride=8), :]
        remainder.append(residual[e] - smooth[e] - total)
    solved = dense_solve(dinv, remainder)
    for c in range(3):
        change = scale_old * update[c] + scale_new * solved[c]
        total = smooth[c] + change
        new_smooth[c] = total
        if stage < SWEEPS - 1:
            new_update[c] = change
            out_outer[c] = total.astype(BF16)
            out_inner[c] = total.astype(BF16)


def coarse_kernel(*refs):
    (place, base, own_couple) = refs[:3]
    first, second, third = refs[3:5], refs[5:7], refs[7:9]
    far_after, far_before, aggregate, smooth = refs[9:13]
    out, field, links, kept = refs[13:]
    subs, me = place[0], place[1]
    groups = base.shape[1]
    even = (me & 1) == 0

    def valid(row):
        inside = jnp.logical_and(me + row >= 0, me + row < subs)
        return jnp.where(inside, 1.0, 0.0).astype(F32)

    def from_after(pair, start):
        return lambda i: jnp.where(
            even, pair[0][start + i].astype(F32), pair[1][start + i].astype(F32)
        )

    def from_before(pair, start):
        return from_after((pair[1], pair[0]), start)

    def plain(ref, start):
        return lambda i: ref[start + i].astype(F32)

    def either(ref, when_even, when_odd):
        return lambda i: jnp.where(
            even, ref[when_even + i].astype(F32), ref[when_odd + i].astype(F32)
        )

    base_rows = {
        -5: either(far_after, 0, 6),
        -4: plain(far_after, 3),
        -3: either(far_after, 6, 0),
        -2: from_after(third, 3),
        -1: from_after(second, 3),
        1: from_before(second, 3),
        2: from_before(third, 3),
        3: either(far_before, 0, 6),
        4: plain(far_before, 3),
        5: either(far_before, 6, 0),
    }
    link_rows = {
        -4: plain(far_after, 9),
        -3: either(far_after, 17, 13),
        -2: from_after(second, 6),
        -1: from_after(first, 3),
        1: from_before(first, 3),
        2: from_before(second, 6),
        3: either(far_before, 13, 17),
        4: plain(far_before, 9),
    }

    def base_of(row, c):
        if row == 0:
            return base[c]
        return base_rows[row](c) * valid(row)

    for k in range(4):
        for g in range(groups):
            links[STEPS - 1, k, g : g + 1, :] = own_couple[
                k : k + 1, g * LANES : (g + 1) * LANES
            ]
    for row, read in link_rows.items():
        for k in range(4):
            links[row + STEPS - 1, k] = read(k) * valid(row)
    lane = lax.broadcasted_iota(jnp.int32, (groups, LANES), 1)
    line = lax.broadcasted_iota(jnp.int32, (groups, LANES), 0)
    inner_first = jnp.logical_or(lane > 0, line > 0)
    inner_last = jnp.logical_or(lane < LANES - 1, line < groups - 1)
    for row in range(2 * STEPS - 1):
        links[row, 2] = jnp.where(inner_first, links[row, 2], 0.0)
        links[row, 3] = jnp.where(inner_last, links[row, 3], 0.0)
    for row in range(-STEPS, STEPS + 1):
        for c in range(3):
            value = base_of(row, c)
            kept[row + STEPS, c] = value
            field[0, row + STEPS, c] = value
    for step in range(STEPS):
        old, new = step % 2, (step + 1) % 2
        reach = STEPS - 1 - step
        for row in range(-reach, reach + 1):
            spot = row + STEPS
            weights = [links[row + STEPS - 1, k] for k in range(4)]
            for c in range(3):
                x = field[old, spot, c]
                right = pltpu.roll(x, 1, 1)
                right = jnp.where(lane == 0, pltpu.roll(right, 1, 0), right)
                left = pltpu.roll(x, LANES - 1, 1)
                left = jnp.where(lane == LANES - 1, pltpu.roll(left, groups - 1, 0), left)
                field[new, spot, c] = kept[spot, c] + (
                    weights[0] * field[old, spot - 1, c]
                    + weights[1] * field[old, spot + 1, c]
                    + weights[2] * right
                    + weights[3] * left
                )
    final = STEPS % 2
    agg = aggregate[...] & (groups * LANES - 1)
    for block in range(agg.shape[0] // 8):
        index = agg[block * 8 : (block + 1) * 8]
        low = index & (LANES - 1)
        high = index >> 7
        found = [jnp.zeros((8, LANES), F32)] * 3
        for g in range(groups):
            chosen = high == g
            for c in range(3):
                rows = jnp.broadcast_to(field[final, STEPS, c, g : g + 1, :], (8, LANES))
                found[c] = jnp.where(chosen, lane_gather(rows, low), found[c])
        for c in range(3):
            result = smooth[c, block * 8 : (block + 1) * 8, :] + found[c]
            for r in range(8):
                lanes = slice((block * 8 + r) * LANES, (block * 8 + r + 1) * LANES)
                out[c : c + 1, lanes] = result[r : r + 1]


def shifted(value, steps):
    count = lax.axis_size("sub")
    return lax.ppermute(value, "sub", [(i, (i + steps) % count) for i in range(count)])


def exchanged_by_pairs(outer, inner):
    count = lax.axis_size("sub")
    across = [(i, (i + 1) % count) for i in range(1, count, 2)]
    within = [(i, i + 1) for i in range(0, count, 2)]
    outer = lax.ppermute(outer, "sub", across + [(j, i) for i, j in across])
    inner = lax.ppermute(inner, "sub", within + [(j, i) for i, j in within])
    return outer, inner


def body(
    fine_residual, bonds, bond_col, ghost_points, fine_dinv, aggregate, coarse_dinv, coarse_couple
):
    points = fine_residual.shape[1]
    groups = points // LANES
    bonds_of = bond_col.shape[0]
    per_group = coarse_dinv.shape[2]
    coarse_groups = per_group // LANES
    assert per_group & (per_group - 1) == 0
    sub = lax.axis_index("sub")
    doms = lax.axis_size("dom")
    ghost = ghost_points.reshape(-1, LANES)
    agg = aggregate.reshape(groups, LANES)
    relaid = bonds.transpose(1, 2, 0, 3)
    sds = jax.ShapeDtypeStruct
    field = sds((3, groups, LANES), F32)
    coarse_field = sds((3, coarse_groups, LANES), F32)

    def message(rows):
        return sds((rows, groups, LANES), BF16)

    dinv, residual, smooth, packed, rhs = call(
        first_kernel,
        (sds((3, 3, groups, LANES), F32), field, field, message(7), coarse_field),
        tuple(
            pltpu.with_memory_space_constraint(x, pltpu.HBM)
            for x in (fine_residual, agg, fine_dinv, coarse_couple)
        ),
        scratch=[
            VMEM(fine_residual.shape, F32),
            VMEM(agg.shape, jnp.int32),
            VMEM(fine_dinv.shape, F32),
            VMEM(coarse_couple.shape, F32),
            pltpu.SemaphoreType.DMA((4,)),
        ],
        us=2.2,
        spaces={i: pltpu.HBM for i in range(4)},
    )
    update = smooth
    own_packed = packed
    place = jnp.stack([jnp.int32(lax.axis_size("sub")), sub.astype(jnp.int32)])
    def exchanged(value, step):
        return lax.ppermute(value, "dom", [(i, i ^ step) for i in range(doms)])

    arrived = exchanged(rhs, 1)
    columns, rhs = lax.optimization_barrier((bond_col, rhs))

    def shorts(rows):
        return sds((rows, points), jnp.int16)

    picks, start, halo_start, spot, rank, most = call(
        prepare_kernel,
        (
            shorts(bonds_of),
            shorts(PACK),
            shorts(PACK),
            shorts(bonds_of),
            shorts(bonds_of),
            sds((2,), jnp.int32),
        ),
        (columns,),
        scratch=[VMEM((8 * (bonds_of + 2), LANES), jnp.int32)],
        us=2.5,
    )
    start, rhs = lax.optimization_barrier((start, rhs))
    rhs = rhs + arrived
    packed, rhs = lax.optimization_barrier((packed, rhs))
    arrived = exchanged(rhs, 2)
    first = arrived_sides = exchanged_by_pairs(packed, packed)
    rhs = rhs + arrived
    arrived = exchanged(rhs, 4)
    start, rhs = lax.optimization_barrier((start, rhs))

    factor = HALF / CENTER
    for stage in range(SWEEPS):
        factor_new = 1.0 / (2.0 * CENTER / HALF - factor)
        found = call(
            functools.partial(local_kernel, first=0, tiles=groups),
            sds((3, bonds_of, points), BF16),
            (smooth, picks, start, spot, rank, most),
            us=3.5,
            spaces={5: pltpu.SMEM},
        )
        if stage == SWEEPS - 1:
            found, far_after, far_before = lax.optimization_barrier(
                (found, far_after, far_before)
            )
        inputs = [place, most, picks, halo_start, spot, rank, ghost, *arrived_sides]
        inputs += [residual, dinv, smooth, update, relaid, found]
        if stage == 0:
            inputs += [rhs, arrived, coarse_dinv]
            outs = (field, field, coarse_field, message(10), message(10))
        elif stage == 1:
            inputs += [*first, base, own_packed]
            outs = (field, field, message(6), message(6), message(21))
        else:
            outs = (field,)
        result = call(
            functools.partial(
                halo_kernel,
                stage=stage,
                scale_old=factor_new * factor,
                scale_new=2.0 * factor_new / HALF,
            ),
            outs,
            inputs,
            scratch=[VMEM((3, groups, LANES), F32)] * 2 + [VMEM((3, 8 * groups, LANES), F32)],
            us=2.5,
            spaces={0: pltpu.SMEM, 1: pltpu.SMEM},
        )
        factor = factor_new
        if stage == 0:
            smooth, update, base, outer, inner = result
            second = arrived_sides = exchanged_by_pairs(outer, inner)
        elif stage == 1:
            smooth, update, outer, inner, far = result
            third = arrived_sides = exchanged_by_pairs(outer, inner)
            far_after = shifted(far, 4)
            far_before = shifted(far, -4)
        else:
            (smooth,) = result
    return call(
        coarse_kernel,
        sds((3, points), F32),
        (
            place,
            base,
            coarse_couple,
            *first,
            *second,
            *third,
            far_after,
            far_before,
            agg,
            smooth,
        ),
        scratch=[
            VMEM((2, 2 * STEPS + 1, 3, coarse_groups, LANES), F32),
            VMEM((2 * STEPS - 1, 4, coarse_groups, LANES), F32),
            VMEM((2 * STEPS + 1, 3, coarse_groups, LANES), F32),
        ],
        us=2.0,
        spaces={0: pltpu.SMEM},
    )


def solution(mesh):
    placed = (
        P(None, ("dom", "sub")),
        P(None, None, None, ("dom", "sub")),
        P(None, ("dom", "sub")),
        P(("dom", "sub"), None, None),
        P(None, None, ("dom", "sub")),
        P(("dom", "sub")),
        P(None, None, "sub"),
        P(None, "sub"),
    )
    return jax.shard_map(
        body, mesh=mesh, in_specs=placed, out_specs=P(None, ("dom", "sub")), check_vma=False
    )
```

```python
import functools

import jax
import jax.numpy as jnp
from jax import lax
from jax.experimental import pallas as pl
from jax.experimental.pallas import tpu as pltpu
from jax.sharding import PartitionSpec as P

SWEEPS = 3
STEPS = 5
LOW_EIG = 0.3
HIGH_EIG = 2.2
CENTER = (HIGH_EIG + LOW_EIG) / 2.0
HALF = (HIGH_EIG - LOW_EIG) / 2.0
LANES = 128
PACK = 16
F32 = jnp.float32
BF16 = jnp.bfloat16
VMEM = pltpu.VMEM


def gather(rows, index, axis):
    numbers = lax.GatherDimensionNumbers(
        offset_dims=(),
        collapsed_slice_dims=(axis,),
        start_index_map=(axis,),
        operand_batching_dims=(1 - axis,),
        start_indices_batching_dims=(1 - axis,),
    )
    return lax.gather(
        rows,
        index[..., None],
        numbers,
        (1, 1),
        mode=lax.GatherScatterMode.PROMISE_IN_BOUNDS,
    )


def lane_gather(rows, index):
    return gather(rows, index, 1)


def row_gather(rows, index):
    return gather(rows, index, 0)


def sorting_network(count):
    pairs = []
    span = 1
    while span < count:
        gap = span
        while gap >= 1:
            for j in range(gap % span, count - gap, 2 * gap):
                for i in range(min(gap, count - j - gap)):
                    if (i + j) // (2 * span) == (i + j + gap) // (2 * span):
                        pairs.append((i + j, i + j + gap))
            gap //= 2
        span *= 2
    return pairs


def sort_planes(planes):
    planes = list(planes)
    for i, j in sorting_network(len(planes)):
        planes[i], planes[j] = (
            jnp.minimum(planes[i], planes[j]),
            jnp.maximum(planes[i], planes[j]),
        )
    return planes


def call(kernel, out, inputs, scratch=(), us=1.0, spaces={}, limit=16):
    return pl.pallas_call(
        kernel,
        out_shape=out,
        in_specs=[
            pl.BlockSpec(memory_space=spaces.get(i, VMEM)) for i in range(len(inputs))
        ],
        out_specs=jax.tree.map(
            lambda _: pl.BlockSpec(memory_space=VMEM), out
        ),
        scratch_shapes=list(scratch),
        cost_estimate=pl.CostEstimate(
            flops=int(us * 1.0e9), transcendentals=0, bytes_accessed=int(us * 1.0e6)
        ),
        compiler_params=pltpu.CompilerParams(vmem_limit_bytes=limit * 1024 * 1024),
    )(*inputs)


def rows_of(ref, lead, group):
    return ref[lead + (slice(group * LANES, (group + 1) * LANES),)]


def first_kernel(*refs):
    sources = refs[:4]
    dense_dinv, dense_residual, smooth, message, rhs = refs[4:9]
    residual, aggregate, dinv, couple, semaphores = refs[9:]
    copies = [
        pltpu.make_async_copy(source, target, semaphores.at[i])
        for i, (source, target) in enumerate(zip(sources, (residual, aggregate, dinv, couple)))
    ]
    for copy in copies:
        copy.start()
    groups = smooth.shape[1]
    copies[0].wait()
    for g in range(groups):
        for e in range(3):
            dense_residual[e, g : g + 1, :] = residual[
                e : e + 1, g * LANES : (g + 1) * LANES
            ]
    copies[1].wait()
    restrict(dense_residual, aggregate, rhs)
    copies[2].wait()
    copies[3].wait()
    coarse_groups = message.shape[1]
    for g in range(groups):
        lanes = slice(g * LANES, (g + 1) * LANES)
        for e in range(3):
            for c in range(3):
                dense_dinv[c, e, g : g + 1, :] = dinv[c, e : e + 1, lanes]
    for g in range(coarse_groups):
        lanes = slice(g * LANES, (g + 1) * LANES)
        for k in range(4):
            message[3 + k, g : g + 1, :] = couple[k : k + 1, lanes].astype(BF16)
    for c in range(3):
        total = dense_dinv[c, 0] * dense_residual[0]
        for e in range(1, 3):
            total = total + dense_dinv[c, e] * dense_residual[e]
        total = total * (1.0 / CENTER)
        smooth[c] = total
        message[c] = total.astype(BF16)


def restrict(residual, aggregate, out):
    groups = residual.shape[1]
    bins = out.shape[1]
    agg = aggregate[...] & (bins * LANES - 1)
    low = agg & (LANES - 1)
    high = agg >> 7
    batch = 4
    total = [jnp.zeros((2 * bins, LANES), F32) for c in range(3)]
    lane_ids = lax.broadcasted_iota(jnp.int32, (LANES, LANES), 0)
    bin_ids = lax.broadcasted_iota(jnp.int32, (bins, LANES), 0)
    for block in range(groups // batch):
        onehot = []
        spread = [[] for c in range(3)]
        for g in range(block * batch, (block + 1) * batch):
            same = jnp.broadcast_to(low[g : g + 1], (LANES, LANES)) == lane_ids
            onehot.append(jnp.where(same, 1.0, 0.0).astype(BF16))
            chosen = jnp.broadcast_to(high[g : g + 1], (bins, LANES)) == bin_ids
            for c in range(3):
                value = residual[c, g : g + 1, :]
                upper = value.astype(BF16).astype(F32)
                lower = value - upper
                spread[c].append(
                    jnp.concatenate(
                        [
                            jnp.where(chosen, jnp.broadcast_to(part, (bins, LANES)), 0.0)
                            for part in (upper, lower)
                        ],
                        axis=0,
                    ).astype(BF16)
                )
        onehot = jnp.concatenate(onehot, axis=1)
        for c in range(3):
            total[c] = total[c] + lax.dot_general(
                jnp.concatenate(spread[c], axis=1),
                onehot,
                (((1,), (1,)), ((), ())),
                preferred_element_type=F32,
            )
    for c in range(3):
        out[c] = total[c][:bins] + total[c][bins:]


def spread_max(values):
    top = jnp.max(jnp.max(values, axis=1, keepdims=True), axis=0, keepdims=True)
    return jnp.broadcast_to(top, values.shape)


def prepare_kernel(col, picks, start, halo_start, spot, rank, most, flip):
    bonds_of = col.shape[0]
    groups = col.shape[1] // LANES
    stride = bonds_of + 1

    def eight_tiles(block, carry):
        best, halo_best = carry

        def lanes_of(t):
            return pl.ds(pl.multiple_of((block * 8 + t) * LANES, LANES), LANES)

        for t in range(8):
            flip[pl.ds(t * stride, bonds_of), :] = col[:, lanes_of(t)]
        keys = []
        for k in range(bonds_of):
            c = flip[pl.ds(k, 8, stride=stride), :]
            keys.append(((c >> 8) << 13) | (k << 8) | (c & 255))
        keys = sort_planes(keys)
        pairs = [key >> 13 for key in keys]
        ranks = [jnp.zeros((8, LANES), jnp.int32)]
        for k in range(1, bonds_of):
            ranks.append(jnp.where(pairs[k] == pairs[k - 1], ranks[k - 1] + 1, 0))
        back = []
        here = jnp.zeros((8, LANES), jnp.int32)
        for k in range(bonds_of):
            local = pairs[k] < PACK
            here = jnp.maximum(here, jnp.where(local, ranks[k], 0))
            halo_best = jnp.maximum(halo_best, jnp.where(local, 0, ranks[k]))
            code = jnp.where(
                local,
                (ranks[k] << 4) | pairs[k],
                ((ranks[k] >> 2) << 4) | ((ranks[k] & 3) << 2) | ((pairs[k] - PACK) + (32 << 4)),
            )
            back.append((((keys[k] >> 8) & 31) << 10) | code)
            flip[pl.ds(k, 8, stride=stride), :] = keys[k]
        row = lax.broadcasted_iota(jnp.int32, (PACK, LANES), 0)
        for t in range(8):
            halves = [flip[pl.ds(t * stride + h * PACK, PACK), :] for h in range(2)]
            for h in range(2):
                picks[h * PACK : (h + 1) * PACK, lanes_of(t)] = (halves[h] & 255).astype(jnp.int16)
            first, second = [(x >> 13).astype(jnp.int16) for x in halves]
            for target, pair, extra in (
                (start, row.astype(jnp.int16), None),
                (halo_start, (PACK + (row & 3)).astype(jnp.int16), (row >> 2).astype(jnp.int16)),
            ):
                place = jnp.zeros((PACK, LANES), jnp.int16)
                for step in (16, 8, 4, 2, 1, 1):
                    probe = place + jnp.int16(step - 1)
                    inner = probe & jnp.int16(PACK - 1)
                    value = jnp.where(
                        probe < PACK, row_gather(first, inner), row_gather(second, inner)
                    )
                    place = jnp.where(value < pair, place + jnp.int16(step), place)
                target[:, lanes_of(t)] = place if extra is None else place + extra
        back = sort_planes(back)
        for k in range(bonds_of):
            flip[pl.ds(k, 8, stride=stride), :] = back[k] & 1023
        for t in range(8):
            for h in range(2):
                code = flip[pl.ds(t * stride + h * PACK, PACK), :]
                rows = slice(h * PACK, (h + 1) * PACK)
                spot[rows, lanes_of(t)] = (code & 15).astype(jnp.int16)
                rank[rows, lanes_of(t)] = (code >> 4).astype(jnp.int16)
        most[pl.ds(pl.multiple_of(block * 8, 8), 8), :] = spread_max(here)
        return jnp.maximum(best, here), halo_best

    zero = jnp.zeros((8, LANES), jnp.int32)
    best, halo_best = lax.fori_loop(0, groups // 8, eight_tiles, (zero, zero))
    most[groups : groups + 8, :] = spread_max(best)
    most[groups + 8 :, :] = spread_max(halo_best) >> 2


def layer(place, picks, even, odd):
    inner = place & jnp.int16(PACK - 1)
    pick = jnp.where(
        place < PACK, row_gather(picks[0], inner), row_gather(picks[1], inner)
    )
    lane = pick & jnp.int16(LANES - 1)
    second = pick >= LANES
    return [
        jnp.where(second, lane_gather(odd[e], lane), lane_gather(even[e], lane))
        for e in range(3)
    ]


def put_back(values, number, spots, ranks, out):
    for h in range(2):
        hit = ranks[h] == number
        for e in range(3):
            out[h][e] = jnp.where(hit, row_gather(values[e], spots[h]), out[h][e])


def halves_of(ref, lanes):
    return [ref[h * PACK : (h + 1) * PACK, lanes] for h in range(2)]


def splat(number):
    return jnp.full((PACK, LANES), number, jnp.int32).astype(jnp.int16)


LAYERS = 10
HALO_LAYERS = 3


def local_kernel(smooth, picks, start, spot, rank, most, out, *, first, tiles, unroll=8):
    even = [smooth[e, pl.ds(0, PACK, stride=2), :].astype(BF16) for e in range(3)]
    odd = [smooth[e, pl.ds(1, PACK, stride=2), :].astype(BF16) for e in range(3)]

    def some_tiles(t, carry):
        for u in range(unroll):
            source = pl.ds(pl.multiple_of((first + t * unroll + u) * LANES, LANES), LANES)
            target = pl.ds(pl.multiple_of((t * unroll + u) * LANES, LANES), LANES)
            place = start[:, source]
            chosen = halves_of(picks, source)
            spots, ranks = halves_of(spot, source), halves_of(rank, source)
            found = [[jnp.zeros((PACK, LANES), BF16)] * 3 for h in range(2)]
            for m in range(LAYERS):
                values = layer(place + jnp.int16(m), chosen, even, odd)
                put_back(values, jnp.int16(m), spots, ranks, found)
            for h in range(2):
                for e in range(3):
                    out[e, h * PACK : (h + 1) * PACK, target] = found[h][e]
        return carry

    lax.fori_loop(0, tiles // unroll, some_tiles, 0)

    @pl.when(most[smooth.shape[1], 0] >= LAYERS)
    def _():
        def eight_tiles(block, carry):
            def more(m, inner):
                number = splat(m)
                for t in range(8):
                    tile = block * 8 + t
                    source = pl.ds(pl.multiple_of((first + tile) * LANES, LANES), LANES)
                    target = pl.ds(pl.multiple_of(tile * LANES, LANES), LANES)
                    found = [
                        [out[e, h * PACK : (h + 1) * PACK, target] for e in range(3)]
                        for h in range(2)
                    ]
                    values = layer(
                        start[:, source] + number, halves_of(picks, source), even, odd
                    )
                    put_back(
                        values, number, halves_of(spot, source), halves_of(rank, source), found
                    )
                    for h in range(2):
                        for e in range(3):
                            out[e, h * PACK : (h + 1) * PACK, target] = found[h][e]
                return inner

            lax.fori_loop(LAYERS, most[first + block * 8, 0] + 1, more, 0)
            return carry

        lax.fori_loop(0, tiles // 8, eight_tiles, 0)


def dense_solve(matrix, vector):
    solved = []
    for c in range(3):
        total = matrix[c, 0] * vector[0]
        for e in range(1, 3):
            total = total + matrix[c, e] * vector[e]
        solved.append(total)
    return solved


def halo_kernel(*refs, stage, scale_old, scale_new, unroll=8):
    (place, most, picks, halo_start, spot, rank, ghost, outer, inner) = refs[:9]
    (residual, dinv, smooth, update, bonds, local_found) = refs[9:15]
    refs = refs[15:]
    if stage == 0:
        rhs, arrived, coarse_dinv = refs[:3]
        new_smooth, new_update, base, out_outer, out_inner = refs[3:8]
        refs = refs[8:]
    elif stage == 1:
        first_outer, first_inner, base, couple_own = refs[:4]
        new_smooth, new_update, out_outer, out_inner, far = refs[4:9]
        refs = refs[9:]
    else:
        (new_smooth,) = refs[:1]
        refs = refs[1:]
    applied, other, partial = refs
    groups = smooth.shape[1]
    if stage == 0:
        vector = [rhs[e] + arrived[e] for e in range(3)]
        coarse_groups = base.shape[1]
        for c in range(3):
            for g in range(coarse_groups):
                lanes = slice(g * LANES, (g + 1) * LANES)
                total = coarse_dinv[c, 0:1, lanes] * vector[0][g : g + 1]
                for e in range(1, 3):
                    total = total + coarse_dinv[c, e : e + 1, lanes] * vector[e][g : g + 1]
                base[c, g : g + 1, :] = total
        for c in range(3):
            row = base[c].astype(BF16)
            out_outer[3 + c] = row
            out_inner[3 + c] = row
        out_outer[6:10] = inner[3:7]
        out_inner[6:10] = outer[3:7]
    elif stage == 1:
        out_outer[3:6] = inner[3:6]
        out_inner[3:6] = outer[3:6]
        far[0:3] = outer[3:6]
        far[3:6] = base[...].astype(BF16)
        far[6:9] = inner[3:6]
        far[9:13] = couple_own[3:7]
        far[13:17] = first_outer[3:7]
        far[17:21] = first_inner[3:7]
    wanted = ghost[...]
    half = wanted.shape[0] // 2
    low = wanted & (LANES - 1)
    high = wanted >> 7
    upper = jnp.where(lax.broadcasted_iota(jnp.int32, wanted.shape, 0) < half, 1, 0)
    from_outer = (upper ^ (place[...] & 1)) == 1
    found = [jnp.zeros(wanted.shape, F32)] * 3
    for e in range(3):
        applied[e] = outer[e].astype(F32)
        other[e] = inner[e].astype(F32)
    for g in range(groups):
        chosen = high == g
        for e in range(3):
            rows = jnp.where(
                from_outer,
                jnp.broadcast_to(applied[e, g : g + 1, :], wanted.shape),
                jnp.broadcast_to(other[e, g : g + 1, :], wanted.shape),
            )
            found[e] = jnp.where(chosen, lane_gather(rows, low), found[e])
    pair = (lax.broadcasted_iota(jnp.int32, wanted.shape, 0) & 3) * 2

    def four_times(rows):
        return jnp.concatenate([rows, rows], axis=0).astype(BF16)

    even = [four_times(row_gather(found[e], pair)) for e in range(3)]
    odd = [four_times(row_gather(found[e], pair + 1)) for e in range(3)]

    def apply_tile(tile, values):
        here = pl.ds(pl.multiple_of(tile * LANES, LANES), LANES)
        totals = []
        for c in range(3):
            total = jnp.zeros((PACK, LANES), F32)
            for h in range(2):
                for e in range(3):
                    block = bonds[c, e, h * PACK : (h + 1) * PACK, here].astype(F32)
                    total = total + block * values[h][e].astype(F32)
            totals.append(total[:8] + total[8:])
        return totals

    def some_tiles(t, carry):
        for u in range(unroll):
            tile = t * unroll + u
            here = pl.ds(pl.multiple_of(tile * LANES, LANES), LANES)
            chosen = halves_of(picks, here)
            spots, ranks = halves_of(spot, here), halves_of(rank, here)
            values = [
                [local_found[e, h * PACK : (h + 1) * PACK, here] for e in range(3)]
                for h in range(2)
            ]
            for v in range(HALO_LAYERS):
                row = layer(halo_start[:, here] + jnp.int16(4 * v), chosen, even, odd)
                put_back(row, jnp.int16(32 + v), spots, ranks, values)
            totals = apply_tile(tile, values)
            for c in range(3):
                partial[c, pl.ds(pl.multiple_of(tile * 8, 8), 8), :] = totals[c]
        return carry

    lax.fori_loop(0, groups // unroll, some_tiles, 0)

    last_layer = most[groups + 8, 0]

    @pl.when(last_layer >= HALO_LAYERS)
    def _():
        def one_tile(tile, carry):
            here = pl.ds(pl.multiple_of(tile * LANES, LANES), LANES)

            def more(v, flat):
                values = [list(flat[:3]), list(flat[3:])]
                row = layer(halo_start[:, here] + splat(4 * v), halves_of(picks, here), even, odd)
                put_back(row, splat(32 + v), halves_of(spot, here), halves_of(rank, here), values)
                return tuple(values[0] + values[1])

            empty = (jnp.zeros((PACK, LANES), BF16),) * 6
            flat = lax.fori_loop(HALO_LAYERS, last_layer + 1, more, empty)
            totals = apply_tile(tile, [flat[:3], flat[3:]])
            for c in range(3):
                rows = pl.ds(pl.multiple_of(tile * 8, 8), 8)
                partial[c, rows, :] = partial[c, rows, :] + totals[c]
            return carry

        lax.fori_loop(0, groups, one_tile, 0)

    remainder = []
    for e in range(3):
        total = partial[e, pl.ds(0, groups, stride=8), :]
        for row in range(1, 8):
            total = total + partial[e, pl.ds(row, groups, stride=8), :]
        remainder.append(residual[e] - smooth[e] - total)
    solved = dense_solve(dinv, remainder)
    for c in range(3):
        change = scale_old * update[c] + scale_new * solved[c]
        total = smooth[c] + change
        new_smooth[c] = total
        if stage < SWEEPS - 1:
            new_update[c] = change
            out_outer[c] = total.astype(BF16)
            out_inner[c] = total.astype(BF16)


def coarse_kernel(*refs, subs):
    (place, base, own_couple) = refs[:3]
    first, second, third = refs[3:5], refs[5:7], refs[7:9]
    far_after, far_before, aggregate, smooth = refs[9:13]
    out, field, links, kept = refs[13:]
    groups = base.shape[1]
    me = jnp.concatenate([place[...]] * (groups // 8), axis=0)
    even = (me & 1) == 0

    def valid(row):
        if row < 0:
            return jnp.where(me + row >= 0, 1.0, 0.0)
        return jnp.where(me + row < subs, 1.0, 0.0)

    def from_after(pair, start):
        return lambda i: jnp.where(
            even, pair[0][start + i].astype(F32), pair[1][start + i].astype(F32)
        )

    def from_before(pair, start):
        return from_after((pair[1], pair[0]), start)

    def plain(ref, start):
        return lambda i: ref[start + i].astype(F32)

    def either(ref, when_even, when_odd):
        return lambda i: jnp.where(
            even, ref[when_even + i].astype(F32), ref[when_odd + i].astype(F32)
        )

    base_rows = {
        -5: either(far_after, 0, 6),
        -4: plain(far_after, 3),
        -3: either(far_after, 6, 0),
        -2: from_after(third, 3),
        -1: from_after(second, 3),
        1: from_before(second, 3),
        2: from_before(third, 3),
        3: either(far_before, 0, 6),
        4: plain(far_before, 3),
        5: either(far_before, 6, 0),
    }
    link_rows = {
        -4: plain(far_after, 9),
        -3: either(far_after, 17, 13),
        -2: from_after(second, 6),
        -1: from_after(first, 3),
        1: from_before(first, 3),
        2: from_before(second, 6),
        3: either(far_before, 13, 17),
        4: plain(far_before, 9),
    }

    def base_of(row, c):
        if row == 0:
            return base[c]
        return base_rows[row](c) * valid(row)

    for k in range(4):
        for g in range(groups):
            links[STEPS - 1, k, g : g + 1, :] = own_couple[
                k : k + 1, g * LANES : (g + 1) * LANES
            ]
    for row, read in link_rows.items():
        for k in range(4):
            links[row + STEPS - 1, k] = read(k) * valid(row)
    lane = lax.broadcasted_iota(jnp.int32, (groups, LANES), 1)
    line = lax.broadcasted_iota(jnp.int32, (groups, LANES), 0)
    inner_first = jnp.logical_or(lane > 0, line > 0)
    inner_last = jnp.logical_or(lane < LANES - 1, line < groups - 1)
    for row in range(2 * STEPS - 1):
        links[row, 2] = jnp.where(inner_first, links[row, 2], 0.0)
        links[row, 3] = jnp.where(inner_last, links[row, 3], 0.0)
    for row in range(-STEPS, STEPS + 1):
        for c in range(3):
            value = base_of(row, c)
            kept[row + STEPS, c] = value
            field[0, row + STEPS, c] = value
    for step in range(STEPS):
        old, new = step % 2, (step + 1) % 2
        reach = STEPS - 1 - step
        for row in range(-reach, reach + 1):
            spot = row + STEPS
            weights = [links[row + STEPS - 1, k] for k in range(4)]
            for c in range(3):
                x = field[old, spot, c]
                right = pltpu.roll(x, 1, 1)
                right = jnp.where(lane == 0, pltpu.roll(right, 1, 0), right)
                left = pltpu.roll(x, LANES - 1, 1)
                left = jnp.where(lane == LANES - 1, pltpu.roll(left, groups - 1, 0), left)
                field[new, spot, c] = kept[spot, c] + (
                    weights[0] * field[old, spot - 1, c]
                    + weights[1] * field[old, spot + 1, c]
                    + weights[2] * right
                    + weights[3] * left
                )
    final = STEPS % 2
    agg = aggregate[...] & (groups * LANES - 1)
    for block in range(agg.shape[0] // 8):
        index = agg[block * 8 : (block + 1) * 8]
        low = index & (LANES - 1)
        high = index >> 7
        found = [jnp.zeros((8, LANES), F32)] * 3
        for g in range(groups):
            chosen = high == g
            for c in range(3):
                rows = jnp.broadcast_to(field[final, STEPS, c, g : g + 1, :], (8, LANES))
                found[c] = jnp.where(chosen, lane_gather(rows, low), found[c])
        for c in range(3):
            result = smooth[c, block * 8 : (block + 1) * 8, :] + found[c]
            for r in range(8):
                lanes = slice((block * 8 + r) * LANES, (block * 8 + r + 1) * LANES)
                out[c : c + 1, lanes] = result[r : r + 1]


def shifted(value, steps):
    count = lax.axis_size("sub")
    return lax.ppermute(value, "sub", [(i, (i + steps) % count) for i in range(count)])


def exchanged_by_pairs(outer, inner):
    count = lax.axis_size("sub")
    across = [(i, (i + 1) % count) for i in range(1, count, 2)]
    within = [(i, i + 1) for i in range(0, count, 2)]
    outer = lax.ppermute(outer, "sub", across + [(j, i) for i, j in across])
    inner = lax.ppermute(inner, "sub", within + [(j, i) for i, j in within])
    return outer, inner


def body(
    fine_residual, bonds, bond_col, ghost_points, fine_dinv, aggregate, coarse_dinv, coarse_couple
):
    points = fine_residual.shape[1]
    groups = points // LANES
    bonds_of = bond_col.shape[0]
    per_group = coarse_dinv.shape[2]
    coarse_groups = per_group // LANES
    assert per_group & (per_group - 1) == 0
    sub = lax.axis_index("sub")
    doms = lax.axis_size("dom")
    ghost = ghost_points.reshape(-1, LANES)
    agg = aggregate.reshape(groups, LANES)
    relaid = bonds.transpose(1, 2, 0, 3)
    sds = jax.ShapeDtypeStruct
    field = sds((3, groups, LANES), F32)
    coarse_field = sds((3, coarse_groups, LANES), F32)

    def message(rows):
        return sds((rows, groups, LANES), BF16)

    dinv, residual, smooth, packed, rhs = call(
        first_kernel,
        (sds((3, 3, groups, LANES), F32), field, field, message(7), coarse_field),
        tuple(
            pltpu.with_memory_space_constraint(x, pltpu.HBM)
            for x in (fine_residual, agg, fine_dinv, coarse_couple)
        ),
        scratch=[
            VMEM(fine_residual.shape, F32),
            VMEM(agg.shape, jnp.int32),
            VMEM(fine_dinv.shape, F32),
            VMEM(coarse_couple.shape, F32),
            pltpu.SemaphoreType.DMA((4,)),
        ],
        us=2.2,
        spaces={i: pltpu.HBM for i in range(4)},
    )
    update = smooth
    own_packed = packed
    place = jnp.full((8, LANES), sub, jnp.int32)
    def exchanged(value, step):
        return lax.ppermute(value, "dom", [(i, i ^ step) for i in range(doms)])

    arrived = exchanged(rhs, 1)
    columns, rhs = lax.optimization_barrier((bond_col, rhs))

    def shorts(rows):
        return sds((rows, points), jnp.int16)

    picks, start, halo_start, spot, rank, most = call(
        prepare_kernel,
        (
            shorts(bonds_of),
            shorts(PACK),
            shorts(PACK),
            shorts(bonds_of),
            shorts(bonds_of),
            sds((groups + 16, LANES), jnp.int32),
        ),
        (columns,),
        scratch=[VMEM((8 * (bonds_of + 2), LANES), jnp.int32)],
        us=2.5,
    )
    start, rhs = lax.optimization_barrier((start, rhs))
    rhs = rhs + arrived
    packed, rhs = lax.optimization_barrier((packed, rhs))
    arrived = exchanged(rhs, 2)
    first = arrived_sides = exchanged_by_pairs(packed, packed)
    rhs = rhs + arrived
    arrived = exchanged(rhs, 4)
    start, rhs = lax.optimization_barrier((start, rhs))

    factor = HALF / CENTER
    for stage in range(SWEEPS):
        factor_new = 1.0 / (2.0 * CENTER / HALF - factor)
        found = call(
            functools.partial(local_kernel, first=0, tiles=groups),
            sds((3, bonds_of, points), BF16),
            (smooth, picks, start, spot, rank, most),
            us=3.5,
        )
        if stage == SWEEPS - 1:
            found, far_after, far_before = lax.optimization_barrier(
                (found, far_after, far_before)
            )
        inputs = [place, most, picks, halo_start, spot, rank, ghost, *arrived_sides]
        inputs += [residual, dinv, smooth, update, relaid, found]
        if stage == 0:
            inputs += [rhs, arrived, coarse_dinv]
            outs = (field, field, coarse_field, message(10), message(10))
        elif stage == 1:
            inputs += [*first, base, own_packed]
            outs = (field, field, message(6), message(6), message(21))
        else:
            outs = (field,)
        result = call(
            functools.partial(
                halo_kernel,
                stage=stage,
                scale_old=factor_new * factor,
                scale_new=2.0 * factor_new / HALF,
            ),
            outs,
            inputs,
            scratch=[VMEM((3, groups, LANES), F32)] * 2 + [VMEM((3, 8 * groups, LANES), F32)],
            us=2.5,
        )
        factor = factor_new
        if stage == 0:
            smooth, update, base, outer, inner = result
            second = arrived_sides = exchanged_by_pairs(outer, inner)
        elif stage == 1:
            smooth, update, outer, inner, far = result
            third = arrived_sides = exchanged_by_pairs(outer, inner)
            far_after = shifted(far, 4)
            far_before = shifted(far, -4)
        else:
            (smooth,) = result
    return call(
        functools.partial(coarse_kernel, subs=lax.axis_size("sub")),
        sds((3, points), F32),
        (
            place,
            base,
            coarse_couple,
            *first,
            *second,
            *third,
            far_after,
            far_before,
            agg,
            smooth,
        ),
        scratch=[
            VMEM((2, 2 * STEPS + 1, 3, coarse_groups, LANES), F32),
            VMEM((2 * STEPS - 1, 4, coarse_groups, LANES), F32),
            VMEM((2 * STEPS + 1, 3, coarse_groups, LANES), F32),
        ],
        us=2.0,
    )


def solution(mesh):
    placed = (
        P(None, ("dom", "sub")),
        P(None, None, None, ("dom", "sub")),
        P(None, ("dom", "sub")),
        P(("dom", "sub"), None, None),
        P(None, None, ("dom", "sub")),
        P(("dom", "sub")),
        P(None, None, "sub"),
        P(None, "sub"),
    )
    return jax.shard_map(
        body, mesh=mesh, in_specs=placed, out_specs=P(None, ("dom", "sub")), check_vma=False
    )
```

```python
import functools

import jax
import jax.numpy as jnp
from jax import lax
from jax.experimental import pallas as pl
from jax.experimental.pallas import tpu as pltpu
from jax.sharding import PartitionSpec as P

SWEEPS = 3
STEPS = 5
LOW_EIG = 0.3
HIGH_EIG = 2.2
CENTER = (HIGH_EIG + LOW_EIG) / 2.0
HALF = (HIGH_EIG - LOW_EIG) / 2.0
LANES = 128
PACK = 16
F32 = jnp.float32
BF16 = jnp.bfloat16
VMEM = pltpu.VMEM


def gather(rows, index, axis):
    numbers = lax.GatherDimensionNumbers(
        offset_dims=(),
        collapsed_slice_dims=(axis,),
        start_index_map=(axis,),
        operand_batching_dims=(1 - axis,),
        start_indices_batching_dims=(1 - axis,),
    )
    return lax.gather(
        rows,
        index[..., None],
        numbers,
        (1, 1),
        mode=lax.GatherScatterMode.PROMISE_IN_BOUNDS,
    )


def lane_gather(rows, index):
    return gather(rows, index, 1)


def row_gather(rows, index):
    return gather(rows, index, 0)


def sorting_network(count):
    pairs = []
    span = 1
    while span < count:
        gap = span
        while gap >= 1:
            for j in range(gap % span, count - gap, 2 * gap):
                for i in range(min(gap, count - j - gap)):
                    if (i + j) // (2 * span) == (i + j + gap) // (2 * span):
                        pairs.append((i + j, i + j + gap))
            gap //= 2
        span *= 2
    return pairs


def sort_planes(planes):
    planes = list(planes)
    for i, j in sorting_network(len(planes)):
        planes[i], planes[j] = (
            jnp.minimum(planes[i], planes[j]),
            jnp.maximum(planes[i], planes[j]),
        )
    return planes


def call(kernel, out, inputs, scratch=(), us=1.0, spaces={}, limit=16):
    return pl.pallas_call(
        kernel,
        out_shape=out,
        in_specs=[
            pl.BlockSpec(memory_space=spaces.get(i, VMEM)) for i in range(len(inputs))
        ],
        out_specs=jax.tree.map(
            lambda _: pl.BlockSpec(memory_space=VMEM), out
        ),
        scratch_shapes=list(scratch),
        cost_estimate=pl.CostEstimate(
            flops=int(us * 1.0e9), transcendentals=0, bytes_accessed=int(us * 1.0e6)
        ),
        compiler_params=pltpu.CompilerParams(vmem_limit_bytes=limit * 1024 * 1024),
    )(*inputs)


def rows_of(ref, lead, group):
    return ref[lead + (slice(group * LANES, (group + 1) * LANES),)]


def restrict_kernel(*refs):
    sources = refs[:2]
    dense_residual, rhs = refs[2:4]
    residual, aggregate, semaphores = refs[4:]
    copies = [
        pltpu.make_async_copy(source, target, semaphores.at[i])
        for i, (source, target) in enumerate(zip(sources, (residual, aggregate)))
    ]
    for copy in copies:
        copy.start()
    copies[0].wait()
    for g in range(dense_residual.shape[1]):
        for e in range(3):
            dense_residual[e, g : g + 1, :] = residual[
                e : e + 1, g * LANES : (g + 1) * LANES
            ]
    copies[1].wait()
    restrict(dense_residual, aggregate, rhs)


def first_kernel(dense_residual, dinv, couple, dense_dinv, smooth, message):
    groups = smooth.shape[1]
    coarse_groups = message.shape[1]
    for g in range(groups):
        lanes = slice(g * LANES, (g + 1) * LANES)
        for e in range(3):
            for c in range(3):
                dense_dinv[c, e, g : g + 1, :] = dinv[c, e : e + 1, lanes]
    for g in range(coarse_groups):
        lanes = slice(g * LANES, (g + 1) * LANES)
        for k in range(4):
            message[3 + k, g : g + 1, :] = couple[k : k + 1, lanes].astype(BF16)
    for c in range(3):
        total = dense_dinv[c, 0] * dense_residual[0]
        for e in range(1, 3):
            total = total + dense_dinv[c, e] * dense_residual[e]
        total = total * (1.0 / CENTER)
        smooth[c] = total
        message[c] = total.astype(BF16)


def restrict(residual, aggregate, out):
    groups = residual.shape[1]
    bins = out.shape[1]
    agg = aggregate[...] & (bins * LANES - 1)
    low = agg & (LANES - 1)
    high = agg >> 7
    batch = 4
    total = [jnp.zeros((2 * bins, LANES), F32) for c in range(3)]
    lane_ids = lax.broadcasted_iota(jnp.int32, (LANES, LANES), 0)
    bin_ids = lax.broadcasted_iota(jnp.int32, (bins, LANES), 0)
    for block in range(groups // batch):
        onehot = []
        spread = [[] for c in range(3)]
        for g in range(block * batch, (block + 1) * batch):
            same = jnp.broadcast_to(low[g : g + 1], (LANES, LANES)) == lane_ids
            onehot.append(jnp.where(same, 1.0, 0.0).astype(BF16))
            chosen = jnp.broadcast_to(high[g : g + 1], (bins, LANES)) == bin_ids
            for c in range(3):
                value = residual[c, g : g + 1, :]
                upper = value.astype(BF16).astype(F32)
                lower = value - upper
                spread[c].append(
                    jnp.concatenate(
                        [
                            jnp.where(chosen, jnp.broadcast_to(part, (bins, LANES)), 0.0)
                            for part in (upper, lower)
                        ],
                        axis=0,
                    ).astype(BF16)
                )
        onehot = jnp.concatenate(onehot, axis=1)
        for c in range(3):
            total[c] = total[c] + lax.dot_general(
                jnp.concatenate(spread[c], axis=1),
                onehot,
                (((1,), (1,)), ((), ())),
                preferred_element_type=F32,
            )
    for c in range(3):
        out[c] = total[c][:bins] + total[c][bins:]


def spread_max(values):
    top = jnp.max(jnp.max(values, axis=1, keepdims=True), axis=0, keepdims=True)
    return jnp.broadcast_to(top, values.shape)


def prepare_kernel(col, picks, start, halo_start, spot, rank, most, flip):
    bonds_of = col.shape[0]
    groups = col.shape[1] // LANES
    stride = bonds_of + 1

    def eight_tiles(block, carry):
        best, halo_best = carry

        def lanes_of(t):
            return pl.ds(pl.multiple_of((block * 8 + t) * LANES, LANES), LANES)

        for t in range(8):
            flip[pl.ds(t * stride, bonds_of), :] = col[:, lanes_of(t)]
        keys = []
        for k in range(bonds_of):
            c = flip[pl.ds(k, 8, stride=stride), :]
            keys.append(((c >> 8) << 13) | (k << 8) | (c & 255))
        keys = sort_planes(keys)
        pairs = [key >> 13 for key in keys]
        ranks = [jnp.zeros((8, LANES), jnp.int32)]
        for k in range(1, bonds_of):
            ranks.append(jnp.where(pairs[k] == pairs[k - 1], ranks[k - 1] + 1, 0))
        back = []
        here = jnp.zeros((8, LANES), jnp.int32)
        for k in range(bonds_of):
            local = pairs[k] < PACK
            here = jnp.maximum(here, jnp.where(local, ranks[k], 0))
            halo_best = jnp.maximum(halo_best, jnp.where(local, 0, ranks[k]))
            code = jnp.where(
                local,
                (ranks[k] << 4) | pairs[k],
                ((ranks[k] >> 2) << 4) | ((ranks[k] & 3) << 2) | ((pairs[k] - PACK) + (32 << 4)),
            )
            back.append((((keys[k] >> 8) & 31) << 10) | code)
            flip[pl.ds(k, 8, stride=stride), :] = keys[k]
        row = lax.broadcasted_iota(jnp.int32, (PACK, LANES), 0)
        for t in range(8):
            halves = [flip[pl.ds(t * stride + h * PACK, PACK), :] for h in range(2)]
            for h in range(2):
                picks[h * PACK : (h + 1) * PACK, lanes_of(t)] = (halves[h] & 255).astype(jnp.int16)
            first, second = [(x >> 13).astype(jnp.int16) for x in halves]
            for target, pair, extra in (
                (start, row.astype(jnp.int16), None),
                (halo_start, (PACK + (row & 3)).astype(jnp.int16), (row >> 2).astype(jnp.int16)),
            ):
                place = jnp.zeros((PACK, LANES), jnp.int16)
                for step in (16, 8, 4, 2, 1, 1):
                    probe = place + jnp.int16(step - 1)
                    inner = probe & jnp.int16(PACK - 1)
                    value = jnp.where(
                        probe < PACK, row_gather(first, inner), row_gather(second, inner)
                    )
                    place = jnp.where(value < pair, place + jnp.int16(step), place)
                target[:, lanes_of(t)] = place if extra is None else place + extra
        back = sort_planes(back)
        for k in range(bonds_of):
            flip[pl.ds(k, 8, stride=stride), :] = back[k] & 1023
        for t in range(8):
            for h in range(2):
                code = flip[pl.ds(t * stride + h * PACK, PACK), :]
                rows = slice(h * PACK, (h + 1) * PACK)
                spot[rows, lanes_of(t)] = (code & 15).astype(jnp.int16)
                rank[rows, lanes_of(t)] = (code >> 4).astype(jnp.int16)
        most[pl.ds(pl.multiple_of(block * 8, 8), 8), :] = spread_max(here)
        return jnp.maximum(best, here), halo_best

    zero = jnp.zeros((8, LANES), jnp.int32)
    best, halo_best = lax.fori_loop(0, groups // 8, eight_tiles, (zero, zero))
    most[groups : groups + 8, :] = spread_max(best)
    most[groups + 8 :, :] = spread_max(halo_best) >> 2


def layer(place, picks, even, odd):
    inner = place & jnp.int16(PACK - 1)
    pick = jnp.where(
        place < PACK, row_gather(picks[0], inner), row_gather(picks[1], inner)
    )
    lane = pick & jnp.int16(LANES - 1)
    second = pick >= LANES
    return [
        jnp.where(second, lane_gather(odd[e], lane), lane_gather(even[e], lane))
        for e in range(3)
    ]


def put_back(values, number, spots, ranks, out):
    for h in range(2):
        hit = ranks[h] == number
        for e in range(3):
            out[h][e] = jnp.where(hit, row_gather(values[e], spots[h]), out[h][e])


def halves_of(ref, lanes):
    return [ref[h * PACK : (h + 1) * PACK, lanes] for h in range(2)]


def splat(number):
    return jnp.full((PACK, LANES), number, jnp.int32).astype(jnp.int16)


LAYERS = 10
HALO_LAYERS = 3


def local_kernel(smooth, picks, start, spot, rank, most, out, *, first, tiles, unroll=8):
    even = [smooth[e, pl.ds(0, PACK, stride=2), :].astype(BF16) for e in range(3)]
    odd = [smooth[e, pl.ds(1, PACK, stride=2), :].astype(BF16) for e in range(3)]

    def some_tiles(t, carry):
        for u in range(unroll):
            source = pl.ds(pl.multiple_of((first + t * unroll + u) * LANES, LANES), LANES)
            target = pl.ds(pl.multiple_of((t * unroll + u) * LANES, LANES), LANES)
            place = start[:, source]
            chosen = halves_of(picks, source)
            spots, ranks = halves_of(spot, source), halves_of(rank, source)
            found = [[jnp.zeros((PACK, LANES), BF16)] * 3 for h in range(2)]
            for m in range(LAYERS):
                values = layer(place + jnp.int16(m), chosen, even, odd)
                put_back(values, jnp.int16(m), spots, ranks, found)
            for h in range(2):
                for e in range(3):
                    out[e, h * PACK : (h + 1) * PACK, target] = found[h][e]
        return carry

    lax.fori_loop(0, tiles // unroll, some_tiles, 0)

    @pl.when(most[smooth.shape[1], 0] >= LAYERS)
    def _():
        def eight_tiles(block, carry):
            def more(m, inner):
                number = splat(m)
                for t in range(8):
                    tile = block * 8 + t
                    source = pl.ds(pl.multiple_of((first + tile) * LANES, LANES), LANES)
                    target = pl.ds(pl.multiple_of(tile * LANES, LANES), LANES)
                    found = [
                        [out[e, h * PACK : (h + 1) * PACK, target] for e in range(3)]
                        for h in range(2)
                    ]
                    values = layer(
                        start[:, source] + number, halves_of(picks, source), even, odd
                    )
                    put_back(
                        values, number, halves_of(spot, source), halves_of(rank, source), found
                    )
                    for h in range(2):
                        for e in range(3):
                            out[e, h * PACK : (h + 1) * PACK, target] = found[h][e]
                return inner

            lax.fori_loop(LAYERS, most[first + block * 8, 0] + 1, more, 0)
            return carry

        lax.fori_loop(0, tiles // 8, eight_tiles, 0)


def dense_solve(matrix, vector):
    solved = []
    for c in range(3):
        total = matrix[c, 0] * vector[0]
        for e in range(1, 3):
            total = total + matrix[c, e] * vector[e]
        solved.append(total)
    return solved


def halo_kernel(*refs, stage, scale_old, scale_new, unroll=8):
    (place, most, picks, halo_start, spot, rank, ghost, outer, inner) = refs[:9]
    (residual, dinv, smooth, update, bonds) = refs[9:14]
    pieces = 2 if stage == SWEEPS - 1 else 1
    local_found = refs[14 : 14 + pieces]
    refs = refs[14 + pieces :]
    if stage == 0:
        rhs, arrived, coarse_dinv = refs[:3]
        new_smooth, new_update, base, out_outer, out_inner = refs[3:8]
        refs = refs[8:]
    elif stage == 1:
        first_outer, first_inner, base, couple_own = refs[:4]
        new_smooth, new_update, out_outer, out_inner, far = refs[4:9]
        refs = refs[9:]
    else:
        (new_smooth,) = refs[:1]
        refs = refs[1:]
    applied, other, partial = refs
    groups = smooth.shape[1]
    if stage == 0:
        vector = [rhs[e] + arrived[e] for e in range(3)]
        coarse_groups = base.shape[1]
        for c in range(3):
            for g in range(coarse_groups):
                lanes = slice(g * LANES, (g + 1) * LANES)
                total = coarse_dinv[c, 0:1, lanes] * vector[0][g : g + 1]
                for e in range(1, 3):
                    total = total + coarse_dinv[c, e : e + 1, lanes] * vector[e][g : g + 1]
                base[c, g : g + 1, :] = total
        for c in range(3):
            row = base[c].astype(BF16)
            out_outer[3 + c] = row
            out_inner[3 + c] = row
        out_outer[6:10] = inner[3:7]
        out_inner[6:10] = outer[3:7]
    elif stage == 1:
        out_outer[3:6] = inner[3:6]
        out_inner[3:6] = outer[3:6]
        far[0:3] = outer[3:6]
        far[3:6] = base[...].astype(BF16)
        far[6:9] = inner[3:6]
        far[9:13] = couple_own[3:7]
        far[13:17] = first_outer[3:7]
        far[17:21] = first_inner[3:7]
    wanted = ghost[...]
    half = wanted.shape[0] // 2
    low = wanted & (LANES - 1)
    high = wanted >> 7
    upper = jnp.where(lax.broadcasted_iota(jnp.int32, wanted.shape, 0) < half, 1, 0)
    from_outer = (upper ^ (place[...] & 1)) == 1
    found = [jnp.zeros(wanted.shape, F32)] * 3
    for e in range(3):
        applied[e] = outer[e].astype(F32)
        other[e] = inner[e].astype(F32)
    for g in range(groups):
        chosen = high == g
        for e in range(3):
            rows = jnp.where(
                from_outer,
                jnp.broadcast_to(applied[e, g : g + 1, :], wanted.shape),
                jnp.broadcast_to(other[e, g : g + 1, :], wanted.shape),
            )
            found[e] = jnp.where(chosen, lane_gather(rows, low), found[e])
    pair = (lax.broadcasted_iota(jnp.int32, wanted.shape, 0) & 3) * 2

    def four_times(rows):
        return jnp.concatenate([rows, rows], axis=0).astype(BF16)

    even = [four_times(row_gather(found[e], pair)) for e in range(3)]
    odd = [four_times(row_gather(found[e], pair + 1)) for e in range(3)]

    def apply_tile(tile, values):
        here = pl.ds(pl.multiple_of(tile * LANES, LANES), LANES)
        totals = []
        for c in range(3):
            total = jnp.zeros((PACK, LANES), F32)
            for h in range(2):
                for e in range(3):
                    block = bonds[c, e, h * PACK : (h + 1) * PACK, here].astype(F32)
                    total = total + block * values[h][e].astype(F32)
            totals.append(total[:8] + total[8:])
        return totals

    for piece, part in enumerate(local_found):
        first = piece * (groups // pieces)

        def some_tiles(t, carry, part=part, first=first):
            for u in range(unroll):
                there = pl.ds(pl.multiple_of((t * unroll + u) * LANES, LANES), LANES)
                tile = first + t * unroll + u
                here = pl.ds(pl.multiple_of(tile * LANES, LANES), LANES)
                chosen = halves_of(picks, here)
                spots, ranks = halves_of(spot, here), halves_of(rank, here)
                values = [
                    [part[e, h * PACK : (h + 1) * PACK, there] for e in range(3)]
                    for h in range(2)
                ]
                for v in range(HALO_LAYERS):
                    row = layer(halo_start[:, here] + jnp.int16(4 * v), chosen, even, odd)
                    put_back(row, jnp.int16(32 + v), spots, ranks, values)
                totals = apply_tile(tile, values)
                for c in range(3):
                    partial[c, pl.ds(pl.multiple_of(tile * 8, 8), 8), :] = totals[c]
            return carry

        lax.fori_loop(0, groups // pieces // unroll, some_tiles, 0)

    last_layer = most[groups + 8, 0]

    @pl.when(last_layer >= HALO_LAYERS)
    def _():
        def one_tile(tile, carry):
            here = pl.ds(pl.multiple_of(tile * LANES, LANES), LANES)

            def more(v, flat):
                values = [list(flat[:3]), list(flat[3:])]
                row = layer(halo_start[:, here] + splat(4 * v), halves_of(picks, here), even, odd)
                put_back(row, splat(32 + v), halves_of(spot, here), halves_of(rank, here), values)
                return tuple(values[0] + values[1])

            empty = (jnp.zeros((PACK, LANES), BF16),) * 6
            flat = lax.fori_loop(HALO_LAYERS, last_layer + 1, more, empty)
            totals = apply_tile(tile, [flat[:3], flat[3:]])
            for c in range(3):
                rows = pl.ds(pl.multiple_of(tile * 8, 8), 8)
                partial[c, rows, :] = partial[c, rows, :] + totals[c]
            return carry

        lax.fori_loop(0, groups, one_tile, 0)

    remainder = []
    for e in range(3):
        total = partial[e, pl.ds(0, groups, stride=8), :]
        for row in range(1, 8):
            total = total + partial[e, pl.ds(row, groups, stride=8), :]
        remainder.append(residual[e] - smooth[e] - total)
    solved = dense_solve(dinv, remainder)
    for c in range(3):
        change = scale_old * update[c] + scale_new * solved[c]
        total = smooth[c] + change
        new_smooth[c] = total
        if stage < SWEEPS - 1:
            new_update[c] = change
            out_outer[c] = total.astype(BF16)
            out_inner[c] = total.astype(BF16)


def coarse_kernel(*refs, subs):
    (place, base, own_couple) = refs[:3]
    first, second, third = refs[3:5], refs[5:7], refs[7:9]
    far_after, far_before, aggregate, smooth = refs[9:13]
    out, field, links, kept = refs[13:]
    groups = base.shape[1]
    me = jnp.concatenate([place[...]] * (groups // 8), axis=0)
    even = (me & 1) == 0

    def valid(row):
        if row < 0:
            return jnp.where(me + row >= 0, 1.0, 0.0)
        return jnp.where(me + row < subs, 1.0, 0.0)

    def from_after(pair, start):
        return lambda i: jnp.where(
            even, pair[0][start + i].astype(F32), pair[1][start + i].astype(F32)
        )

    def from_before(pair, start):
        return from_after((pair[1], pair[0]), start)

    def plain(ref, start):
        return lambda i: ref[start + i].astype(F32)

    def either(ref, when_even, when_odd):
        return lambda i: jnp.where(
            even, ref[when_even + i].astype(F32), ref[when_odd + i].astype(F32)
        )

    base_rows = {
        -5: either(far_after, 0, 6),
        -4: plain(far_after, 3),
        -3: either(far_after, 6, 0),
        -2: from_after(third, 3),
        -1: from_after(second, 3),
        1: from_before(second, 3),
        2: from_before(third, 3),
        3: either(far_before, 0, 6),
        4: plain(far_before, 3),
        5: either(far_before, 6, 0),
    }
    link_rows = {
        -4: plain(far_after, 9),
        -3: either(far_after, 17, 13),
        -2: from_after(second, 6),
        -1: from_after(first, 3),
        1: from_before(first, 3),
        2: from_before(second, 6),
        3: either(far_before, 13, 17),
        4: plain(far_before, 9),
    }

    def base_of(row, c):
        if row == 0:
            return base[c]
        return base_rows[row](c) * valid(row)

    for k in range(4):
        for g in range(groups):
            links[STEPS - 1, k, g : g + 1, :] = own_couple[
                k : k + 1, g * LANES : (g + 1) * LANES
            ]
    for row, read in link_rows.items():
        for k in range(4):
            links[row + STEPS - 1, k] = read(k) * valid(row)
    lane = lax.broadcasted_iota(jnp.int32, (groups, LANES), 1)
    line = lax.broadcasted_iota(jnp.int32, (groups, LANES), 0)
    inner_first = jnp.logical_or(lane > 0, line > 0)
    inner_last = jnp.logical_or(lane < LANES - 1, line < groups - 1)
    for row in range(2 * STEPS - 1):
        links[row, 2] = jnp.where(inner_first, links[row, 2], 0.0)
        links[row, 3] = jnp.where(inner_last, links[row, 3], 0.0)
    for row in range(-STEPS, STEPS + 1):
        for c in range(3):
            value = base_of(row, c)
            kept[row + STEPS, c] = value
            field[0, row + STEPS, c] = value
    for step in range(STEPS):
        old, new = step % 2, (step + 1) % 2
        reach = STEPS - 1 - step
        for row in range(-reach, reach + 1):
            spot = row + STEPS
            weights = [links[row + STEPS - 1, k] for k in range(4)]
            for c in range(3):
                x = field[old, spot, c]
                right = pltpu.roll(x, 1, 1)
                right = jnp.where(lane == 0, pltpu.roll(right, 1, 0), right)
                left = pltpu.roll(x, LANES - 1, 1)
                left = jnp.where(lane == LANES - 1, pltpu.roll(left, groups - 1, 0), left)
                field[new, spot, c] = kept[spot, c] + (
                    weights[0] * field[old, spot - 1, c]
                    + weights[1] * field[old, spot + 1, c]
                    + weights[2] * right
                    + weights[3] * left
                )
    final = STEPS % 2
    agg = aggregate[...] & (groups * LANES - 1)
    for block in range(agg.shape[0] // 8):
        index = agg[block * 8 : (block + 1) * 8]
        low = index & (LANES - 1)
        high = index >> 7
        found = [jnp.zeros((8, LANES), F32)] * 3
        for g in range(groups):
            chosen = high == g
            for c in range(3):
                rows = jnp.broadcast_to(field[final, STEPS, c, g : g + 1, :], (8, LANES))
                found[c] = jnp.where(chosen, lane_gather(rows, low), found[c])
        for c in range(3):
            result = smooth[c, block * 8 : (block + 1) * 8, :] + found[c]
            for r in range(8):
                lanes = slice((block * 8 + r) * LANES, (block * 8 + r + 1) * LANES)
                out[c : c + 1, lanes] = result[r : r + 1]


def shifted(value, steps):
    count = lax.axis_size("sub")
    return lax.ppermute(value, "sub", [(i, (i + steps) % count) for i in range(count)])


def exchanged_by_pairs(outer, inner):
    count = lax.axis_size("sub")
    across = [(i, (i + 1) % count) for i in range(1, count, 2)]
    within = [(i, i + 1) for i in range(0, count, 2)]
    outer = lax.ppermute(outer, "sub", across + [(j, i) for i, j in across])
    inner = lax.ppermute(inner, "sub", within + [(j, i) for i, j in within])
    return outer, inner


def body(
    fine_residual, bonds, bond_col, ghost_points, fine_dinv, aggregate, coarse_dinv, coarse_couple
):
    points = fine_residual.shape[1]
    groups = points // LANES
    bonds_of = bond_col.shape[0]
    per_group = coarse_dinv.shape[2]
    coarse_groups = per_group // LANES
    assert per_group & (per_group - 1) == 0
    sub = lax.axis_index("sub")
    doms = lax.axis_size("dom")
    ghost = ghost_points.reshape(-1, LANES)
    agg = aggregate.reshape(groups, LANES)
    relaid = bonds.transpose(1, 2, 0, 3)
    sds = jax.ShapeDtypeStruct
    field = sds((3, groups, LANES), F32)
    coarse_field = sds((3, coarse_groups, LANES), F32)

    def message(rows):
        return sds((rows, groups, LANES), BF16)

    residual, rhs = call(
        restrict_kernel,
        (field, coarse_field),
        tuple(pltpu.with_memory_space_constraint(x, pltpu.HBM) for x in (fine_residual, agg)),
        scratch=[
            VMEM(fine_residual.shape, F32),
            VMEM(agg.shape, jnp.int32),
            pltpu.SemaphoreType.DMA((2,)),
        ],
        us=1.6,
        spaces={0: pltpu.HBM, 1: pltpu.HBM},
    )
    dinv, smooth, packed = call(
        first_kernel,
        (sds((3, 3, groups, LANES), F32), field, message(7)),
        (residual, fine_dinv, coarse_couple),
        us=0.8,
    )
    update = smooth
    own_packed = packed
    place = jnp.full((8, LANES), sub, jnp.int32)
    def exchanged(value, step):
        return lax.ppermute(value, "dom", [(i, i ^ step) for i in range(doms)])

    assert doms == 8
    arrived = exchanged(rhs, 1)
    columns, rhs = lax.optimization_barrier((bond_col, rhs))

    def shorts(rows):
        return sds((rows, points), jnp.int16)

    picks, start, halo_start, spot, rank, most = call(
        prepare_kernel,
        (
            shorts(bonds_of),
            shorts(PACK),
            shorts(PACK),
            shorts(bonds_of),
            shorts(bonds_of),
            sds((groups + 16, LANES), jnp.int32),
        ),
        (columns,),
        scratch=[VMEM((8 * (bonds_of + 2), LANES), jnp.int32)],
        us=2.5,
    )
    start, rhs = lax.optimization_barrier((start, rhs))
    rhs = rhs + arrived
    packed, rhs = lax.optimization_barrier((packed, rhs))
    arrived = exchanged(rhs, 2)
    first = arrived_sides = exchanged_by_pairs(packed, packed)
    rhs = rhs + arrived
    arrived = exchanged(rhs, 6)
    start, rhs = lax.optimization_barrier((start, rhs))

    factor = HALF / CENTER
    for stage in range(SWEEPS):
        factor_new = 1.0 / (2.0 * CENTER / HALF - factor)
        pieces = 2 if stage == SWEEPS - 1 else 1
        tiles = groups // pieces
        found = []
        for piece in range(pieces):
            found.append(
                call(
                    functools.partial(local_kernel, first=piece * tiles, tiles=tiles),
                    sds((3, bonds_of, tiles * LANES), BF16),
                    (smooth, picks, start, spot, rank, most),
                    us=3.7 if pieces == 1 else 0.2,
                )
            )
            if stage == SWEEPS - 1 and piece == 0:
                far, start, found[0] = lax.optimization_barrier((far, start, found[0]))
                far_after = shifted(far, 4)
                far_before = shifted(far, -4)
        inputs = [place, most, picks, halo_start, spot, rank, ghost, *arrived_sides]
        inputs += [residual, dinv, smooth, update, relaid, *found]
        if stage == 0:
            inputs += [rhs, arrived, coarse_dinv]
            outs = (field, field, coarse_field, message(10), message(10))
        elif stage == 1:
            inputs += [*first, base, own_packed]
            outs = (field, field, message(6), message(6), message(21))
        else:
            outs = (field,)
        result = call(
            functools.partial(
                halo_kernel,
                stage=stage,
                scale_old=factor_new * factor,
                scale_new=2.0 * factor_new / HALF,
            ),
            outs,
            inputs,
            scratch=[VMEM((3, groups, LANES), F32)] * 2 + [VMEM((3, 8 * groups, LANES), F32)],
            us=2.5,
        )
        factor = factor_new
        if stage == 0:
            smooth, update, base, outer, inner = result
            second = arrived_sides = exchanged_by_pairs(outer, inner)
        elif stage == 1:
            smooth, update, outer, inner, far = result
            third = arrived_sides = exchanged_by_pairs(outer, inner)
        else:
            (smooth,) = result
    return call(
        functools.partial(coarse_kernel, subs=lax.axis_size("sub")),
        sds((3, points), F32),
        (
            place,
            base,
            coarse_couple,
            *first,
            *second,
            *third,
            far_after,
            far_before,
            agg,
            smooth,
        ),
        scratch=[
            VMEM((2, 2 * STEPS + 1, 3, coarse_groups, LANES), F32),
            VMEM((2 * STEPS - 1, 4, coarse_groups, LANES), F32),
            VMEM((2 * STEPS + 1, 3, coarse_groups, LANES), F32),
        ],
        us=2.0,
    )


def solution(mesh):
    placed = (
        P(None, ("dom", "sub")),
        P(None, None, None, ("dom", "sub")),
        P(None, ("dom", "sub")),
        P(("dom", "sub"), None, None),
        P(None, None, ("dom", "sub")),
        P(("dom", "sub")),
        P(None, None, "sub"),
        P(None, "sub"),
    )
    return jax.shard_map(
        body, mesh=mesh, in_specs=placed, out_specs=P(None, ("dom", "sub")), check_vma=False
    )
```

```python
import functools

import jax
import jax.numpy as jnp
from jax import lax
from jax.experimental import pallas as pl
from jax.experimental.pallas import tpu as pltpu
from jax.sharding import PartitionSpec as P

SWEEPS = 3
STEPS = 5
FAR = 4
LOW_EIG = 0.3
HIGH_EIG = 2.2
CENTER = (HIGH_EIG + LOW_EIG) / 2.0
HALF = (HIGH_EIG - LOW_EIG) / 2.0
LANES = 128
PACK = 16
F32 = jnp.float32
BF16 = jnp.bfloat16
VMEM = pltpu.VMEM


def gather(rows, index, axis):
    numbers = lax.GatherDimensionNumbers(
        offset_dims=(),
        collapsed_slice_dims=(axis,),
        start_index_map=(axis,),
        operand_batching_dims=(1 - axis,),
        start_indices_batching_dims=(1 - axis,),
    )
    return lax.gather(
        rows,
        index[..., None],
        numbers,
        (1, 1),
        mode=lax.GatherScatterMode.PROMISE_IN_BOUNDS,
    )


def lane_gather(rows, index):
    return gather(rows, index, 1)


def row_gather(rows, index):
    return gather(rows, index, 0)


def sorting_network(count):
    pairs = []
    span = 1
    while span < count:
        gap = span
        while gap >= 1:
            for j in range(gap % span, count - gap, 2 * gap):
                for i in range(min(gap, count - j - gap)):
                    if (i + j) // (2 * span) == (i + j + gap) // (2 * span):
                        pairs.append((i + j, i + j + gap))
            gap //= 2
        span *= 2
    return pairs


def sort_planes(planes):
    planes = list(planes)
    for i, j in sorting_network(len(planes)):
        planes[i], planes[j] = (
            jnp.minimum(planes[i], planes[j]),
            jnp.maximum(planes[i], planes[j]),
        )
    return planes


def call(kernel, out, inputs, scratch=(), us=1.0, spaces={}, limit=16):
    return pl.pallas_call(
        kernel,
        out_shape=out,
        in_specs=[
            pl.BlockSpec(memory_space=spaces.get(i, VMEM)) for i in range(len(inputs))
        ],
        out_specs=jax.tree.map(
            lambda _: pl.BlockSpec(memory_space=VMEM), out
        ),
        scratch_shapes=list(scratch),
        cost_estimate=pl.CostEstimate(
            flops=int(us * 1.0e9), transcendentals=0, bytes_accessed=int(us * 1.0e6)
        ),
        compiler_params=pltpu.CompilerParams(vmem_limit_bytes=limit * 1024 * 1024),
    )(*inputs)


def rows_of(ref, lead, group):
    return ref[lead + (slice(group * LANES, (group + 1) * LANES),)]


def restrict_kernel(*refs):
    sources = refs[:2]
    dense_residual, rhs = refs[2:4]
    residual, aggregate, semaphores = refs[4:]
    copies = [
        pltpu.make_async_copy(source, target, semaphores.at[i])
        for i, (source, target) in enumerate(zip(sources, (residual, aggregate)))
    ]
    for copy in copies:
        copy.start()
    copies[0].wait()
    for g in range(dense_residual.shape[1]):
        for e in range(3):
            dense_residual[e, g : g + 1, :] = residual[
                e : e + 1, g * LANES : (g + 1) * LANES
            ]
    copies[1].wait()
    restrict(dense_residual, aggregate, rhs)


def first_kernel(dense_residual, dinv, couple, dense_dinv, smooth, message):
    groups = smooth.shape[1]
    coarse_groups = message.shape[1]
    for g in range(groups):
        lanes = slice(g * LANES, (g + 1) * LANES)
        for e in range(3):
            for c in range(3):
                dense_dinv[c, e, g : g + 1, :] = dinv[c, e : e + 1, lanes]
    for g in range(coarse_groups):
        lanes = slice(g * LANES, (g + 1) * LANES)
        for k in range(4):
            message[3 + k, g : g + 1, :] = couple[k : k + 1, lanes].astype(BF16)
    for c in range(3):
        total = dense_dinv[c, 0] * dense_residual[0]
        for e in range(1, 3):
            total = total + dense_dinv[c, e] * dense_residual[e]
        total = total * (1.0 / CENTER)
        smooth[c] = total
        message[c] = total.astype(BF16)


def restrict(residual, aggregate, out):
    groups = residual.shape[1]
    bins = out.shape[1]
    agg = aggregate[...] & (bins * LANES - 1)
    low = agg & (LANES - 1)
    high = agg >> 7
    batch = 8
    row16 = lax.broadcasted_iota(jnp.int32, (PACK, LANES), 0).astype(jnp.int16)
    one, zero = jnp.ones((PACK, LANES), BF16), jnp.zeros((PACK, LANES), BF16)

    def wide(row, kind):
        return jnp.broadcast_to(row, (PACK, LANES)).astype(kind)

    total = jnp.zeros((6 * bins, LANES), F32)
    for block in range(groups // batch):
        onehot, spread = [], []
        for g in range(block * batch, (block + 1) * batch):
            lane = wide(low[g : g + 1], jnp.int16)
            line = wide(high[g : g + 1], jnp.int16)
            onehot.append(
                jnp.concatenate(
                    [
                        jnp.where(lane == row16 + jnp.int16(first), one, zero)
                        for first in range(0, LANES, PACK)
                    ],
                    axis=0,
                )
            )
            chosen = [line == row16 + jnp.int16(first) for first in range(0, bins, PACK)]
            column = []
            for c in range(3):
                value = residual[c, g : g + 1, :]
                upper = value.astype(BF16).astype(F32)
                for part in (upper, value - upper):
                    part = wide(part, BF16)
                    column += [jnp.where(mask, part, zero) for mask in chosen]
            spread.append(jnp.concatenate(column, axis=0))
        total = total + lax.dot_general(
            jnp.concatenate(spread, axis=1),
            jnp.concatenate(onehot, axis=1),
            (((1,), (1,)), ((), ())),
            preferred_element_type=F32,
        )
    for c in range(3):
        first = 2 * c * bins
        out[c] = total[first : first + bins] + total[first + bins : first + 2 * bins]


def spread_max(values):
    top = jnp.max(jnp.max(values, axis=1, keepdims=True), axis=0, keepdims=True)
    return jnp.broadcast_to(top, values.shape)


def prepare_kernel(col, picks, start, halo_start, spot, rank, most, flip):
    bonds_of = col.shape[0]
    groups = col.shape[1] // LANES
    stride = bonds_of + 1

    def eight_tiles(block, carry):
        best, halo_best = carry

        def lanes_of(t):
            return pl.ds(pl.multiple_of((block * 8 + t) * LANES, LANES), LANES)

        for t in range(8):
            flip[pl.ds(t * stride, bonds_of), :] = col[:, lanes_of(t)]
        keys = []
        for k in range(bonds_of):
            c = flip[pl.ds(k, 8, stride=stride), :]
            keys.append(((c >> 8) << 13) | (k << 8) | (c & 255))
        keys = sort_planes(keys)
        pairs = [key >> 13 for key in keys]
        ranks = [jnp.zeros((8, LANES), jnp.int32)]
        for k in range(1, bonds_of):
            ranks.append(jnp.where(pairs[k] == pairs[k - 1], ranks[k - 1] + 1, 0))
        back = []
        here = jnp.zeros((8, LANES), jnp.int32)
        for k in range(bonds_of):
            local = pairs[k] < PACK
            here = jnp.maximum(here, jnp.where(local, ranks[k], 0))
            halo_best = jnp.maximum(halo_best, jnp.where(local, 0, ranks[k]))
            code = jnp.where(
                local,
                (ranks[k] << 4) | pairs[k],
                ((ranks[k] >> 2) << 4) | ((ranks[k] & 3) << 2) | ((pairs[k] - PACK) + (32 << 4)),
            )
            back.append((((keys[k] >> 8) & 31) << 10) | code)
            flip[pl.ds(k, 8, stride=stride), :] = keys[k]
        row = lax.broadcasted_iota(jnp.int32, (PACK, LANES), 0)
        for t in range(8):
            halves = [flip[pl.ds(t * stride + h * PACK, PACK), :] for h in range(2)]
            for h in range(2):
                picks[h * PACK : (h + 1) * PACK, lanes_of(t)] = (halves[h] & 255).astype(jnp.int16)
            first, second = [(x >> 13).astype(jnp.int16) for x in halves]
            for target, pair, extra in (
                (start, row.astype(jnp.int16), None),
                (halo_start, (PACK + (row & 3)).astype(jnp.int16), (row >> 2).astype(jnp.int16)),
            ):
                place = jnp.zeros((PACK, LANES), jnp.int16)
                for step in (16, 8, 4, 2, 1, 1):
                    probe = place + jnp.int16(step - 1)
                    inner = probe & jnp.int16(PACK - 1)
                    value = jnp.where(
                        probe < PACK, row_gather(first, inner), row_gather(second, inner)
                    )
                    place = jnp.where(value < pair, place + jnp.int16(step), place)
                target[:, lanes_of(t)] = place if extra is None else place + extra
        back = sort_planes(back)
        for k in range(bonds_of):
            flip[pl.ds(k, 8, stride=stride), :] = back[k] & 1023
        for t in range(8):
            for h in range(2):
                code = flip[pl.ds(t * stride + h * PACK, PACK), :]
                rows = slice(h * PACK, (h + 1) * PACK)
                spot[rows, lanes_of(t)] = (code & 15).astype(jnp.int16)
                rank[rows, lanes_of(t)] = (code >> 4).astype(jnp.int16)
        most[pl.ds(pl.multiple_of(block * 8, 8), 8), :] = spread_max(here)
        return jnp.maximum(best, here), halo_best

    zero = jnp.zeros((8, LANES), jnp.int32)
    best, halo_best = lax.fori_loop(0, groups // 8, eight_tiles, (zero, zero))
    most[groups : groups + 8, :] = spread_max(best)
    most[groups + 8 :, :] = spread_max(halo_best) >> 2


def layer(place, picks, even, odd):
    inner = place & jnp.int16(PACK - 1)
    pick = jnp.where(
        place < PACK, row_gather(picks[0], inner), row_gather(picks[1], inner)
    )
    lane = pick & jnp.int16(LANES - 1)
    second = pick >= LANES
    return [
        jnp.where(second, lane_gather(odd[e], lane), lane_gather(even[e], lane))
        for e in range(3)
    ]


def put_back(values, number, spots, ranks, out):
    for h in range(2):
        hit = ranks[h] == number
        for e in range(3):
            out[h][e] = jnp.where(hit, row_gather(values[e], spots[h]), out[h][e])


def halves_of(ref, lanes):
    return [ref[h * PACK : (h + 1) * PACK, lanes] for h in range(2)]


def splat(number):
    return jnp.full((PACK, LANES), number, jnp.int32).astype(jnp.int16)


LAYERS = 10
HALO_LAYERS = 3


def local_kernel(smooth, picks, start, spot, rank, most, out, *, first, tiles, unroll=8):
    even = [smooth[e, pl.ds(0, PACK, stride=2), :].astype(BF16) for e in range(3)]
    odd = [smooth[e, pl.ds(1, PACK, stride=2), :].astype(BF16) for e in range(3)]

    def some_tiles(t, carry):
        for u in range(unroll):
            source = pl.ds(pl.multiple_of((first + t * unroll + u) * LANES, LANES), LANES)
            target = pl.ds(pl.multiple_of((t * unroll + u) * LANES, LANES), LANES)
            place = start[:, source]
            chosen = halves_of(picks, source)
            spots, ranks = halves_of(spot, source), halves_of(rank, source)
            found = [[jnp.zeros((PACK, LANES), BF16)] * 3 for h in range(2)]
            for m in range(LAYERS):
                values = layer(place + jnp.int16(m), chosen, even, odd)
                put_back(values, jnp.int16(m), spots, ranks, found)
            for h in range(2):
                for e in range(3):
                    out[e, h * PACK : (h + 1) * PACK, target] = found[h][e]
        return carry

    lax.fori_loop(0, tiles // unroll, some_tiles, 0)

    @pl.when(most[smooth.shape[1], 0] >= LAYERS)
    def _():
        def eight_tiles(block, carry):
            def more(m, inner):
                number = splat(m)
                for t in range(8):
                    tile = block * 8 + t
                    source = pl.ds(pl.multiple_of((first + tile) * LANES, LANES), LANES)
                    target = pl.ds(pl.multiple_of(tile * LANES, LANES), LANES)
                    found = [
                        [out[e, h * PACK : (h + 1) * PACK, target] for e in range(3)]
                        for h in range(2)
                    ]
                    values = layer(
                        start[:, source] + number, halves_of(picks, source), even, odd
                    )
                    put_back(
                        values, number, halves_of(spot, source), halves_of(rank, source), found
                    )
                    for h in range(2):
                        for e in range(3):
                            out[e, h * PACK : (h + 1) * PACK, target] = found[h][e]
                return inner

            lax.fori_loop(LAYERS, most[first + block * 8, 0] + 1, more, 0)
            return carry

        lax.fori_loop(0, tiles // 8, eight_tiles, 0)


def dense_solve(matrix, vector):
    solved = []
    for c in range(3):
        total = matrix[c, 0] * vector[0]
        for e in range(1, 3):
            total = total + matrix[c, e] * vector[e]
        solved.append(total)
    return solved


def sideways(x):
    lines = x.shape[0]
    lane = lax.broadcasted_iota(jnp.int32, x.shape, 1)
    right = pltpu.roll(x, 1, 1)
    right = jnp.where(lane == 0, pltpu.roll(right, 1, 0), right)
    left = pltpu.roll(x, LANES - 1, 1)
    left = jnp.where(lane == LANES - 1, pltpu.roll(left, lines - 1, 0), left)
    return right, left


def inside_masks(shape):
    lane = lax.broadcasted_iota(jnp.int32, shape, 1)
    line = lax.broadcasted_iota(jnp.int32, shape, 0)
    return (
        jnp.logical_or(lane > 0, line > 0),
        jnp.logical_or(lane < LANES - 1, line < shape[0] - 1),
    )


def halo_kernel(*refs, stage, scale_old, scale_new, subs, unroll=8):
    (place, most, picks, halo_start, spot, rank, ghost, outer, inner) = refs[:9]
    (residual, dinv, smooth, update, bonds) = refs[9:14]
    pieces = 2 if stage == SWEEPS - 1 else 1
    local_found = refs[14 : 14 + pieces]
    refs = refs[14 + pieces :]
    if stage == 0:
        rhs, arrived, coarse_dinv = refs[:3]
        new_smooth, new_update, base, out_outer, out_inner = refs[3:8]
        refs = refs[8:]
    elif stage == 1:
        first_outer, first_inner, base, couple_own = refs[:4]
        new_smooth, new_update, out_outer, out_inner, far_next, far_prev = refs[4:10]
        refs = refs[10:]
    else:
        (new_smooth,) = refs[:1]
        refs = refs[1:]
    applied, other, partial = refs
    groups = smooth.shape[1]
    if stage == 0:
        vector = [rhs[e] + arrived[e] for e in range(3)]
        coarse_groups = base.shape[1]
        for c in range(3):
            for g in range(coarse_groups):
                lanes = slice(g * LANES, (g + 1) * LANES)
                total = coarse_dinv[c, 0:1, lanes] * vector[0][g : g + 1]
                for e in range(1, 3):
                    total = total + coarse_dinv[c, e : e + 1, lanes] * vector[e][g : g + 1]
                base[c, g : g + 1, :] = total
        for c in range(3):
            row = base[c].astype(BF16)
            out_outer[3 + c] = row
            out_inner[3 + c] = row
        out_outer[6:10] = inner[3:7]
        out_inner[6:10] = outer[3:7]
    elif stage == 1:
        out_outer[3:6] = inner[3:6]
        out_inner[3:6] = outer[3:6]
        me = jnp.concatenate([place[...]] * (base.shape[1] // 8), axis=0)
        even = (me & 1) == 0
        links = [couple_own[3 + k].astype(F32) for k in range(4)]
        links[0] = jnp.where(me > 0, links[0], 0.0)
        links[1] = jnp.where(me < subs - 1, links[1], 0.0)
        for k, mask in zip((2, 3), inside_masks(me.shape)):
            links[k] = jnp.where(mask, links[k], 0.0)
        for c in range(3):
            own = base[c]
            outer_row, inner_row = outer[3 + c].astype(F32), inner[3 + c].astype(F32)
            below = jnp.where(even, outer_row, inner_row)
            above = jnp.where(even, inner_row, outer_row)
            right, left = sideways(own)
            iterate = own + (
                links[0] * below + links[1] * above + links[2] * right + links[3] * left
            )
            for message, beyond in ((far_next, above), (far_prev, below)):
                message[c] = own.astype(BF16)
                message[3 + c] = iterate.astype(BF16)
                message[6 + c] = beyond.astype(BF16)
        for k in range(4):
            outer_row = first_outer[3 + k].astype(F32)
            inner_row = first_inner[3 + k].astype(F32)
            far_next[9 + k] = jnp.where(even, inner_row, outer_row).astype(BF16)
            far_prev[9 + k] = jnp.where(even, outer_row, inner_row).astype(BF16)
    wanted = ghost[...]
    half = wanted.shape[0] // 2
    low = wanted & (LANES - 1)
    high = wanted >> 7
    upper = jnp.where(lax.broadcasted_iota(jnp.int32, wanted.shape, 0) < half, 1, 0)
    from_outer = (upper ^ (place[...] & 1)) == 1
    found = [jnp.zeros(wanted.shape, F32)] * 3
    for e in range(3):
        applied[e] = outer[e].astype(F32)
        other[e] = inner[e].astype(F32)
    for g in range(groups):
        chosen = high == g
        for e in range(3):
            rows = jnp.where(
                from_outer,
                jnp.broadcast_to(applied[e, g : g + 1, :], wanted.shape),
                jnp.broadcast_to(other[e, g : g + 1, :], wanted.shape),
            )
            found[e] = jnp.where(chosen, lane_gather(rows, low), found[e])
    pair = (lax.broadcasted_iota(jnp.int32, wanted.shape, 0) & 3) * 2

    def four_times(rows):
        return jnp.concatenate([rows, rows], axis=0).astype(BF16)

    even = [four_times(row_gather(found[e], pair)) for e in range(3)]
    odd = [four_times(row_gather(found[e], pair + 1)) for e in range(3)]

    def apply_tile(tile, values):
        here = pl.ds(pl.multiple_of(tile * LANES, LANES), LANES)
        totals = []
        for c in range(3):
            total = jnp.zeros((PACK, LANES), F32)
            for h in range(2):
                for e in range(3):
                    block = bonds[c, e, h * PACK : (h + 1) * PACK, here].astype(F32)
                    total = total + block * values[h][e].astype(F32)
            totals.append(total[:8] + total[8:])
        return totals

    for piece, part in enumerate(local_found):
        first = piece * (groups // pieces)

        def some_tiles(t, carry, part=part, first=first):
            for u in range(unroll):
                there = pl.ds(pl.multiple_of((t * unroll + u) * LANES, LANES), LANES)
                tile = first + t * unroll + u
                here = pl.ds(pl.multiple_of(tile * LANES, LANES), LANES)
                chosen = halves_of(picks, here)
                spots, ranks = halves_of(spot, here), halves_of(rank, here)
                values = [
                    [part[e, h * PACK : (h + 1) * PACK, there] for e in range(3)]
                    for h in range(2)
                ]
                for v in range(HALO_LAYERS):
                    row = layer(halo_start[:, here] + jnp.int16(4 * v), chosen, even, odd)
                    put_back(row, jnp.int16(32 + v), spots, ranks, values)
                totals = apply_tile(tile, values)
                for c in range(3):
                    partial[c, pl.ds(pl.multiple_of(tile * 8, 8), 8), :] = totals[c]
            return carry

        lax.fori_loop(0, groups // pieces // unroll, some_tiles, 0)

    last_layer = most[groups + 8, 0]

    @pl.when(last_layer >= HALO_LAYERS)
    def _():
        def one_tile(tile, carry):
            here = pl.ds(pl.multiple_of(tile * LANES, LANES), LANES)

            def more(v, flat):
                values = [list(flat[:3]), list(flat[3:])]
                row = layer(halo_start[:, here] + splat(4 * v), halves_of(picks, here), even, odd)
                put_back(row, splat(32 + v), halves_of(spot, here), halves_of(rank, here), values)
                return tuple(values[0] + values[1])

            empty = (jnp.zeros((PACK, LANES), BF16),) * 6
            flat = lax.fori_loop(HALO_LAYERS, last_layer + 1, more, empty)
            totals = apply_tile(tile, [flat[:3], flat[3:]])
            for c in range(3):
                rows = pl.ds(pl.multiple_of(tile * 8, 8), 8)
                partial[c, rows, :] = partial[c, rows, :] + totals[c]
            return carry

        lax.fori_loop(0, groups, one_tile, 0)

    remainder = []
    for e in range(3):
        total = partial[e, pl.ds(0, groups, stride=8), :]
        for row in range(1, 8):
            total = total + partial[e, pl.ds(row, groups, stride=8), :]
        remainder.append(residual[e] - smooth[e] - total)
    solved = dense_solve(dinv, remainder)
    for c in range(3):
        change = scale_old * update[c] + scale_new * solved[c]
        total = smooth[c] + change
        new_smooth[c] = total
        if stage < SWEEPS - 1:
            new_update[c] = change
            out_outer[c] = total.astype(BF16)
            out_inner[c] = total.astype(BF16)


def coarse_kernel(*refs, subs):
    (place, base, own_couple) = refs[:3]
    first, second, third = refs[3:5], refs[5:7], refs[7:9]
    far_after, far_before, aggregate, smooth = refs[9:13]
    out, field, links, kept = refs[13:]
    groups = base.shape[1]
    me = jnp.concatenate([place[...]] * (groups // 8), axis=0)
    even = (me & 1) == 0

    def valid(row):
        if row < 0:
            return jnp.where(me + row >= 0, 1.0, 0.0)
        return jnp.where(me + row < subs, 1.0, 0.0)

    def from_after(pair, start):
        return lambda i: jnp.where(
            even, pair[0][start + i].astype(F32), pair[1][start + i].astype(F32)
        )

    def from_before(pair, start):
        return from_after((pair[1], pair[0]), start)

    def plain(ref, start):
        return lambda i: ref[start + i].astype(F32)

    base_rows = {
        -4: plain(far_after, 0),
        -3: plain(far_after, 6),
        -2: from_after(third, 3),
        -1: from_after(second, 3),
        1: from_before(second, 3),
        2: from_before(third, 3),
        3: plain(far_before, 6),
        4: plain(far_before, 0),
    }
    link_rows = {
        -3: plain(far_after, 9),
        -2: from_after(second, 6),
        -1: from_after(first, 3),
        1: from_before(first, 3),
        2: from_before(second, 6),
        3: plain(far_before, 9),
    }
    for g in range(groups):
        for k in range(4):
            links[FAR - 1, k, g : g + 1, :] = own_couple[
                k : k + 1, g * LANES : (g + 1) * LANES
            ]
    for row, read in link_rows.items():
        for k in range(4):
            links[row + FAR - 1, k] = read(k) * valid(row)
    for k, mask in zip((2, 3), inside_masks(me.shape)):
        for row in range(2 * FAR - 1):
            links[row, k] = jnp.where(mask, links[row, k], 0.0)
    for c in range(3):
        field[0, FAR, c] = base[c]
        for row, read in base_rows.items():
            field[0, row + FAR, c] = read(c) * valid(row)
        field[1, 0, c] = far_after[3 + c].astype(F32) * valid(-FAR)
        field[1, 2 * FAR, c] = far_before[3 + c].astype(F32) * valid(FAR)
        for row in range(2 * FAR + 1):
            kept[row, c] = field[0, row, c]
    for step in range(STEPS):
        old, new = step % 2, (step + 1) % 2
        reach = min(STEPS - 1 - step, FAR - 1)
        for row in range(-reach, reach + 1):
            spot = row + FAR
            weights = [links[spot - 1, k] for k in range(4)]
            for c in range(3):
                right, left = sideways(field[old, spot, c])
                field[new, spot, c] = kept[spot, c] + (
                    weights[0] * field[old, spot - 1, c]
                    + weights[1] * field[old, spot + 1, c]
                    + weights[2] * right
                    + weights[3] * left
                )
    final = STEPS % 2
    agg = aggregate[...] & (groups * LANES - 1)
    for block in range(agg.shape[0] // 8):
        index = agg[block * 8 : (block + 1) * 8]
        low = index & (LANES - 1)
        high = index >> 7
        found = [jnp.zeros((8, LANES), F32)] * 3
        for g in range(groups):
            chosen = high == g
            for c in range(3):
                rows = jnp.broadcast_to(field[final, FAR, c, g : g + 1, :], (8, LANES))
                found[c] = jnp.where(chosen, lane_gather(rows, low), found[c])
        for c in range(3):
            result = smooth[c, block * 8 : (block + 1) * 8, :] + found[c]
            for r in range(8):
                lanes = slice((block * 8 + r) * LANES, (block * 8 + r + 1) * LANES)
                out[c : c + 1, lanes] = result[r : r + 1]


def shifted(value, steps):
    count = lax.axis_size("sub")
    return lax.ppermute(value, "sub", [(i, (i + steps) % count) for i in range(count)])


def exchanged_by_pairs(outer, inner):
    count = lax.axis_size("sub")
    across = [(i, (i + 1) % count) for i in range(1, count, 2)]
    within = [(i, i + 1) for i in range(0, count, 2)]
    outer = lax.ppermute(outer, "sub", across + [(j, i) for i, j in across])
    inner = lax.ppermute(inner, "sub", within + [(j, i) for i, j in within])
    return outer, inner


def body(
    fine_residual, bonds, bond_col, ghost_points, fine_dinv, aggregate, coarse_dinv, coarse_couple
):
    points = fine_residual.shape[1]
    groups = points // LANES
    bonds_of = bond_col.shape[0]
    per_group = coarse_dinv.shape[2]
    coarse_groups = per_group // LANES
    assert per_group & (per_group - 1) == 0
    sub = lax.axis_index("sub")
    doms = lax.axis_size("dom")
    ghost = ghost_points.reshape(-1, LANES)
    agg = aggregate.reshape(groups, LANES)
    relaid = bonds.transpose(1, 2, 0, 3)
    sds = jax.ShapeDtypeStruct
    field = sds((3, groups, LANES), F32)
    coarse_field = sds((3, coarse_groups, LANES), F32)

    def message(rows):
        return sds((rows, groups, LANES), BF16)

    residual, rhs = call(
        restrict_kernel,
        (field, coarse_field),
        tuple(pltpu.with_memory_space_constraint(x, pltpu.HBM) for x in (fine_residual, agg)),
        scratch=[
            VMEM(fine_residual.shape, F32),
            VMEM(agg.shape, jnp.int32),
            pltpu.SemaphoreType.DMA((2,)),
        ],
        us=1.6,
        spaces={0: pltpu.HBM, 1: pltpu.HBM},
    )
    dinv, smooth, packed = call(
        first_kernel,
        (sds((3, 3, groups, LANES), F32), field, message(7)),
        (residual, fine_dinv, coarse_couple),
        us=0.8,
    )
    update = smooth
    own_packed = packed
    place = jnp.full((8, LANES), sub, jnp.int32)
    def exchanged(value, step):
        return lax.ppermute(value, "dom", [(i, i ^ step) for i in range(doms)])

    assert doms == 8
    arrived = exchanged(rhs, 1)
    columns, rhs = lax.optimization_barrier((bond_col, rhs))

    def shorts(rows):
        return sds((rows, points), jnp.int16)

    picks, start, halo_start, spot, rank, most = call(
        prepare_kernel,
        (
            shorts(bonds_of),
            shorts(PACK),
            shorts(PACK),
            shorts(bonds_of),
            shorts(bonds_of),
            sds((groups + 16, LANES), jnp.int32),
        ),
        (columns,),
        scratch=[VMEM((8 * (bonds_of + 2), LANES), jnp.int32)],
        us=2.5,
    )
    start, rhs = lax.optimization_barrier((start, rhs))
    rhs = rhs + arrived
    packed, rhs = lax.optimization_barrier((packed, rhs))
    arrived = exchanged(rhs, 2)
    first = arrived_sides = exchanged_by_pairs(packed, packed)
    rhs = rhs + arrived
    arrived = exchanged(rhs, 6)
    start, rhs = lax.optimization_barrier((start, rhs))

    factor = HALF / CENTER
    for stage in range(SWEEPS):
        factor_new = 1.0 / (2.0 * CENTER / HALF - factor)
        pieces = 2 if stage == SWEEPS - 1 else 1
        tiles = groups // pieces
        found = []
        for piece in range(pieces):
            found.append(
                call(
                    functools.partial(local_kernel, first=piece * tiles, tiles=tiles),
                    sds((3, bonds_of, tiles * LANES), BF16),
                    (smooth, picks, start, spot, rank, most),
                    us=3.7 if pieces == 1 else 0.2,
                )
            )
            if stage == SWEEPS - 1 and piece == 0:
                far_next, far_prev, start, found[0] = lax.optimization_barrier(
                    (far_next, far_prev, start, found[0])
                )
                far_after = shifted(far_next, 4)
                far_before = shifted(far_prev, -4)
        inputs = [place, most, picks, halo_start, spot, rank, ghost, *arrived_sides]
        inputs += [residual, dinv, smooth, update, relaid, *found]
        if stage == 0:
            inputs += [rhs, arrived, coarse_dinv]
            outs = (field, field, coarse_field, message(10), message(10))
        elif stage == 1:
            inputs += [*first, base, own_packed]
            outs = (field, field, message(6), message(6), message(13), message(13))
        else:
            outs = (field,)
        result = call(
            functools.partial(
                halo_kernel,
                stage=stage,
                scale_old=factor_new * factor,
                scale_new=2.0 * factor_new / HALF,
                subs=lax.axis_size("sub"),
            ),
            outs,
            inputs,
            scratch=[VMEM((3, groups, LANES), F32)] * 2 + [VMEM((3, 8 * groups, LANES), F32)],
            us=2.5,
        )
        factor = factor_new
        if stage == 0:
            smooth, update, base, outer, inner = result
            second = arrived_sides = exchanged_by_pairs(outer, inner)
        elif stage == 1:
            smooth, update, outer, inner, far_next, far_prev = result
            third = arrived_sides = exchanged_by_pairs(outer, inner)
        else:
            (smooth,) = result
    return call(
        functools.partial(coarse_kernel, subs=lax.axis_size("sub")),
        sds((3, points), F32),
        (
            place,
            base,
            coarse_couple,
            *first,
            *second,
            *third,
            far_after,
            far_before,
            agg,
            smooth,
        ),
        scratch=[
            VMEM((2, 2 * FAR + 1, 3, coarse_groups, LANES), F32),
            VMEM((2 * FAR - 1, 4, coarse_groups, LANES), F32),
            VMEM((2 * FAR + 1, 3, coarse_groups, LANES), F32),
        ],
        us=2.0,
    )


def solution(mesh):
    placed = (
        P(None, ("dom", "sub")),
        P(None, None, None, ("dom", "sub")),
        P(None, ("dom", "sub")),
        P(("dom", "sub"), None, None),
        P(None, None, ("dom", "sub")),
        P(("dom", "sub")),
        P(None, None, "sub"),
        P(None, "sub"),
    )
    return jax.shard_map(
        body, mesh=mesh, in_specs=placed, out_specs=P(None, ("dom", "sub")), check_vma=False
    )
```

```python
import functools

import jax
import jax.numpy as jnp
from jax import lax
from jax.experimental import pallas as pl
from jax.experimental.pallas import tpu as pltpu
from jax.sharding import PartitionSpec as P

SWEEPS = 3
STEPS = 5
FAR = 4
LOW_EIG = 0.3
HIGH_EIG = 2.2
CENTER = (HIGH_EIG + LOW_EIG) / 2.0
HALF = (HIGH_EIG - LOW_EIG) / 2.0
LANES = 128
PACK = 16
F32 = jnp.float32
BF16 = jnp.bfloat16
VMEM = pltpu.VMEM


def gather(rows, index, axis):
    numbers = lax.GatherDimensionNumbers(
        offset_dims=(),
        collapsed_slice_dims=(axis,),
        start_index_map=(axis,),
        operand_batching_dims=(1 - axis,),
        start_indices_batching_dims=(1 - axis,),
    )
    return lax.gather(
        rows,
        index[..., None],
        numbers,
        (1, 1),
        mode=lax.GatherScatterMode.PROMISE_IN_BOUNDS,
    )


def lane_gather(rows, index):
    return gather(rows, index, 1)


def row_gather(rows, index):
    return gather(rows, index, 0)


def sorting_network(count):
    pairs = []
    span = 1
    while span < count:
        gap = span
        while gap >= 1:
            for j in range(gap % span, count - gap, 2 * gap):
                for i in range(min(gap, count - j - gap)):
                    if (i + j) // (2 * span) == (i + j + gap) // (2 * span):
                        pairs.append((i + j, i + j + gap))
            gap //= 2
        span *= 2
    return pairs


def sort_planes(planes):
    planes = list(planes)
    for i, j in sorting_network(len(planes)):
        planes[i], planes[j] = (
            jnp.minimum(planes[i], planes[j]),
            jnp.maximum(planes[i], planes[j]),
        )
    return planes


def call(kernel, out, inputs, scratch=(), us=1.0, spaces={}, limit=16):
    return pl.pallas_call(
        kernel,
        out_shape=out,
        in_specs=[
            pl.BlockSpec(memory_space=spaces.get(i, VMEM)) for i in range(len(inputs))
        ],
        out_specs=jax.tree.map(
            lambda _: pl.BlockSpec(memory_space=VMEM), out
        ),
        scratch_shapes=list(scratch),
        cost_estimate=pl.CostEstimate(
            flops=int(us * 1.0e9), transcendentals=0, bytes_accessed=int(us * 1.0e6)
        ),
        compiler_params=pltpu.CompilerParams(vmem_limit_bytes=limit * 1024 * 1024),
    )(*inputs)


def rows_of(ref, lead, group):
    return ref[lead + (slice(group * LANES, (group + 1) * LANES),)]


def restrict_kernel(*refs):
    sources = refs[:2]
    dense_residual, rhs = refs[2:4]
    residual, aggregate, semaphores = refs[4:]
    copies = [
        pltpu.make_async_copy(source, target, semaphores.at[i])
        for i, (source, target) in enumerate(zip(sources, (residual, aggregate)))
    ]
    for copy in copies:
        copy.start()
    copies[0].wait()
    for g in range(dense_residual.shape[1]):
        for e in range(3):
            dense_residual[e, g : g + 1, :] = residual[
                e : e + 1, g * LANES : (g + 1) * LANES
            ]
    copies[1].wait()
    restrict(dense_residual, aggregate, rhs)


def first_kernel(dense_residual, dinv, couple, dense_dinv, smooth, message):
    groups = smooth.shape[1]
    coarse_groups = message.shape[1]
    for g in range(groups):
        lanes = slice(g * LANES, (g + 1) * LANES)
        for e in range(3):
            for c in range(3):
                dense_dinv[c, e, g : g + 1, :] = dinv[c, e : e + 1, lanes]
    for g in range(coarse_groups):
        lanes = slice(g * LANES, (g + 1) * LANES)
        for k in range(4):
            message[3 + k, g : g + 1, :] = couple[k : k + 1, lanes].astype(BF16)
    for c in range(3):
        total = dense_dinv[c, 0] * dense_residual[0]
        for e in range(1, 3):
            total = total + dense_dinv[c, e] * dense_residual[e]
        total = total * (1.0 / CENTER)
        smooth[c] = total
        message[c] = total.astype(BF16)


def restrict(residual, aggregate, out):
    groups = residual.shape[1]
    bins = out.shape[1]
    agg = aggregate[...] & (bins * LANES - 1)
    low = agg & (LANES - 1)
    high = agg >> 7
    batch = 8
    row16 = lax.broadcasted_iota(jnp.int32, (PACK, LANES), 0).astype(jnp.int16)
    one, zero = jnp.ones((PACK, LANES), BF16), jnp.zeros((PACK, LANES), BF16)

    def wide(row, kind):
        return jnp.broadcast_to(row, (PACK, LANES)).astype(kind)

    total = jnp.zeros((6 * bins, LANES), F32)
    for block in range(groups // batch):
        onehot, spread = [], []
        for g in range(block * batch, (block + 1) * batch):
            lane = wide(low[g : g + 1], jnp.int16)
            line = wide(high[g : g + 1], jnp.int16)
            onehot.append(
                jnp.concatenate(
                    [
                        jnp.where(lane == row16 + jnp.int16(first), one, zero)
                        for first in range(0, LANES, PACK)
                    ],
                    axis=0,
                )
            )
            chosen = [line == row16 + jnp.int16(first) for first in range(0, bins, PACK)]
            column = []
            for c in range(3):
                value = residual[c, g : g + 1, :]
                upper = value.astype(BF16).astype(F32)
                for part in (upper, value - upper):
                    part = wide(part, BF16)
                    column += [jnp.where(mask, part, zero) for mask in chosen]
            spread.append(jnp.concatenate(column, axis=0))
        total = total + lax.dot_general(
            jnp.concatenate(spread, axis=1),
            jnp.concatenate(onehot, axis=1),
            (((1,), (1,)), ((), ())),
            preferred_element_type=F32,
        )
    for c in range(3):
        first = 2 * c * bins
        out[c] = total[first : first + bins] + total[first + bins : first + 2 * bins]


def spread_max(values):
    top = jnp.max(jnp.max(values, axis=1, keepdims=True), axis=0, keepdims=True)
    return jnp.broadcast_to(top, values.shape)


def prepare_kernel(col, picks, start, halo_start, spot, rank, most, flip):
    bonds_of = col.shape[0]
    groups = col.shape[1] // LANES
    stride = bonds_of + 1

    def eight_tiles(block, carry):
        best, halo_best = carry

        def lanes_of(t):
            return pl.ds(pl.multiple_of((block * 8 + t) * LANES, LANES), LANES)

        for t in range(8):
            flip[pl.ds(t * stride, bonds_of), :] = col[:, lanes_of(t)]
        keys = []
        for k in range(bonds_of):
            c = flip[pl.ds(k, 8, stride=stride), :]
            keys.append(((c >> 8) << 13) | (k << 8) | (c & 255))
        keys = sort_planes(keys)
        pairs = [key >> 13 for key in keys]
        ranks = [jnp.zeros((8, LANES), jnp.int32)]
        for k in range(1, bonds_of):
            ranks.append(jnp.where(pairs[k] == pairs[k - 1], ranks[k - 1] + 1, 0))
        back = []
        here = jnp.zeros((8, LANES), jnp.int32)
        for k in range(bonds_of):
            local = pairs[k] < PACK
            here = jnp.maximum(here, jnp.where(local, ranks[k], 0))
            halo_best = jnp.maximum(halo_best, jnp.where(local, 0, ranks[k]))
            code = jnp.where(
                local,
                (ranks[k] << 4) | pairs[k],
                ((ranks[k] >> 2) << 4) | ((ranks[k] & 3) << 2) | ((pairs[k] - PACK) + (32 << 4)),
            )
            back.append((((keys[k] >> 8) & 31) << 10) | code)
            flip[pl.ds(k, 8, stride=stride), :] = keys[k]
        row = lax.broadcasted_iota(jnp.int32, (PACK, LANES), 0)
        for t in range(8):
            halves = [flip[pl.ds(t * stride + h * PACK, PACK), :] for h in range(2)]
            for h in range(2):
                picks[h * PACK : (h + 1) * PACK, lanes_of(t)] = (halves[h] & 255).astype(jnp.int16)
            first, second = [(x >> 13).astype(jnp.int16) for x in halves]
            for target, pair, extra in (
                (start, row.astype(jnp.int16), None),
                (halo_start, (PACK + (row & 3)).astype(jnp.int16), (row >> 2).astype(jnp.int16)),
            ):
                place = jnp.zeros((PACK, LANES), jnp.int16)
                for step in (16, 8, 4, 2, 1, 1):
                    probe = place + jnp.int16(step - 1)
                    inner = probe & jnp.int16(PACK - 1)
                    value = jnp.where(
                        probe < PACK, row_gather(first, inner), row_gather(second, inner)
                    )
                    place = jnp.where(value < pair, place + jnp.int16(step), place)
                target[:, lanes_of(t)] = place if extra is None else place + extra
        back = sort_planes(back)
        for k in range(bonds_of):
            flip[pl.ds(k, 8, stride=stride), :] = back[k] & 1023
        for t in range(8):
            for h in range(2):
                code = flip[pl.ds(t * stride + h * PACK, PACK), :]
                rows = slice(h * PACK, (h + 1) * PACK)
                spot[rows, lanes_of(t)] = (code & 15).astype(jnp.int16)
                rank[rows, lanes_of(t)] = (code >> 4).astype(jnp.int16)
        most[pl.ds(pl.multiple_of(block * 8, 8), 8), :] = spread_max(here)
        return jnp.maximum(best, here), halo_best

    zero = jnp.zeros((8, LANES), jnp.int32)
    best, halo_best = lax.fori_loop(0, groups // 8, eight_tiles, (zero, zero))
    most[groups : groups + 8, :] = spread_max(best)
    most[groups + 8 :, :] = spread_max(halo_best) >> 2


def layer(place, picks, even, odd):
    inner = place & jnp.int16(PACK - 1)
    pick = jnp.where(
        place < PACK, row_gather(picks[0], inner), row_gather(picks[1], inner)
    )
    lane = pick & jnp.int16(LANES - 1)
    second = pick >= LANES
    return [
        jnp.where(second, lane_gather(odd[e], lane), lane_gather(even[e], lane))
        for e in range(3)
    ]


def put_back(values, number, spots, ranks, out):
    for h in range(2):
        hit = ranks[h] == number
        for e in range(3):
            out[h][e] = jnp.where(hit, row_gather(values[e], spots[h]), out[h][e])


def halves_of(ref, lanes):
    return [ref[h * PACK : (h + 1) * PACK, lanes] for h in range(2)]


def splat(number):
    return jnp.full((PACK, LANES), number, jnp.int32).astype(jnp.int16)


LAYERS = 10
HALO_LAYERS = 3


def local_kernel(smooth, picks, start, spot, rank, most, out, *, first, tiles, unroll=8):
    even = [smooth[e, pl.ds(0, PACK, stride=2), :].astype(BF16) for e in range(3)]
    odd = [smooth[e, pl.ds(1, PACK, stride=2), :].astype(BF16) for e in range(3)]

    def some_tiles(t, carry):
        for u in range(unroll):
            source = pl.ds(pl.multiple_of((first + t * unroll + u) * LANES, LANES), LANES)
            target = pl.ds(pl.multiple_of((t * unroll + u) * LANES, LANES), LANES)
            place = start[:, source]
            chosen = halves_of(picks, source)
            spots, ranks = halves_of(spot, source), halves_of(rank, source)
            found = [[jnp.zeros((PACK, LANES), BF16)] * 3 for h in range(2)]
            for m in range(LAYERS):
                values = layer(place + jnp.int16(m), chosen, even, odd)
                put_back(values, jnp.int16(m), spots, ranks, found)
            for h in range(2):
                for e in range(3):
                    out[e, h * PACK : (h + 1) * PACK, target] = found[h][e]
        return carry

    lax.fori_loop(0, tiles // unroll, some_tiles, 0)

    @pl.when(most[smooth.shape[1], 0] >= LAYERS)
    def _():
        def eight_tiles(block, carry):
            def more(m, inner):
                number = splat(m)
                for t in range(8):
                    tile = block * 8 + t
                    source = pl.ds(pl.multiple_of((first + tile) * LANES, LANES), LANES)
                    target = pl.ds(pl.multiple_of(tile * LANES, LANES), LANES)
                    found = [
                        [out[e, h * PACK : (h + 1) * PACK, target] for e in range(3)]
                        for h in range(2)
                    ]
                    values = layer(
                        start[:, source] + number, halves_of(picks, source), even, odd
                    )
                    put_back(
                        values, number, halves_of(spot, source), halves_of(rank, source), found
                    )
                    for h in range(2):
                        for e in range(3):
                            out[e, h * PACK : (h + 1) * PACK, target] = found[h][e]
                return inner

            lax.fori_loop(LAYERS, most[first + block * 8, 0] + 1, more, 0)
            return carry

        lax.fori_loop(0, tiles // 8, eight_tiles, 0)


def dense_solve(matrix, vector):
    solved = []
    for c in range(3):
        total = matrix[c, 0] * vector[0]
        for e in range(1, 3):
            total = total + matrix[c, e] * vector[e]
        solved.append(total)
    return solved


def sideways(x):
    lines = x.shape[0]
    lane = lax.broadcasted_iota(jnp.int32, x.shape, 1)
    right = pltpu.roll(x, 1, 1)
    right = jnp.where(lane == 0, pltpu.roll(right, 1, 0), right)
    left = pltpu.roll(x, LANES - 1, 1)
    left = jnp.where(lane == LANES - 1, pltpu.roll(left, lines - 1, 0), left)
    return right, left


def inside_masks(shape):
    lane = lax.broadcasted_iota(jnp.int32, shape, 1)
    line = lax.broadcasted_iota(jnp.int32, shape, 0)
    return (
        jnp.logical_or(lane > 0, line > 0),
        jnp.logical_or(lane < LANES - 1, line < shape[0] - 1),
    )


def halo_kernel(*refs, stage, sizes, scale_old, scale_new, subs, unroll=8):
    (place, most, picks, halo_start, spot, rank, ghost, outer, inner) = refs[:9]
    (residual, dinv, smooth, update, bonds) = refs[9:14]
    pieces = len(sizes)
    local_found = refs[14 : 14 + pieces]
    refs = refs[14 + pieces :]
    if stage == 0:
        rhs, arrived, coarse_dinv = refs[:3]
        new_smooth, new_update, base, out_outer, out_inner = refs[3:8]
        refs = refs[8:]
    elif stage == 1:
        first_outer, first_inner, base, couple_own = refs[:4]
        new_smooth, new_update, out_outer, out_inner, far_next, far_prev = refs[4:10]
        refs = refs[10:]
    else:
        (new_smooth,) = refs[:1]
        refs = refs[1:]
    applied, other, partial = refs
    groups = smooth.shape[1]
    if stage == 0:
        vector = [rhs[e] + arrived[e] for e in range(3)]
        coarse_groups = base.shape[1]
        for c in range(3):
            for g in range(coarse_groups):
                lanes = slice(g * LANES, (g + 1) * LANES)
                total = coarse_dinv[c, 0:1, lanes] * vector[0][g : g + 1]
                for e in range(1, 3):
                    total = total + coarse_dinv[c, e : e + 1, lanes] * vector[e][g : g + 1]
                base[c, g : g + 1, :] = total
        for c in range(3):
            row = base[c].astype(BF16)
            out_outer[3 + c] = row
            out_inner[3 + c] = row
        out_outer[6:10] = inner[3:7]
        out_inner[6:10] = outer[3:7]
    elif stage == 1:
        out_outer[3:6] = inner[3:6]
        out_inner[3:6] = outer[3:6]
        me = jnp.concatenate([place[...]] * (base.shape[1] // 8), axis=0)
        even = (me & 1) == 0
        links = [couple_own[3 + k].astype(F32) for k in range(4)]
        links[0] = jnp.where(me > 0, links[0], 0.0)
        links[1] = jnp.where(me < subs - 1, links[1], 0.0)
        for k, mask in zip((2, 3), inside_masks(me.shape)):
            links[k] = jnp.where(mask, links[k], 0.0)
        for c in range(3):
            own = base[c]
            outer_row, inner_row = outer[3 + c].astype(F32), inner[3 + c].astype(F32)
            below = jnp.where(even, outer_row, inner_row)
            above = jnp.where(even, inner_row, outer_row)
            right, left = sideways(own)
            iterate = own + (
                links[0] * below + links[1] * above + links[2] * right + links[3] * left
            )
            for message, beyond in ((far_next, above), (far_prev, below)):
                message[c] = own.astype(BF16)
                message[3 + c] = iterate.astype(BF16)
                message[6 + c] = beyond.astype(BF16)
        for k in range(4):
            outer_row = first_outer[3 + k].astype(F32)
            inner_row = first_inner[3 + k].astype(F32)
            far_next[9 + k] = jnp.where(even, inner_row, outer_row).astype(BF16)
            far_prev[9 + k] = jnp.where(even, outer_row, inner_row).astype(BF16)
    wanted = ghost[...]
    half = wanted.shape[0] // 2
    low = wanted & (LANES - 1)
    high = wanted >> 7
    upper = jnp.where(lax.broadcasted_iota(jnp.int32, wanted.shape, 0) < half, 1, 0)
    from_outer = (upper ^ (place[...] & 1)) == 1
    found = [jnp.zeros(wanted.shape, F32)] * 3
    for e in range(3):
        applied[e] = outer[e].astype(F32)
        other[e] = inner[e].astype(F32)
    for g in range(groups):
        chosen = high == g
        for e in range(3):
            rows = jnp.where(
                from_outer,
                jnp.broadcast_to(applied[e, g : g + 1, :], wanted.shape),
                jnp.broadcast_to(other[e, g : g + 1, :], wanted.shape),
            )
            found[e] = jnp.where(chosen, lane_gather(rows, low), found[e])
    pair = (lax.broadcasted_iota(jnp.int32, wanted.shape, 0) & 3) * 2

    def four_times(rows):
        return jnp.concatenate([rows, rows], axis=0).astype(BF16)

    even = [four_times(row_gather(found[e], pair)) for e in range(3)]
    odd = [four_times(row_gather(found[e], pair + 1)) for e in range(3)]

    def apply_tile(tile, values):
        here = pl.ds(pl.multiple_of(tile * LANES, LANES), LANES)
        totals = []
        for c in range(3):
            total = jnp.zeros((PACK, LANES), F32)
            for h in range(2):
                for e in range(3):
                    block = bonds[c, e, h * PACK : (h + 1) * PACK, here].astype(F32)
                    total = total + block * values[h][e].astype(F32)
            totals.append(total[:8] + total[8:])
        return totals

    for piece, part in enumerate(local_found):
        first = sum(sizes[:piece])

        def some_tiles(t, carry, part=part, first=first):
            for u in range(unroll):
                there = pl.ds(pl.multiple_of((t * unroll + u) * LANES, LANES), LANES)
                tile = first + t * unroll + u
                here = pl.ds(pl.multiple_of(tile * LANES, LANES), LANES)
                chosen = halves_of(picks, here)
                spots, ranks = halves_of(spot, here), halves_of(rank, here)
                values = [
                    [part[e, h * PACK : (h + 1) * PACK, there] for e in range(3)]
                    for h in range(2)
                ]
                for v in range(HALO_LAYERS):
                    row = layer(halo_start[:, here] + jnp.int16(4 * v), chosen, even, odd)
                    put_back(row, jnp.int16(32 + v), spots, ranks, values)
                totals = apply_tile(tile, values)
                for c in range(3):
                    partial[c, pl.ds(pl.multiple_of(tile * 8, 8), 8), :] = totals[c]
            return carry

        lax.fori_loop(0, sizes[piece] // unroll, some_tiles, 0)

    last_layer = most[groups + 8, 0]

    @pl.when(last_layer >= HALO_LAYERS)
    def _():
        def one_tile(tile, carry):
            here = pl.ds(pl.multiple_of(tile * LANES, LANES), LANES)

            def more(v, flat):
                values = [list(flat[:3]), list(flat[3:])]
                row = layer(halo_start[:, here] + splat(4 * v), halves_of(picks, here), even, odd)
                put_back(row, splat(32 + v), halves_of(spot, here), halves_of(rank, here), values)
                return tuple(values[0] + values[1])

            empty = (jnp.zeros((PACK, LANES), BF16),) * 6
            flat = lax.fori_loop(HALO_LAYERS, last_layer + 1, more, empty)
            totals = apply_tile(tile, [flat[:3], flat[3:]])
            for c in range(3):
                rows = pl.ds(pl.multiple_of(tile * 8, 8), 8)
                partial[c, rows, :] = partial[c, rows, :] + totals[c]
            return carry

        lax.fori_loop(0, groups, one_tile, 0)

    remainder = []
    for e in range(3):
        total = partial[e, pl.ds(0, groups, stride=8), :]
        for row in range(1, 8):
            total = total + partial[e, pl.ds(row, groups, stride=8), :]
        remainder.append(residual[e] - smooth[e] - total)
    solved = dense_solve(dinv, remainder)
    for c in range(3):
        change = scale_old * update[c] + scale_new * solved[c]
        total = smooth[c] + change
        new_smooth[c] = total
        if stage < SWEEPS - 1:
            new_update[c] = change
            out_outer[c] = total.astype(BF16)
            out_inner[c] = total.astype(BF16)


def coarse_kernel(*refs, subs):
    (place, base, own_couple) = refs[:3]
    first, second, third = refs[3:5], refs[5:7], refs[7:9]
    far_after, far_before, aggregate, smooth = refs[9:13]
    out, field, links, kept = refs[13:]
    groups = base.shape[1]
    me = jnp.concatenate([place[...]] * (groups // 8), axis=0)
    even = (me & 1) == 0

    def valid(row):
        if row < 0:
            return jnp.where(me + row >= 0, 1.0, 0.0)
        return jnp.where(me + row < subs, 1.0, 0.0)

    def from_after(pair, start):
        return lambda i: jnp.where(
            even, pair[0][start + i].astype(F32), pair[1][start + i].astype(F32)
        )

    def from_before(pair, start):
        return from_after((pair[1], pair[0]), start)

    def plain(ref, start):
        return lambda i: ref[start + i].astype(F32)

    base_rows = {
        -4: plain(far_after, 0),
        -3: plain(far_after, 6),
        -2: from_after(third, 3),
        -1: from_after(second, 3),
        1: from_before(second, 3),
        2: from_before(third, 3),
        3: plain(far_before, 6),
        4: plain(far_before, 0),
    }
    link_rows = {
        -3: plain(far_after, 9),
        -2: from_after(second, 6),
        -1: from_after(first, 3),
        1: from_before(first, 3),
        2: from_before(second, 6),
        3: plain(far_before, 9),
    }
    for g in range(groups):
        for k in range(4):
            links[FAR - 1, k, g : g + 1, :] = own_couple[
                k : k + 1, g * LANES : (g + 1) * LANES
            ]
    for row, read in link_rows.items():
        for k in range(4):
            links[row + FAR - 1, k] = read(k) * valid(row)
    for k, mask in zip((2, 3), inside_masks(me.shape)):
        for row in range(2 * FAR - 1):
            links[row, k] = jnp.where(mask, links[row, k], 0.0)
    for c in range(3):
        field[0, FAR, c] = base[c]
        for row, read in base_rows.items():
            field[0, row + FAR, c] = read(c) * valid(row)
        field[1, 0, c] = far_after[3 + c].astype(F32) * valid(-FAR)
        field[1, 2 * FAR, c] = far_before[3 + c].astype(F32) * valid(FAR)
        for row in range(2 * FAR + 1):
            kept[row, c] = field[0, row, c]
    for step in range(STEPS):
        old, new = step % 2, (step + 1) % 2
        reach = min(STEPS - 1 - step, FAR - 1)
        for row in range(-reach, reach + 1):
            spot = row + FAR
            weights = [links[spot - 1, k] for k in range(4)]
            for c in range(3):
                right, left = sideways(field[old, spot, c])
                field[new, spot, c] = kept[spot, c] + (
                    weights[0] * field[old, spot - 1, c]
                    + weights[1] * field[old, spot + 1, c]
                    + weights[2] * right
                    + weights[3] * left
                )
    final = STEPS % 2
    agg = aggregate[...] & (groups * LANES - 1)
    for block in range(agg.shape[0] // 8):
        index = agg[block * 8 : (block + 1) * 8]
        low = index & (LANES - 1)
        high = index >> 7
        found = [jnp.zeros((8, LANES), F32)] * 3
        for g in range(groups):
            chosen = high == g
            for c in range(3):
                rows = jnp.broadcast_to(field[final, FAR, c, g : g + 1, :], (8, LANES))
                found[c] = jnp.where(chosen, lane_gather(rows, low), found[c])
        for c in range(3):
            result = smooth[c, block * 8 : (block + 1) * 8, :] + found[c]
            for r in range(8):
                lanes = slice((block * 8 + r) * LANES, (block * 8 + r + 1) * LANES)
                out[c : c + 1, lanes] = result[r : r + 1]


def shifted(value, steps):
    count = lax.axis_size("sub")
    return lax.ppermute(value, "sub", [(i, (i + steps) % count) for i in range(count)])


def across_chips(value):
    count = lax.axis_size("sub")
    pairs = [(i, (i + 1) % count) for i in range(1, count, 2)]
    return lax.ppermute(value, "sub", pairs + [(j, i) for i, j in pairs])


def within_chip(value):
    count = lax.axis_size("sub")
    pairs = [(i, i + 1) for i in range(0, count, 2)]
    return lax.ppermute(value, "sub", pairs + [(j, i) for i, j in pairs])


def exchanged_by_pairs(outer, inner):
    return across_chips(outer), within_chip(inner)


def local_pass(smooth, picks, start, spot, rank, most, first, tiles, us=None):
    return call(
        functools.partial(local_kernel, first=first, tiles=tiles),
        jax.ShapeDtypeStruct((3, picks.shape[0], tiles * LANES), BF16),
        (smooth, picks, start, spot, rank, most),
        us=us or 0.12 * tiles,
    )


def body(
    fine_residual, bonds, bond_col, ghost_points, fine_dinv, aggregate, coarse_dinv, coarse_couple
):
    points = fine_residual.shape[1]
    groups = points // LANES
    bonds_of = bond_col.shape[0]
    per_group = coarse_dinv.shape[2]
    coarse_groups = per_group // LANES
    assert per_group & (per_group - 1) == 0
    sub = lax.axis_index("sub")
    doms = lax.axis_size("dom")
    ghost = ghost_points.reshape(-1, LANES)
    agg = aggregate.reshape(groups, LANES)
    relaid = bonds.transpose(1, 2, 0, 3)
    sds = jax.ShapeDtypeStruct
    field = sds((3, groups, LANES), F32)
    coarse_field = sds((3, coarse_groups, LANES), F32)

    def message(rows):
        return sds((rows, groups, LANES), BF16)

    residual, rhs = call(
        restrict_kernel,
        (field, coarse_field),
        tuple(pltpu.with_memory_space_constraint(x, pltpu.HBM) for x in (fine_residual, agg)),
        scratch=[
            VMEM(fine_residual.shape, F32),
            VMEM(agg.shape, jnp.int32),
            pltpu.SemaphoreType.DMA((2,)),
        ],
        us=1.6,
        spaces={0: pltpu.HBM, 1: pltpu.HBM},
    )
    dinv, smooth, packed = call(
        first_kernel,
        (sds((3, 3, groups, LANES), F32), field, message(7)),
        (residual, fine_dinv, coarse_couple),
        us=0.8,
    )
    update = smooth
    own_packed = packed
    place = jnp.full((8, LANES), sub, jnp.int32)
    def exchanged(value, step):
        return lax.ppermute(value, "dom", [(i, i ^ step) for i in range(doms)])

    assert doms == 8
    arrived = exchanged(rhs, 1)
    columns, rhs = lax.optimization_barrier((bond_col, rhs))

    def shorts(rows):
        return sds((rows, points), jnp.int16)

    picks, start, halo_start, spot, rank, most = call(
        prepare_kernel,
        (
            shorts(bonds_of),
            shorts(PACK),
            shorts(PACK),
            shorts(bonds_of),
            shorts(bonds_of),
            sds((groups + 16, LANES), jnp.int32),
        ),
        (columns,),
        scratch=[VMEM((8 * (bonds_of + 2), LANES), jnp.int32)],
        us=2.5,
    )
    start, rhs = lax.optimization_barrier((start, rhs))
    rhs = rhs + arrived
    packed, start, rhs = lax.optimization_barrier((packed, start, rhs))
    arrived = exchanged(rhs, 2)
    first_outer = across_chips(packed)
    early = local_pass(smooth, picks, start, spot, rank, most, 0, 8)
    rhs, early = lax.optimization_barrier((rhs, early))
    rhs = rhs + arrived
    packed_inner, start, rhs = lax.optimization_barrier((packed, start, rhs))
    arrived = exchanged(rhs, 6)
    first = arrived_sides = (first_outer, within_chip(packed_inner))

    factor = HALF / CENTER
    for stage in range(SWEEPS):
        factor_new = 1.0 / (2.0 * CENTER / HALF - factor)
        lists = (smooth, picks, start, spot, rank, most)
        if stage == 0:
            sizes = (8, groups - 8)
            found = [early, local_pass(*lists, *sizes)]
        elif stage == 1:
            sizes = (groups,)
            found = [local_pass(*lists, 0, groups)]
        else:
            sizes = (groups // 2,) * 2
            found = [local_pass(*lists, 0, sizes[0], us=0.2)]
            far_next, far_prev, start, found[0] = lax.optimization_barrier(
                (far_next, far_prev, start, found[0])
            )
            far_after = shifted(far_next, 4)
            far_before = shifted(far_prev, -4)
            found.append(
                local_pass(smooth, picks, start, spot, rank, most, *sizes, us=0.2)
            )
        inputs = [place, most, picks, halo_start, spot, rank, ghost, *arrived_sides]
        inputs += [residual, dinv, smooth, update, relaid, *found]
        if stage == 0:
            inputs += [rhs, arrived, coarse_dinv]
            outs = (field, field, coarse_field, message(10), message(10))
        elif stage == 1:
            inputs += [*first, base, own_packed]
            outs = (field, field, message(6), message(6), message(13), message(13))
        else:
            outs = (field,)
        result = call(
            functools.partial(
                halo_kernel,
                stage=stage,
                sizes=sizes,
                scale_old=factor_new * factor,
                scale_new=2.0 * factor_new / HALF,
                subs=lax.axis_size("sub"),
            ),
            outs,
            inputs,
            scratch=[VMEM((3, groups, LANES), F32)] * 2 + [VMEM((3, 8 * groups, LANES), F32)],
            us=2.5,
        )
        factor = factor_new
        if stage == 0:
            smooth, update, base, outer, inner = result
            second = arrived_sides = exchanged_by_pairs(outer, inner)
        elif stage == 1:
            smooth, update, outer, inner, far_next, far_prev = result
            third = arrived_sides = exchanged_by_pairs(outer, inner)
        else:
            (smooth,) = result
    return call(
        functools.partial(coarse_kernel, subs=lax.axis_size("sub")),
        sds((3, points), F32),
        (
            place,
            base,
            coarse_couple,
            *first,
            *second,
            *third,
            far_after,
            far_before,
            agg,
            smooth,
        ),
        scratch=[
            VMEM((2, 2 * FAR + 1, 3, coarse_groups, LANES), F32),
            VMEM((2 * FAR - 1, 4, coarse_groups, LANES), F32),
            VMEM((2 * FAR + 1, 3, coarse_groups, LANES), F32),
        ],
        us=2.0,
    )


def solution(mesh):
    placed = (
        P(None, ("dom", "sub")),
        P(None, None, None, ("dom", "sub")),
        P(None, ("dom", "sub")),
        P(("dom", "sub"), None, None),
        P(None, None, ("dom", "sub")),
        P(("dom", "sub")),
        P(None, None, "sub"),
        P(None, "sub"),
    )
    return jax.shard_map(
        body, mesh=mesh, in_specs=placed, out_specs=P(None, ("dom", "sub")), check_vma=False
    )
```

```python
import functools

import jax
import jax.numpy as jnp
from jax import lax
from jax.experimental import pallas as pl
from jax.experimental.pallas import tpu as pltpu
from jax.sharding import PartitionSpec as P

SWEEPS = 3
STEPS = 5
FAR = 4
LOW_EIG = 0.3
HIGH_EIG = 2.2
CENTER = (HIGH_EIG + LOW_EIG) / 2.0
HALF = (HIGH_EIG - LOW_EIG) / 2.0
LANES = 128
PACK = 16
LAYERS = 10
HALO_LAYERS = 3
F32 = jnp.float32
BF16 = jnp.bfloat16
VMEM = pltpu.VMEM


def gather(rows, index, axis):
    numbers = lax.GatherDimensionNumbers(
        offset_dims=(),
        collapsed_slice_dims=(axis,),
        start_index_map=(axis,),
        operand_batching_dims=(1 - axis,),
        start_indices_batching_dims=(1 - axis,),
    )
    return lax.gather(
        rows,
        index[..., None],
        numbers,
        (1, 1),
        mode=lax.GatherScatterMode.PROMISE_IN_BOUNDS,
    )


def lane_gather(rows, index):
    return gather(rows, index, 1)


def row_gather(rows, index):
    return gather(rows, index, 0)


def sorting_network(count):
    pairs = []
    span = 1
    while span < count:
        gap = span
        while gap >= 1:
            for j in range(gap % span, count - gap, 2 * gap):
                for i in range(min(gap, count - j - gap)):
                    if (i + j) // (2 * span) == (i + j + gap) // (2 * span):
                        pairs.append((i + j, i + j + gap))
            gap //= 2
        span *= 2
    return pairs


def sort_planes(planes):
    planes = list(planes)
    for i, j in sorting_network(len(planes)):
        planes[i], planes[j] = (
            jnp.minimum(planes[i], planes[j]),
            jnp.maximum(planes[i], planes[j]),
        )
    return planes


def call(kernel, out, inputs, scratch=(), us=1.0, spaces={}, limit=16):
    return pl.pallas_call(
        kernel,
        out_shape=out,
        in_specs=[
            pl.BlockSpec(memory_space=spaces.get(i, VMEM)) for i in range(len(inputs))
        ],
        out_specs=jax.tree.map(
            lambda _: pl.BlockSpec(memory_space=VMEM), out
        ),
        scratch_shapes=list(scratch),
        cost_estimate=pl.CostEstimate(
            flops=int(us * 1.0e9), transcendentals=0, bytes_accessed=int(us * 1.0e6)
        ),
        compiler_params=pltpu.CompilerParams(vmem_limit_bytes=limit * 1024 * 1024),
    )(*inputs)


def rows_of(ref, lead, group):
    return ref[lead + (slice(group * LANES, (group + 1) * LANES),)]


def restrict_kernel(*refs):
    sources = refs[:2]
    dense_residual, rhs = refs[2:4]
    residual, aggregate, semaphores = refs[4:]
    copies = [
        pltpu.make_async_copy(source, target, semaphores.at[i])
        for i, (source, target) in enumerate(zip(sources, (residual, aggregate)))
    ]
    for copy in copies:
        copy.start()
    copies[0].wait()
    for g in range(dense_residual.shape[1]):
        for e in range(3):
            dense_residual[e, g : g + 1, :] = residual[
                e : e + 1, g * LANES : (g + 1) * LANES
            ]
    copies[1].wait()
    restrict(dense_residual, aggregate, rhs)


def first_kernel(dense_residual, dinv, couple, dense_dinv, smooth, message):
    groups = smooth.shape[1]
    coarse_groups = message.shape[1]
    for g in range(groups):
        lanes = slice(g * LANES, (g + 1) * LANES)
        for e in range(3):
            for c in range(3):
                dense_dinv[c, e, g : g + 1, :] = dinv[c, e : e + 1, lanes]
    for g in range(coarse_groups):
        lanes = slice(g * LANES, (g + 1) * LANES)
        for k in range(4):
            message[3 + k, g : g + 1, :] = couple[k : k + 1, lanes].astype(BF16)
    for c in range(3):
        total = dense_dinv[c, 0] * dense_residual[0]
        for e in range(1, 3):
            total = total + dense_dinv[c, e] * dense_residual[e]
        total = total * (1.0 / CENTER)
        smooth[c] = total
        message[c] = total.astype(BF16)


def restrict(residual, aggregate, out):
    groups = residual.shape[1]
    bins = out.shape[1]
    agg = aggregate[...] & (bins * LANES - 1)
    low = agg & (LANES - 1)
    high = agg >> 7
    batch = 8
    row16 = lax.broadcasted_iota(jnp.int32, (PACK, LANES), 0).astype(jnp.int16)
    one, zero = jnp.ones((PACK, LANES), BF16), jnp.zeros((PACK, LANES), BF16)

    def wide(row, kind):
        return jnp.broadcast_to(row, (PACK, LANES)).astype(kind)

    total = jnp.zeros((6 * bins, LANES), F32)
    for block in range(groups // batch):
        onehot, spread = [], []
        for g in range(block * batch, (block + 1) * batch):
            lane = wide(low[g : g + 1], jnp.int16)
            line = wide(high[g : g + 1], jnp.int16)
            onehot.append(
                jnp.concatenate(
                    [
                        jnp.where(lane == row16 + jnp.int16(first), one, zero)
                        for first in range(0, LANES, PACK)
                    ],
                    axis=0,
                )
            )
            chosen = [line == row16 + jnp.int16(first) for first in range(0, bins, PACK)]
            column = []
            for c in range(3):
                value = residual[c, g : g + 1, :]
                upper = value.astype(BF16).astype(F32)
                for part in (upper, value - upper):
                    part = wide(part, BF16)
                    column += [jnp.where(mask, part, zero) for mask in chosen]
            spread.append(jnp.concatenate(column, axis=0))
        total = total + lax.dot_general(
            jnp.concatenate(spread, axis=1),
            jnp.concatenate(onehot, axis=1),
            (((1,), (1,)), ((), ())),
            preferred_element_type=F32,
        )
    for c in range(3):
        first = 2 * c * bins
        out[c] = total[first : first + bins] + total[first + bins : first + 2 * bins]


def spread_max(values):
    top = jnp.max(jnp.max(values, axis=1, keepdims=True), axis=0, keepdims=True)
    return jnp.broadcast_to(top, values.shape)


def prepare_kernel(
    col, picks, start, halo_start, spot, rank, most, columns, halo_columns, flip
):
    bonds_of = col.shape[0]
    groups = col.shape[1] // LANES
    stride = bonds_of + 1

    def eight_tiles(block, carry):
        best, halo_best = carry

        def lanes_of(t):
            return pl.ds(pl.multiple_of((block * 8 + t) * LANES, LANES), LANES)

        for t in range(8):
            flip[pl.ds(t * stride, bonds_of), :] = col[:, lanes_of(t)]
        keys = []
        for k in range(bonds_of):
            c = flip[pl.ds(k, 8, stride=stride), :]
            keys.append(((c >> 8) << 13) | (k << 8) | (c & 255))
        keys = sort_planes(keys)
        pairs = [key >> 13 for key in keys]
        ranks = [jnp.zeros((8, LANES), jnp.int32)]
        for k in range(1, bonds_of):
            ranks.append(jnp.where(pairs[k] == pairs[k - 1], ranks[k - 1] + 1, 0))
        back = []
        here = jnp.zeros((8, LANES), jnp.int32)
        for k in range(bonds_of):
            local = pairs[k] < PACK
            here = jnp.maximum(here, jnp.where(local, ranks[k], 0))
            halo_best = jnp.maximum(halo_best, jnp.where(local, 0, ranks[k]))
            code = jnp.where(
                local,
                (ranks[k] << 4) | pairs[k],
                ((ranks[k] >> 2) << 4) | ((ranks[k] & 3) << 2) | ((pairs[k] - PACK) + (32 << 4)),
            )
            back.append((((keys[k] >> 8) & 31) << 10) | code)
            flip[pl.ds(k, 8, stride=stride), :] = keys[k]
        row = lax.broadcasted_iota(jnp.int32, (PACK, LANES), 0)
        for t in range(8):
            halves = [flip[pl.ds(t * stride + h * PACK, PACK), :] for h in range(2)]
            for h in range(2):
                picks[h * PACK : (h + 1) * PACK, lanes_of(t)] = (halves[h] & 255).astype(jnp.int16)
            first, second = [(x >> 13).astype(jnp.int16) for x in halves]
            for target, pair, extra in (
                (start, row.astype(jnp.int16), None),
                (halo_start, (PACK + (row & 3)).astype(jnp.int16), (row >> 2).astype(jnp.int16)),
            ):
                place = jnp.zeros((PACK, LANES), jnp.int16)
                for step in (16, 8, 4, 2, 1, 1):
                    probe = place + jnp.int16(step - 1)
                    inner = probe & jnp.int16(PACK - 1)
                    value = jnp.where(
                        probe < PACK, row_gather(first, inner), row_gather(second, inner)
                    )
                    place = jnp.where(value < pair, place + jnp.int16(step), place)
                place = place if extra is None else place + extra
                target[:, lanes_of(t)] = place
                chosen = [(x & 255).astype(jnp.int16) for x in halves]
                if extra is None:
                    for m in range(LAYERS):
                        columns[m * PACK : (m + 1) * PACK, lanes_of(t)] = picked(
                            place + jnp.int16(m), chosen
                        )
                else:
                    for v in range(HALO_LAYERS):
                        halo_columns[v * PACK : (v + 1) * PACK, lanes_of(t)] = picked(
                            place + jnp.int16(4 * v), chosen
                        )
        back = sort_planes(back)
        for k in range(bonds_of):
            flip[pl.ds(k, 8, stride=stride), :] = back[k] & 1023
        for t in range(8):
            for h in range(2):
                code = flip[pl.ds(t * stride + h * PACK, PACK), :]
                rows = slice(h * PACK, (h + 1) * PACK)
                spot[rows, lanes_of(t)] = (code & 15).astype(jnp.int16)
                rank[rows, lanes_of(t)] = (code >> 4).astype(jnp.int16)
        most[pl.ds(pl.multiple_of(block * 8, 8), 8), :] = spread_max(here)
        return jnp.maximum(best, here), halo_best

    zero = jnp.zeros((8, LANES), jnp.int32)
    best, halo_best = lax.fori_loop(0, groups // 8, eight_tiles, (zero, zero))
    most[groups : groups + 8, :] = spread_max(best)
    most[groups + 8 :, :] = spread_max(halo_best) >> 2


def picked(place, picks):
    inner = place & jnp.int16(PACK - 1)
    return jnp.where(place < PACK, row_gather(picks[0], inner), row_gather(picks[1], inner))


def layer(column, even, odd):
    lane = column & jnp.int16(LANES - 1)
    second = column >= LANES
    return [
        jnp.where(second, lane_gather(odd[e], lane), lane_gather(even[e], lane))
        for e in range(3)
    ]


def put_back(values, number, spots, ranks, out):
    for h in range(2):
        hit = ranks[h] == number
        for e in range(3):
            out[h][e] = jnp.where(hit, row_gather(values[e], spots[h]), out[h][e])


def halves_of(ref, lanes):
    return [ref[h * PACK : (h + 1) * PACK, lanes] for h in range(2)]


def splat(number):
    return jnp.full((PACK, LANES), number, jnp.int32).astype(jnp.int16)


def local_kernel(
    smooth, picks, start, spot, rank, most, columns, out, *, first, tiles, unroll
):
    even = [smooth[e, pl.ds(0, PACK, stride=2), :].astype(BF16) for e in range(3)]
    odd = [smooth[e, pl.ds(1, PACK, stride=2), :].astype(BF16) for e in range(3)]

    def some_tiles(t, carry):
        for u in range(unroll):
            source = pl.ds(pl.multiple_of((first + t * unroll + u) * LANES, LANES), LANES)
            target = pl.ds(pl.multiple_of((t * unroll + u) * LANES, LANES), LANES)
            spots, ranks = halves_of(spot, source), halves_of(rank, source)
            found = [[jnp.zeros((PACK, LANES), BF16)] * 3 for h in range(2)]
            for m in range(LAYERS):
                values = layer(columns[m * PACK : (m + 1) * PACK, source], even, odd)
                put_back(values, jnp.int16(m), spots, ranks, found)
            for h in range(2):
                for e in range(3):
                    out[e, h * PACK : (h + 1) * PACK, target] = found[h][e]
        return carry

    lax.fori_loop(0, tiles // unroll, some_tiles, 0)

    @pl.when(most[smooth.shape[1], 0] >= LAYERS)
    def _():
        def eight_tiles(block, carry):
            def more(m, inner):
                number = splat(m)
                for t in range(8):
                    tile = block * 8 + t
                    source = pl.ds(pl.multiple_of((first + tile) * LANES, LANES), LANES)
                    target = pl.ds(pl.multiple_of(tile * LANES, LANES), LANES)
                    found = [
                        [out[e, h * PACK : (h + 1) * PACK, target] for e in range(3)]
                        for h in range(2)
                    ]
                    column = picked(start[:, source] + number, halves_of(picks, source))
                    values = layer(column, even, odd)
                    put_back(
                        values, number, halves_of(spot, source), halves_of(rank, source), found
                    )
                    for h in range(2):
                        for e in range(3):
                            out[e, h * PACK : (h + 1) * PACK, target] = found[h][e]
                return inner

            lax.fori_loop(LAYERS, most[first + block * 8, 0] + 1, more, 0)
            return carry

        lax.fori_loop(0, tiles // 8, eight_tiles, 0)


def dense_solve(matrix, vector):
    solved = []
    for c in range(3):
        total = matrix[c, 0] * vector[0]
        for e in range(1, 3):
            total = total + matrix[c, e] * vector[e]
        solved.append(total)
    return solved


def sideways(x):
    lines = x.shape[0]
    lane = lax.broadcasted_iota(jnp.int32, x.shape, 1)
    right = pltpu.roll(x, 1, 1)
    right = jnp.where(lane == 0, pltpu.roll(right, 1, 0), right)
    left = pltpu.roll(x, LANES - 1, 1)
    left = jnp.where(lane == LANES - 1, pltpu.roll(left, lines - 1, 0), left)
    return right, left


def inside_masks(shape):
    lane = lax.broadcasted_iota(jnp.int32, shape, 1)
    line = lax.broadcasted_iota(jnp.int32, shape, 0)
    return (
        jnp.logical_or(lane > 0, line > 0),
        jnp.logical_or(lane < LANES - 1, line < shape[0] - 1),
    )


def halo_kernel(*refs, stage, sizes, scale_old, scale_new, subs, unroll=8):
    (place, most, picks, halo_start, halo_columns, spot, rank, ghost) = refs[:8]
    (outer, inner, residual, dinv, smooth, update, bonds) = refs[8:15]
    pieces = len(sizes)
    local_found = refs[15 : 15 + pieces]
    refs = refs[15 + pieces :]
    if stage == 0:
        rhs, arrived, coarse_dinv = refs[:3]
        new_smooth, new_update, base, out_outer, out_inner = refs[3:8]
        refs = refs[8:]
    elif stage == 1:
        first_outer, first_inner, base, couple_own = refs[:4]
        new_smooth, new_update, out_outer, out_inner, far_next, far_prev = refs[4:10]
        refs = refs[10:]
    else:
        (new_smooth,) = refs[:1]
        refs = refs[1:]
    applied, other, partial = refs
    groups = smooth.shape[1]
    if stage == 0:
        vector = [rhs[e] + arrived[e] for e in range(3)]
        coarse_groups = base.shape[1]
        for c in range(3):
            for g in range(coarse_groups):
                lanes = slice(g * LANES, (g + 1) * LANES)
                total = coarse_dinv[c, 0:1, lanes] * vector[0][g : g + 1]
                for e in range(1, 3):
                    total = total + coarse_dinv[c, e : e + 1, lanes] * vector[e][g : g + 1]
                base[c, g : g + 1, :] = total
        for c in range(3):
            row = base[c].astype(BF16)
            out_outer[3 + c] = row
            out_inner[3 + c] = row
        out_outer[6:10] = inner[3:7]
        out_inner[6:10] = outer[3:7]
    elif stage == 1:
        out_outer[3:6] = inner[3:6]
        out_inner[3:6] = outer[3:6]
        me = jnp.concatenate([place[...]] * (base.shape[1] // 8), axis=0)
        even = (me & 1) == 0
        links = [couple_own[3 + k].astype(F32) for k in range(4)]
        links[0] = jnp.where(me > 0, links[0], 0.0)
        links[1] = jnp.where(me < subs - 1, links[1], 0.0)
        for k, mask in zip((2, 3), inside_masks(me.shape)):
            links[k] = jnp.where(mask, links[k], 0.0)
        for c in range(3):
            own = base[c]
            outer_row, inner_row = outer[3 + c].astype(F32), inner[3 + c].astype(F32)
            below = jnp.where(even, outer_row, inner_row)
            above = jnp.where(even, inner_row, outer_row)
            right, left = sideways(own)
            iterate = own + (
                links[0] * below + links[1] * above + links[2] * right + links[3] * left
            )
            for message, beyond in ((far_next, above), (far_prev, below)):
                message[c] = own.astype(BF16)
                message[3 + c] = iterate.astype(BF16)
                message[6 + c] = beyond.astype(BF16)
        for k in range(4):
            outer_row = first_outer[3 + k].astype(F32)
            inner_row = first_inner[3 + k].astype(F32)
            far_next[9 + k] = jnp.where(even, inner_row, outer_row).astype(BF16)
            far_prev[9 + k] = jnp.where(even, outer_row, inner_row).astype(BF16)
    wanted = ghost[...]
    half = wanted.shape[0] // 2
    low = wanted & (LANES - 1)
    high = wanted >> 7
    upper = jnp.where(lax.broadcasted_iota(jnp.int32, wanted.shape, 0) < half, 1, 0)
    from_outer = (upper ^ (place[...] & 1)) == 1
    found = [jnp.zeros(wanted.shape, F32)] * 3
    for e in range(3):
        applied[e] = outer[e].astype(F32)
        other[e] = inner[e].astype(F32)
    for g in range(groups):
        chosen = high == g
        for e in range(3):
            rows = jnp.where(
                from_outer,
                jnp.broadcast_to(applied[e, g : g + 1, :], wanted.shape),
                jnp.broadcast_to(other[e, g : g + 1, :], wanted.shape),
            )
            found[e] = jnp.where(chosen, lane_gather(rows, low), found[e])
    pair = (lax.broadcasted_iota(jnp.int32, wanted.shape, 0) & 3) * 2

    def four_times(rows):
        return jnp.concatenate([rows, rows], axis=0).astype(BF16)

    even = [four_times(row_gather(found[e], pair)) for e in range(3)]
    odd = [four_times(row_gather(found[e], pair + 1)) for e in range(3)]

    def apply_tile(tile, values):
        here = pl.ds(pl.multiple_of(tile * LANES, LANES), LANES)
        totals = []
        for c in range(3):
            total = jnp.zeros((PACK, LANES), F32)
            for h in range(2):
                for e in range(3):
                    block = bonds[c, e, h * PACK : (h + 1) * PACK, here].astype(F32)
                    total = total + block * values[h][e].astype(F32)
            totals.append(total[:8] + total[8:])
        return totals

    for piece, part in enumerate(local_found):
        first = sum(sizes[:piece])

        def some_tiles(t, carry, part=part, first=first):
            for u in range(unroll):
                there = pl.ds(pl.multiple_of((t * unroll + u) * LANES, LANES), LANES)
                tile = first + t * unroll + u
                here = pl.ds(pl.multiple_of(tile * LANES, LANES), LANES)
                spots, ranks = halves_of(spot, here), halves_of(rank, here)
                values = [
                    [part[e, h * PACK : (h + 1) * PACK, there] for e in range(3)]
                    for h in range(2)
                ]
                for v in range(HALO_LAYERS):
                    row = layer(halo_columns[v * PACK : (v + 1) * PACK, here], even, odd)
                    put_back(row, jnp.int16(32 + v), spots, ranks, values)
                totals = apply_tile(tile, values)
                for c in range(3):
                    partial[c, pl.ds(pl.multiple_of(tile * 8, 8), 8), :] = totals[c]
            return carry

        lax.fori_loop(0, sizes[piece] // unroll, some_tiles, 0)

    last_layer = most[groups + 8, 0]

    @pl.when(last_layer >= HALO_LAYERS)
    def _():
        def one_tile(tile, carry):
            here = pl.ds(pl.multiple_of(tile * LANES, LANES), LANES)

            def more(v, flat):
                values = [list(flat[:3]), list(flat[3:])]
                column = picked(halo_start[:, here] + splat(4 * v), halves_of(picks, here))
                row = layer(column, even, odd)
                put_back(row, splat(32 + v), halves_of(spot, here), halves_of(rank, here), values)
                return tuple(values[0] + values[1])

            empty = (jnp.zeros((PACK, LANES), BF16),) * 6
            flat = lax.fori_loop(HALO_LAYERS, last_layer + 1, more, empty)
            totals = apply_tile(tile, [flat[:3], flat[3:]])
            for c in range(3):
                rows = pl.ds(pl.multiple_of(tile * 8, 8), 8)
                partial[c, rows, :] = partial[c, rows, :] + totals[c]
            return carry

        lax.fori_loop(0, groups, one_tile, 0)

    remainder = []
    for e in range(3):
        total = partial[e, pl.ds(0, groups, stride=8), :]
        for row in range(1, 8):
            total = total + partial[e, pl.ds(row, groups, stride=8), :]
        remainder.append(residual[e] - smooth[e] - total)
    solved = dense_solve(dinv, remainder)
    for c in range(3):
        change = scale_old * update[c] + scale_new * solved[c]
        total = smooth[c] + change
        new_smooth[c] = total
        if stage < SWEEPS - 1:
            new_update[c] = change
            out_outer[c] = total.astype(BF16)
            out_inner[c] = total.astype(BF16)


def coarse_kernel(*refs, subs):
    (place, base, own_couple) = refs[:3]
    first, second, third = refs[3:5], refs[5:7], refs[7:9]
    far_after, far_before, aggregate, smooth = refs[9:13]
    out, field, links, kept = refs[13:]
    groups = base.shape[1]
    me = jnp.concatenate([place[...]] * (groups // 8), axis=0)
    even = (me & 1) == 0

    def valid(row):
        if row < 0:
            return jnp.where(me + row >= 0, 1.0, 0.0)
        return jnp.where(me + row < subs, 1.0, 0.0)

    def from_after(pair, start):
        return lambda i: jnp.where(
            even, pair[0][start + i].astype(F32), pair[1][start + i].astype(F32)
        )

    def from_before(pair, start):
        return from_after((pair[1], pair[0]), start)

    def plain(ref, start):
        return lambda i: ref[start + i].astype(F32)

    base_rows = {
        -4: plain(far_after, 0),
        -3: plain(far_after, 6),
        -2: from_after(third, 3),
        -1: from_after(second, 3),
        1: from_before(second, 3),
        2: from_before(third, 3),
        3: plain(far_before, 6),
        4: plain(far_before, 0),
    }
    link_rows = {
        -3: plain(far_after, 9),
        -2: from_after(second, 6),
        -1: from_after(first, 3),
        1: from_before(first, 3),
        2: from_before(second, 6),
        3: plain(far_before, 9),
    }
    for g in range(groups):
        for k in range(4):
            links[FAR - 1, k, g : g + 1, :] = own_couple[
                k : k + 1, g * LANES : (g + 1) * LANES
            ]
    for row, read in link_rows.items():
        for k in range(4):
            links[row + FAR - 1, k] = read(k) * valid(row)
    for k, mask in zip((2, 3), inside_masks(me.shape)):
        for row in range(2 * FAR - 1):
            links[row, k] = jnp.where(mask, links[row, k], 0.0)
    for c in range(3):
        field[0, FAR, c] = base[c]
        for row, read in base_rows.items():
            field[0, row + FAR, c] = read(c) * valid(row)
        field[1, 0, c] = far_after[3 + c].astype(F32) * valid(-FAR)
        field[1, 2 * FAR, c] = far_before[3 + c].astype(F32) * valid(FAR)
        for row in range(2 * FAR + 1):
            kept[row, c] = field[0, row, c]
    for step in range(STEPS):
        old, new = step % 2, (step + 1) % 2
        reach = min(STEPS - 1 - step, FAR - 1)
        for row in range(-reach, reach + 1):
            spot = row + FAR
            weights = [links[spot - 1, k] for k in range(4)]
            for c in range(3):
                right, left = sideways(field[old, spot, c])
                field[new, spot, c] = kept[spot, c] + (
                    weights[0] * field[old, spot - 1, c]
                    + weights[1] * field[old, spot + 1, c]
                    + weights[2] * right
                    + weights[3] * left
                )
    final = STEPS % 2
    agg = aggregate[...] & (groups * LANES - 1)
    for block in range(agg.shape[0] // 8):
        index = agg[block * 8 : (block + 1) * 8]
        low = index & (LANES - 1)
        high = index >> 7
        found = [jnp.zeros((8, LANES), F32)] * 3
        for g in range(groups):
            chosen = high == g
            for c in range(3):
                rows = jnp.broadcast_to(field[final, FAR, c, g : g + 1, :], (8, LANES))
                found[c] = jnp.where(chosen, lane_gather(rows, low), found[c])
        for c in range(3):
            result = smooth[c, block * 8 : (block + 1) * 8, :] + found[c]
            for r in range(8):
                lanes = slice((block * 8 + r) * LANES, (block * 8 + r + 1) * LANES)
                out[c : c + 1, lanes] = result[r : r + 1]


def shifted(value, steps):
    count = lax.axis_size("sub")
    return lax.ppermute(value, "sub", [(i, (i + steps) % count) for i in range(count)])


def across_chips(value):
    count = lax.axis_size("sub")
    pairs = [(i, (i + 1) % count) for i in range(1, count, 2)]
    return lax.ppermute(value, "sub", pairs + [(j, i) for i, j in pairs])


def within_chip(value):
    count = lax.axis_size("sub")
    pairs = [(i, i + 1) for i in range(0, count, 2)]
    return lax.ppermute(value, "sub", pairs + [(j, i) for i, j in pairs])


def exchanged_by_pairs(outer, inner):
    return across_chips(outer), within_chip(inner)


def local_pass(smooth, lists, first, tiles, us=None):
    unroll = max(n for n in range(1, 17) if tiles % n == 0)
    return call(
        functools.partial(local_kernel, first=first, tiles=tiles, unroll=unroll),
        jax.ShapeDtypeStruct((3, lists[0].shape[0], tiles * LANES), BF16),
        (smooth, *lists),
        us=us or 0.12 * tiles,
    )


def body(
    fine_residual, bonds, bond_col, ghost_points, fine_dinv, aggregate, coarse_dinv, coarse_couple
):
    points = fine_residual.shape[1]
    groups = points // LANES
    bonds_of = bond_col.shape[0]
    per_group = coarse_dinv.shape[2]
    coarse_groups = per_group // LANES
    assert per_group & (per_group - 1) == 0
    sub = lax.axis_index("sub")
    doms = lax.axis_size("dom")
    ghost = ghost_points.reshape(-1, LANES)
    agg = aggregate.reshape(groups, LANES)
    relaid = bonds.transpose(1, 2, 0, 3)
    sds = jax.ShapeDtypeStruct
    field = sds((3, groups, LANES), F32)
    coarse_field = sds((3, coarse_groups, LANES), F32)

    def message(rows):
        return sds((rows, groups, LANES), BF16)

    residual, rhs = call(
        restrict_kernel,
        (field, coarse_field),
        tuple(pltpu.with_memory_space_constraint(x, pltpu.HBM) for x in (fine_residual, agg)),
        scratch=[
            VMEM(fine_residual.shape, F32),
            VMEM(agg.shape, jnp.int32),
            pltpu.SemaphoreType.DMA((2,)),
        ],
        us=1.6,
        spaces={0: pltpu.HBM, 1: pltpu.HBM},
    )
    dinv, smooth, packed = call(
        first_kernel,
        (sds((3, 3, groups, LANES), F32), field, message(7)),
        (residual, fine_dinv, coarse_couple),
        us=0.8,
    )
    update = smooth
    own_packed = packed
    place = jnp.full((8, LANES), sub, jnp.int32)
    def exchanged(value, step):
        return lax.ppermute(value, "dom", [(i, i ^ step) for i in range(doms)])

    assert doms == 8
    arrived = exchanged(rhs, 1)
    later_col, rhs = lax.optimization_barrier((bond_col, rhs))

    def shorts(rows):
        return sds((rows, points), jnp.int16)

    picks, start, halo_start, spot, rank, most, columns, halo_columns = call(
        prepare_kernel,
        (
            shorts(bonds_of),
            shorts(PACK),
            shorts(PACK),
            shorts(bonds_of),
            shorts(bonds_of),
            sds((groups + 16, LANES), jnp.int32),
            shorts(LAYERS * PACK),
            shorts(HALO_LAYERS * PACK),
        ),
        (later_col,),
        scratch=[VMEM((8 * (bonds_of + 2), LANES), jnp.int32)],
        us=2.5,
    )
    start, rhs = lax.optimization_barrier((start, rhs))
    rhs = rhs + arrived
    packed, start, rhs = lax.optimization_barrier((packed, start, rhs))
    arrived = exchanged(rhs, 2)
    first_outer = across_chips(packed)
    early = local_pass(smooth, (picks, start, spot, rank, most, columns), 0, 8)
    rhs, early = lax.optimization_barrier((rhs, early))
    rhs = rhs + arrived
    packed_inner, start, rhs = lax.optimization_barrier((packed, start, rhs))
    arrived = exchanged(rhs, 6)
    first = arrived_sides = (first_outer, within_chip(packed_inner))

    factor = HALF / CENTER
    for stage in range(SWEEPS):
        factor_new = 1.0 / (2.0 * CENTER / HALF - factor)
        lists = (picks, start, spot, rank, most, columns)
        if stage == 0:
            sizes = (8, groups - 8)
            found = [early, local_pass(smooth, lists, *sizes)]
        elif stage == 1:
            sizes = (groups,)
            found = [local_pass(smooth, lists, 0, groups)]
        else:
            sizes = (groups // 2,) * 2
            found = [local_pass(smooth, lists, 0, sizes[0], us=0.2)]
            far_next, far_prev, start, found[0] = lax.optimization_barrier(
                (far_next, far_prev, start, found[0])
            )
            far_after = shifted(far_next, 4)
            far_before = shifted(far_prev, -4)
            lists = (picks, start, spot, rank, most, columns)
            found.append(local_pass(smooth, lists, *sizes, us=0.2))
        inputs = [place, most, picks, halo_start, halo_columns, spot, rank, ghost]
        inputs += arrived_sides
        inputs += [residual, dinv, smooth, update, relaid, *found]
        if stage == 0:
            inputs += [rhs, arrived, coarse_dinv]
            outs = (field, field, coarse_field, message(10), message(10))
        elif stage == 1:
            inputs += [*first, base, own_packed]
            outs = (field, field, message(6), message(6), message(13), message(13))
        else:
            outs = (field,)
        result = call(
            functools.partial(
                halo_kernel,
                stage=stage,
                sizes=sizes,
                scale_old=factor_new * factor,
                scale_new=2.0 * factor_new / HALF,
                subs=lax.axis_size("sub"),
            ),
            outs,
            inputs,
            scratch=[VMEM((3, groups, LANES), F32)] * 2 + [VMEM((3, 8 * groups, LANES), F32)],
            us=2.5,
        )
        factor = factor_new
        if stage == 0:
            smooth, update, base, outer, inner = result
            second = arrived_sides = exchanged_by_pairs(outer, inner)
        elif stage == 1:
            smooth, update, outer, inner, far_next, far_prev = result
            third = arrived_sides = exchanged_by_pairs(outer, inner)
        else:
            (smooth,) = result
    return call(
        functools.partial(coarse_kernel, subs=lax.axis_size("sub")),
        sds((3, points), F32),
        (
            place,
            base,
            coarse_couple,
            *first,
            *second,
            *third,
            far_after,
            far_before,
            agg,
            smooth,
        ),
        scratch=[
            VMEM((2, 2 * FAR + 1, 3, coarse_groups, LANES), F32),
            VMEM((2 * FAR - 1, 4, coarse_groups, LANES), F32),
            VMEM((2 * FAR + 1, 3, coarse_groups, LANES), F32),
        ],
        us=2.0,
    )


def solution(mesh):
    placed = (
        P(None, ("dom", "sub")),
        P(None, None, None, ("dom", "sub")),
        P(None, ("dom", "sub")),
        P(("dom", "sub"), None, None),
        P(None, None, ("dom", "sub")),
        P(("dom", "sub")),
        P(None, None, "sub"),
        P(None, "sub"),
    )
    return jax.shard_map(
        body, mesh=mesh, in_specs=placed, out_specs=P(None, ("dom", "sub")), check_vma=False
    )
```

```python
import functools

import jax
import jax.numpy as jnp
from jax import lax
from jax.experimental import pallas as pl
from jax.experimental.pallas import tpu as pltpu
from jax.sharding import PartitionSpec as P

SWEEPS = 3
STEPS = 5
FAR = 4
LOW_EIG = 0.3
HIGH_EIG = 2.2
CENTER = (HIGH_EIG + LOW_EIG) / 2.0
HALF = (HIGH_EIG - LOW_EIG) / 2.0
LANES = 128
PACK = 16
LAYERS = 10
FIRST_HALF_LAYERS = 8
HALO_LAYERS = 3
F32 = jnp.float32
BF16 = jnp.bfloat16
VMEM = pltpu.VMEM


def gather(rows, index, axis):
    numbers = lax.GatherDimensionNumbers(
        offset_dims=(),
        collapsed_slice_dims=(axis,),
        start_index_map=(axis,),
        operand_batching_dims=(1 - axis,),
        start_indices_batching_dims=(1 - axis,),
    )
    return lax.gather(
        rows,
        index[..., None],
        numbers,
        (1, 1),
        mode=lax.GatherScatterMode.PROMISE_IN_BOUNDS,
    )


def lane_gather(rows, index):
    return gather(rows, index, 1)


def row_gather(rows, index):
    return gather(rows, index, 0)


def sorting_network(count):
    pairs = []
    span = 1
    while span < count:
        gap = span
        while gap >= 1:
            for j in range(gap % span, count - gap, 2 * gap):
                for i in range(min(gap, count - j - gap)):
                    if (i + j) // (2 * span) == (i + j + gap) // (2 * span):
                        pairs.append((i + j, i + j + gap))
            gap //= 2
        span *= 2
    return pairs


def sort_planes(planes):
    planes = list(planes)
    for i, j in sorting_network(len(planes)):
        planes[i], planes[j] = (
            jnp.minimum(planes[i], planes[j]),
            jnp.maximum(planes[i], planes[j]),
        )
    return planes


def call(kernel, out, inputs, scratch=(), us=1.0, spaces={}, limit=16):
    return pl.pallas_call(
        kernel,
        out_shape=out,
        in_specs=[
            pl.BlockSpec(memory_space=spaces.get(i, VMEM)) for i in range(len(inputs))
        ],
        out_specs=jax.tree.map(
            lambda _: pl.BlockSpec(memory_space=VMEM), out
        ),
        scratch_shapes=list(scratch),
        cost_estimate=pl.CostEstimate(
            flops=int(us * 1.0e9), transcendentals=0, bytes_accessed=int(us * 1.0e6)
        ),
        compiler_params=pltpu.CompilerParams(vmem_limit_bytes=limit * 1024 * 1024),
    )(*inputs)


def rows_of(ref, lead, group):
    return ref[lead + (slice(group * LANES, (group + 1) * LANES),)]


def restrict_kernel(*refs):
    sources = refs[:2]
    dense_residual, rhs = refs[2:4]
    residual, aggregate, semaphores = refs[4:]
    copies = [
        pltpu.make_async_copy(source, target, semaphores.at[i])
        for i, (source, target) in enumerate(zip(sources, (residual, aggregate)))
    ]
    for copy in copies:
        copy.start()
    copies[0].wait()
    for g in range(dense_residual.shape[1]):
        for e in range(3):
            dense_residual[e, g : g + 1, :] = residual[
                e : e + 1, g * LANES : (g + 1) * LANES
            ]
    copies[1].wait()
    restrict(dense_residual, aggregate, rhs)


def first_kernel(dense_residual, dinv, couple, dense_dinv, smooth, message):
    groups = smooth.shape[1]
    coarse_groups = message.shape[1]
    for g in range(groups):
        lanes = slice(g * LANES, (g + 1) * LANES)
        for e in range(3):
            for c in range(3):
                dense_dinv[c, e, g : g + 1, :] = dinv[c, e : e + 1, lanes]
    for g in range(coarse_groups):
        lanes = slice(g * LANES, (g + 1) * LANES)
        for k in range(4):
            message[3 + k, g : g + 1, :] = couple[k : k + 1, lanes].astype(BF16)
    for c in range(3):
        total = dense_dinv[c, 0] * dense_residual[0]
        for e in range(1, 3):
            total = total + dense_dinv[c, e] * dense_residual[e]
        total = total * (1.0 / CENTER)
        smooth[c] = total
        message[c] = total.astype(BF16)


def restrict(residual, aggregate, out):
    groups = residual.shape[1]
    bins = out.shape[1]
    agg = aggregate[...] & (bins * LANES - 1)
    low = agg & (LANES - 1)
    high = agg >> 7
    batch = 8
    row16 = lax.broadcasted_iota(jnp.int32, (PACK, LANES), 0).astype(jnp.int16)
    one, zero = jnp.ones((PACK, LANES), BF16), jnp.zeros((PACK, LANES), BF16)

    def wide(row, kind):
        return jnp.broadcast_to(row, (PACK, LANES)).astype(kind)

    total = jnp.zeros((6 * bins, LANES), F32)
    for block in range(groups // batch):
        onehot, spread = [], []
        for g in range(block * batch, (block + 1) * batch):
            lane = wide(low[g : g + 1], jnp.int16)
            line = wide(high[g : g + 1], jnp.int16)
            onehot.append(
                jnp.concatenate(
                    [
                        jnp.where(lane == row16 + jnp.int16(first), one, zero)
                        for first in range(0, LANES, PACK)
                    ],
                    axis=0,
                )
            )
            chosen = [line == row16 + jnp.int16(first) for first in range(0, bins, PACK)]
            column = []
            for c in range(3):
                value = residual[c, g : g + 1, :]
                upper = value.astype(BF16).astype(F32)
                for part in (upper, value - upper):
                    part = wide(part, BF16)
                    column += [jnp.where(mask, part, zero) for mask in chosen]
            spread.append(jnp.concatenate(column, axis=0))
        total = total + lax.dot_general(
            jnp.concatenate(spread, axis=1),
            jnp.concatenate(onehot, axis=1),
            (((1,), (1,)), ((), ())),
            preferred_element_type=F32,
        )
    for c in range(3):
        first = 2 * c * bins
        out[c] = total[first : first + bins] + total[first + bins : first + 2 * bins]


def spread_max(values):
    top = jnp.max(jnp.max(values, axis=1, keepdims=True), axis=0, keepdims=True)
    return jnp.broadcast_to(top, values.shape)


def prepare_kernel(
    col, picks, start, halo_start, spot, rank, most, columns, halo_columns, flip
):
    bonds_of = col.shape[0]
    groups = col.shape[1] // LANES
    stride = bonds_of + 1

    def eight_tiles(block, carry):
        best, halo_best = carry

        def lanes_of(t):
            return pl.ds(pl.multiple_of((block * 8 + t) * LANES, LANES), LANES)

        for t in range(8):
            flip[pl.ds(t * stride, bonds_of), :] = col[:, lanes_of(t)]
        keys = []
        for k in range(bonds_of):
            c = flip[pl.ds(k, 8, stride=stride), :]
            keys.append(((c >> 8) << 13) | (k << 8) | (c & 255))
        keys = sort_planes(keys)
        pairs = [key >> 13 for key in keys]
        ranks = [jnp.zeros((8, LANES), jnp.int32)]
        for k in range(1, bonds_of):
            ranks.append(jnp.where(pairs[k] == pairs[k - 1], ranks[k - 1] + 1, 0))
        back = []
        here = jnp.zeros((8, LANES), jnp.int32)
        for k in range(bonds_of):
            local = pairs[k] < PACK
            early = ((keys[k] >> 8) & 31) < PACK
            depth = ranks[k] + jnp.where(early, LAYERS - FIRST_HALF_LAYERS, 0)
            here = jnp.maximum(here, jnp.where(local, depth, 0))
            halo_best = jnp.maximum(halo_best, jnp.where(local, 0, ranks[k]))
            code = jnp.where(
                local,
                (ranks[k] << 4) | pairs[k],
                ((ranks[k] >> 2) << 4) | ((ranks[k] & 3) << 2) | ((pairs[k] - PACK) + (32 << 4)),
            )
            back.append((((keys[k] >> 8) & 31) << 10) | code)
            flip[pl.ds(k, 8, stride=stride), :] = keys[k]
        row = lax.broadcasted_iota(jnp.int32, (PACK, LANES), 0)
        for t in range(8):
            halves = [flip[pl.ds(t * stride + h * PACK, PACK), :] for h in range(2)]
            for h in range(2):
                picks[h * PACK : (h + 1) * PACK, lanes_of(t)] = (halves[h] & 255).astype(jnp.int16)
            first, second = [(x >> 13).astype(jnp.int16) for x in halves]
            for target, pair, extra in (
                (start, row.astype(jnp.int16), None),
                (halo_start, (PACK + (row & 3)).astype(jnp.int16), (row >> 2).astype(jnp.int16)),
            ):
                place = jnp.zeros((PACK, LANES), jnp.int16)
                for step in (16, 8, 4, 2, 1, 1):
                    probe = place + jnp.int16(step - 1)
                    inner = probe & jnp.int16(PACK - 1)
                    value = jnp.where(
                        probe < PACK, row_gather(first, inner), row_gather(second, inner)
                    )
                    place = jnp.where(value < pair, place + jnp.int16(step), place)
                place = place if extra is None else place + extra
                target[:, lanes_of(t)] = place
                chosen = [(x & 255).astype(jnp.int16) for x in halves]
                if extra is None:
                    for m in range(LAYERS):
                        columns[m * PACK : (m + 1) * PACK, lanes_of(t)] = picked(
                            place + jnp.int16(m), chosen
                        )
                else:
                    for v in range(HALO_LAYERS):
                        halo_columns[v * PACK : (v + 1) * PACK, lanes_of(t)] = picked(
                            place + jnp.int16(4 * v), chosen
                        )
        back = sort_planes(back)
        for k in range(bonds_of):
            flip[pl.ds(k, 8, stride=stride), :] = back[k] & 1023
        for t in range(8):
            for h in range(2):
                code = flip[pl.ds(t * stride + h * PACK, PACK), :]
                rows = slice(h * PACK, (h + 1) * PACK)
                spot[rows, lanes_of(t)] = (code & 15).astype(jnp.int16)
                rank[rows, lanes_of(t)] = (code >> 4).astype(jnp.int16)
        most[pl.ds(pl.multiple_of(block * 8, 8), 8), :] = spread_max(here)
        return jnp.maximum(best, here), halo_best

    zero = jnp.zeros((8, LANES), jnp.int32)
    best, halo_best = lax.fori_loop(0, groups // 8, eight_tiles, (zero, zero))
    most[groups : groups + 8, :] = spread_max(best)
    most[groups + 8 :, :] = spread_max(halo_best) >> 2


def picked(place, picks):
    inner = place & jnp.int16(PACK - 1)
    return jnp.where(place < PACK, row_gather(picks[0], inner), row_gather(picks[1], inner))


def layer(column, even, odd):
    lane = column & jnp.int16(LANES - 1)
    second = column >= LANES
    return [
        jnp.where(second, lane_gather(odd[e], lane), lane_gather(even[e], lane))
        for e in range(3)
    ]


def put_back(values, number, spots, ranks, out, halves=(0, 1)):
    for h in halves:
        hit = ranks[h] == number
        for e in range(3):
            out[h][e] = jnp.where(hit, row_gather(values[e], spots[h]), out[h][e])


def halves_of(ref, lanes):
    return [ref[h * PACK : (h + 1) * PACK, lanes] for h in range(2)]


def splat(number):
    return jnp.full((PACK, LANES), number, jnp.int32).astype(jnp.int16)


def local_kernel(
    smooth, picks, start, spot, rank, most, columns, out, *, first, tiles, unroll
):
    even = [smooth[e, pl.ds(0, PACK, stride=2), :].astype(BF16) for e in range(3)]
    odd = [smooth[e, pl.ds(1, PACK, stride=2), :].astype(BF16) for e in range(3)]

    def some_tiles(t, carry):
        for u in range(unroll):
            source = pl.ds(pl.multiple_of((first + t * unroll + u) * LANES, LANES), LANES)
            target = pl.ds(pl.multiple_of((t * unroll + u) * LANES, LANES), LANES)
            spots, ranks = halves_of(spot, source), halves_of(rank, source)
            found = [[jnp.zeros((PACK, LANES), BF16)] * 3 for h in range(2)]
            for m in range(LAYERS):
                values = layer(columns[m * PACK : (m + 1) * PACK, source], even, odd)
                halves = (0, 1) if m < FIRST_HALF_LAYERS else (1,)
                put_back(values, jnp.int16(m), spots, ranks, found, halves)
            for h in range(2):
                for e in range(3):
                    out[e, h * PACK : (h + 1) * PACK, target] = found[h][e]
        return carry

    lax.fori_loop(0, tiles // unroll, some_tiles, 0)

    @pl.when(most[smooth.shape[1], 0] >= LAYERS)
    def _():
        def eight_tiles(block, carry):
            def more(m, inner):
                number = splat(m)
                for t in range(8):
                    tile = block * 8 + t
                    source = pl.ds(pl.multiple_of((first + tile) * LANES, LANES), LANES)
                    target = pl.ds(pl.multiple_of(tile * LANES, LANES), LANES)
                    found = [
                        [out[e, h * PACK : (h + 1) * PACK, target] for e in range(3)]
                        for h in range(2)
                    ]
                    column = picked(start[:, source] + number, halves_of(picks, source))
                    values = layer(column, even, odd)
                    put_back(
                        values, number, halves_of(spot, source), halves_of(rank, source), found
                    )
                    for h in range(2):
                        for e in range(3):
                            out[e, h * PACK : (h + 1) * PACK, target] = found[h][e]
                return inner

            deepest = most[first + block * 8, 0]
            begin = jnp.where(deepest >= LAYERS, FIRST_HALF_LAYERS, deepest + 1)
            lax.fori_loop(begin, deepest + 1, more, 0)
            return carry

        lax.fori_loop(0, tiles // 8, eight_tiles, 0)


def dense_solve(matrix, vector):
    solved = []
    for c in range(3):
        total = matrix[c, 0] * vector[0]
        for e in range(1, 3):
            total = total + matrix[c, e] * vector[e]
        solved.append(total)
    return solved


def sideways(x):
    lines = x.shape[0]
    lane = lax.broadcasted_iota(jnp.int32, x.shape, 1)
    right = pltpu.roll(x, 1, 1)
    right = jnp.where(lane == 0, pltpu.roll(right, 1, 0), right)
    left = pltpu.roll(x, LANES - 1, 1)
    left = jnp.where(lane == LANES - 1, pltpu.roll(left, lines - 1, 0), left)
    return right, left


def inside_masks(shape):
    lane = lax.broadcasted_iota(jnp.int32, shape, 1)
    line = lax.broadcasted_iota(jnp.int32, shape, 0)
    return (
        jnp.logical_or(lane > 0, line > 0),
        jnp.logical_or(lane < LANES - 1, line < shape[0] - 1),
    )


def halo_kernel(*refs, stage, sizes, scale_old, scale_new, subs, unroll=8):
    (place, most, picks, halo_start, halo_columns, spot, rank, ghost) = refs[:8]
    (outer, inner, residual, dinv, smooth, update, bonds) = refs[8:15]
    pieces = len(sizes)
    local_found = refs[15 : 15 + pieces]
    refs = refs[15 + pieces :]
    if stage == 0:
        rhs, arrived, coarse_dinv = refs[:3]
        new_smooth, new_update, base, out_outer, out_inner = refs[3:8]
        refs = refs[8:]
    elif stage == 1:
        first_outer, first_inner, base, couple_own = refs[:4]
        new_smooth, new_update, out_outer, out_inner, far_next, far_prev = refs[4:10]
        refs = refs[10:]
    else:
        (new_smooth,) = refs[:1]
        refs = refs[1:]
    applied, other, partial = refs
    groups = smooth.shape[1]
    if stage == 0:
        vector = [rhs[e] + arrived[e] for e in range(3)]
        coarse_groups = base.shape[1]
        for c in range(3):
            for g in range(coarse_groups):
                lanes = slice(g * LANES, (g + 1) * LANES)
                total = coarse_dinv[c, 0:1, lanes] * vector[0][g : g + 1]
                for e in range(1, 3):
                    total = total + coarse_dinv[c, e : e + 1, lanes] * vector[e][g : g + 1]
                base[c, g : g + 1, :] = total
        for c in range(3):
            row = base[c].astype(BF16)
            out_outer[3 + c] = row
            out_inner[3 + c] = row
        out_outer[6:10] = inner[3:7]
        out_inner[6:10] = outer[3:7]
    elif stage == 1:
        out_outer[3:6] = inner[3:6]
        out_inner[3:6] = outer[3:6]
        me = jnp.concatenate([place[...]] * (base.shape[1] // 8), axis=0)
        even = (me & 1) == 0
        links = [couple_own[3 + k].astype(F32) for k in range(4)]
        links[0] = jnp.where(me > 0, links[0], 0.0)
        links[1] = jnp.where(me < subs - 1, links[1], 0.0)
        for k, mask in zip((2, 3), inside_masks(me.shape)):
            links[k] = jnp.where(mask, links[k], 0.0)
        for c in range(3):
            own = base[c]
            outer_row, inner_row = outer[3 + c].astype(F32), inner[3 + c].astype(F32)
            below = jnp.where(even, outer_row, inner_row)
            above = jnp.where(even, inner_row, outer_row)
            right, left = sideways(own)
            iterate = own + (
                links[0] * below + links[1] * above + links[2] * right + links[3] * left
            )
            for message, beyond in ((far_next, above), (far_prev, below)):
                message[c] = own.astype(BF16)
                message[3 + c] = iterate.astype(BF16)
                message[6 + c] = beyond.astype(BF16)
        for k in range(4):
            outer_row = first_outer[3 + k].astype(F32)
            inner_row = first_inner[3 + k].astype(F32)
            far_next[9 + k] = jnp.where(even, inner_row, outer_row).astype(BF16)
            far_prev[9 + k] = jnp.where(even, outer_row, inner_row).astype(BF16)
    wanted = ghost[...]
    half = wanted.shape[0] // 2
    low = wanted & (LANES - 1)
    high = wanted >> 7
    upper = jnp.where(lax.broadcasted_iota(jnp.int32, wanted.shape, 0) < half, 1, 0)
    from_outer = (upper ^ (place[...] & 1)) == 1
    found = [jnp.zeros(wanted.shape, F32)] * 3
    for e in range(3):
        applied[e] = outer[e].astype(F32)
        other[e] = inner[e].astype(F32)
    for g in range(groups):
        chosen = high == g
        for e in range(3):
            rows = jnp.where(
                from_outer,
                jnp.broadcast_to(applied[e, g : g + 1, :], wanted.shape),
                jnp.broadcast_to(other[e, g : g + 1, :], wanted.shape),
            )
            found[e] = jnp.where(chosen, lane_gather(rows, low), found[e])
    pair = (lax.broadcasted_iota(jnp.int32, wanted.shape, 0) & 3) * 2

    def four_times(rows):
        return jnp.concatenate([rows, rows], axis=0).astype(BF16)

    even = [four_times(row_gather(found[e], pair)) for e in range(3)]
    odd = [four_times(row_gather(found[e], pair + 1)) for e in range(3)]

    def apply_tile(tile, values):
        here = pl.ds(pl.multiple_of(tile * LANES, LANES), LANES)
        totals = []
        for c in range(3):
            total = jnp.zeros((PACK, LANES), F32)
            for h in range(2):
                for e in range(3):
                    block = bonds[c, e, h * PACK : (h + 1) * PACK, here].astype(F32)
                    total = total + block * values[h][e].astype(F32)
            totals.append(total[:8] + total[8:])
        return totals

    for piece, part in enumerate(local_found):
        first = sum(sizes[:piece])

        def some_tiles(t, carry, part=part, first=first):
            for u in range(unroll):
                there = pl.ds(pl.multiple_of((t * unroll + u) * LANES, LANES), LANES)
                tile = first + t * unroll + u
                here = pl.ds(pl.multiple_of(tile * LANES, LANES), LANES)
                spots, ranks = halves_of(spot, here), halves_of(rank, here)
                values = [
                    [part[e, h * PACK : (h + 1) * PACK, there] for e in range(3)]
                    for h in range(2)
                ]
                for v in range(HALO_LAYERS):
                    row = layer(halo_columns[v * PACK : (v + 1) * PACK, here], even, odd)
                    put_back(row, jnp.int16(32 + v), spots, ranks, values)
                totals = apply_tile(tile, values)
                for c in range(3):
                    partial[c, pl.ds(pl.multiple_of(tile * 8, 8), 8), :] = totals[c]
            return carry

        lax.fori_loop(0, sizes[piece] // unroll, some_tiles, 0)

    last_layer = most[groups + 8, 0]

    @pl.when(last_layer >= HALO_LAYERS)
    def _():
        def one_tile(tile, carry):
            here = pl.ds(pl.multiple_of(tile * LANES, LANES), LANES)

            def more(v, flat):
                values = [list(flat[:3]), list(flat[3:])]
                column = picked(halo_start[:, here] + splat(4 * v), halves_of(picks, here))
                row = layer(column, even, odd)
                put_back(row, splat(32 + v), halves_of(spot, here), halves_of(rank, here), values)
                return tuple(values[0] + values[1])

            empty = (jnp.zeros((PACK, LANES), BF16),) * 6
            flat = lax.fori_loop(HALO_LAYERS, last_layer + 1, more, empty)
            totals = apply_tile(tile, [flat[:3], flat[3:]])
            for c in range(3):
                rows = pl.ds(pl.multiple_of(tile * 8, 8), 8)
                partial[c, rows, :] = partial[c, rows, :] + totals[c]
            return carry

        lax.fori_loop(0, groups, one_tile, 0)

    remainder = []
    for e in range(3):
        total = partial[e, pl.ds(0, groups, stride=8), :]
        for row in range(1, 8):
            total = total + partial[e, pl.ds(row, groups, stride=8), :]
        remainder.append(residual[e] - smooth[e] - total)
    solved = dense_solve(dinv, remainder)
    for c in range(3):
        change = scale_old * update[c] + scale_new * solved[c]
        total = smooth[c] + change
        new_smooth[c] = total
        if stage < SWEEPS - 1:
            new_update[c] = change
            out_outer[c] = total.astype(BF16)
            out_inner[c] = total.astype(BF16)


def coarse_kernel(*refs, subs):
    (place, base, own_couple) = refs[:3]
    first, second, third = refs[3:5], refs[5:7], refs[7:9]
    far_after, far_before, aggregate, smooth = refs[9:13]
    out, field, links, kept = refs[13:]
    groups = base.shape[1]
    me = jnp.concatenate([place[...]] * (groups // 8), axis=0)
    even = (me & 1) == 0

    def valid(row):
        if row < 0:
            return jnp.where(me + row >= 0, 1.0, 0.0)
        return jnp.where(me + row < subs, 1.0, 0.0)

    def from_after(pair, start):
        return lambda i: jnp.where(
            even, pair[0][start + i].astype(F32), pair[1][start + i].astype(F32)
        )

    def from_before(pair, start):
        return from_after((pair[1], pair[0]), start)

    def plain(ref, start):
        return lambda i: ref[start + i].astype(F32)

    base_rows = {
        -4: plain(far_after, 0),
        -3: plain(far_after, 6),
        -2: from_after(third, 3),
        -1: from_after(second, 3),
        1: from_before(second, 3),
        2: from_before(third, 3),
        3: plain(far_before, 6),
        4: plain(far_before, 0),
    }
    link_rows = {
        -3: plain(far_after, 9),
        -2: from_after(second, 6),
        -1: from_after(first, 3),
        1: from_before(first, 3),
        2: from_before(second, 6),
        3: plain(far_before, 9),
    }
    for g in range(groups):
        for k in range(4):
            links[FAR - 1, k, g : g + 1, :] = own_couple[
                k : k + 1, g * LANES : (g + 1) * LANES
            ]
    for row, read in link_rows.items():
        for k in range(4):
            links[row + FAR - 1, k] = read(k) * valid(row)
    for k, mask in zip((2, 3), inside_masks(me.shape)):
        for row in range(2 * FAR - 1):
            links[row, k] = jnp.where(mask, links[row, k], 0.0)
    for c in range(3):
        field[0, FAR, c] = base[c]
        for row, read in base_rows.items():
            field[0, row + FAR, c] = read(c) * valid(row)
        field[1, 0, c] = far_after[3 + c].astype(F32) * valid(-FAR)
        field[1, 2 * FAR, c] = far_before[3 + c].astype(F32) * valid(FAR)
        for row in range(2 * FAR + 1):
            kept[row, c] = field[0, row, c]
    for step in range(STEPS):
        old, new = step % 2, (step + 1) % 2
        reach = min(STEPS - 1 - step, FAR - 1)
        for row in range(-reach, reach + 1):
            spot = row + FAR
            weights = [links[spot - 1, k] for k in range(4)]
            for c in range(3):
                right, left = sideways(field[old, spot, c])
                field[new, spot, c] = kept[spot, c] + (
                    weights[0] * field[old, spot - 1, c]
                    + weights[1] * field[old, spot + 1, c]
                    + weights[2] * right
                    + weights[3] * left
                )
    final = STEPS % 2
    agg = aggregate[...] & (groups * LANES - 1)
    for block in range(agg.shape[0] // 8):
        index = agg[block * 8 : (block + 1) * 8]
        low = index & (LANES - 1)
        high = index >> 7
        found = [jnp.zeros((8, LANES), F32)] * 3
        for g in range(groups):
            chosen = high == g
            for c in range(3):
                rows = jnp.broadcast_to(field[final, FAR, c, g : g + 1, :], (8, LANES))
                found[c] = jnp.where(chosen, lane_gather(rows, low), found[c])
        for c in range(3):
            result = smooth[c, block * 8 : (block + 1) * 8, :] + found[c]
            for r in range(8):
                lanes = slice((block * 8 + r) * LANES, (block * 8 + r + 1) * LANES)
                out[c : c + 1, lanes] = result[r : r + 1]


def shifted(value, steps):
    count = lax.axis_size("sub")
    return lax.ppermute(value, "sub", [(i, (i + steps) % count) for i in range(count)])


def across_chips(value):
    count = lax.axis_size("sub")
    pairs = [(i, (i + 1) % count) for i in range(1, count, 2)]
    return lax.ppermute(value, "sub", pairs + [(j, i) for i, j in pairs])


def within_chip(value):
    count = lax.axis_size("sub")
    pairs = [(i, i + 1) for i in range(0, count, 2)]
    return lax.ppermute(value, "sub", pairs + [(j, i) for i, j in pairs])


def exchanged_by_pairs(outer, inner):
    return across_chips(outer), within_chip(inner)


def local_pass(smooth, lists, first, tiles, us=None):
    unroll = max(n for n in range(1, 17) if tiles % n == 0)
    return call(
        functools.partial(local_kernel, first=first, tiles=tiles, unroll=unroll),
        jax.ShapeDtypeStruct((3, lists[0].shape[0], tiles * LANES), BF16),
        (smooth, *lists),
        us=us or 0.12 * tiles,
    )


def body(
    fine_residual, bonds, bond_col, ghost_points, fine_dinv, aggregate, coarse_dinv, coarse_couple
):
    points = fine_residual.shape[1]
    groups = points // LANES
    bonds_of = bond_col.shape[0]
    per_group = coarse_dinv.shape[2]
    coarse_groups = per_group // LANES
    assert per_group & (per_group - 1) == 0
    sub = lax.axis_index("sub")
    doms = lax.axis_size("dom")
    ghost = ghost_points.reshape(-1, LANES)
    agg = aggregate.reshape(groups, LANES)
    relaid = bonds.transpose(1, 2, 0, 3)
    sds = jax.ShapeDtypeStruct
    field = sds((3, groups, LANES), F32)
    coarse_field = sds((3, coarse_groups, LANES), F32)

    def message(rows):
        return sds((rows, groups, LANES), BF16)

    residual, rhs = call(
        restrict_kernel,
        (field, coarse_field),
        tuple(pltpu.with_memory_space_constraint(x, pltpu.HBM) for x in (fine_residual, agg)),
        scratch=[
            VMEM(fine_residual.shape, F32),
            VMEM(agg.shape, jnp.int32),
            pltpu.SemaphoreType.DMA((2,)),
        ],
        us=1.6,
        spaces={0: pltpu.HBM, 1: pltpu.HBM},
    )
    dinv, smooth, packed = call(
        first_kernel,
        (sds((3, 3, groups, LANES), F32), field, message(7)),
        (residual, fine_dinv, coarse_couple),
        us=0.8,
    )
    update = smooth
    own_packed = packed
    place = jnp.full((8, LANES), sub, jnp.int32)
    def exchanged(value, step):
        return lax.ppermute(value, "dom", [(i, i ^ step) for i in range(doms)])

    assert doms == 8
    arrived = exchanged(rhs, 1)
    later_col, rhs = lax.optimization_barrier((bond_col, rhs))

    def shorts(rows):
        return sds((rows, points), jnp.int16)

    picks, start, halo_start, spot, rank, most, columns, halo_columns = call(
        prepare_kernel,
        (
            shorts(bonds_of),
            shorts(PACK),
            shorts(PACK),
            shorts(bonds_of),
            shorts(bonds_of),
            sds((groups + 16, LANES), jnp.int32),
            shorts(LAYERS * PACK),
            shorts(HALO_LAYERS * PACK),
        ),
        (later_col,),
        scratch=[VMEM((8 * (bonds_of + 2), LANES), jnp.int32)],
        us=2.5,
    )
    start, rhs = lax.optimization_barrier((start, rhs))
    rhs = rhs + arrived
    packed, start, rhs = lax.optimization_barrier((packed, start, rhs))
    arrived = exchanged(rhs, 2)
    first_outer = across_chips(packed)
    early = local_pass(smooth, (picks, start, spot, rank, most, columns), 0, 8)
    rhs, early = lax.optimization_barrier((rhs, early))
    rhs = rhs + arrived
    packed_inner, start, rhs = lax.optimization_barrier((packed, start, rhs))
    arrived = exchanged(rhs, 6)
    first = arrived_sides = (first_outer, within_chip(packed_inner))

    factor = HALF / CENTER
    for stage in range(SWEEPS):
        factor_new = 1.0 / (2.0 * CENTER / HALF - factor)
        lists = (picks, start, spot, rank, most, columns)
        if stage == 0:
            sizes = (8, groups - 8)
            found = [early, local_pass(smooth, lists, *sizes)]
        elif stage == 1:
            sizes = (groups,)
            found = [local_pass(smooth, lists, 0, groups)]
        else:
            sizes = (groups // 2,) * 2
            found = [local_pass(smooth, lists, 0, sizes[0], us=0.2)]
            far_next, far_prev, start, found[0] = lax.optimization_barrier(
                (far_next, far_prev, start, found[0])
            )
            far_after = shifted(far_next, 4)
            far_before = shifted(far_prev, -4)
            lists = (picks, start, spot, rank, most, columns)
            found.append(local_pass(smooth, lists, *sizes, us=0.2))
        inputs = [place, most, picks, halo_start, halo_columns, spot, rank, ghost]
        inputs += arrived_sides
        inputs += [residual, dinv, smooth, update, relaid, *found]
        if stage == 0:
            inputs += [rhs, arrived, coarse_dinv]
            outs = (field, field, coarse_field, message(10), message(10))
        elif stage == 1:
            inputs += [*first, base, own_packed]
            outs = (field, field, message(6), message(6), message(13), message(13))
        else:
            outs = (field,)
        result = call(
            functools.partial(
                halo_kernel,
                stage=stage,
                sizes=sizes,
                scale_old=factor_new * factor,
                scale_new=2.0 * factor_new / HALF,
                subs=lax.axis_size("sub"),
            ),
            outs,
            inputs,
            scratch=[VMEM((3, groups, LANES), F32)] * 2 + [VMEM((3, 8 * groups, LANES), F32)],
            us=2.5,
        )
        factor = factor_new
        if stage == 0:
            smooth, update, base, outer, inner = result
            second = arrived_sides = exchanged_by_pairs(outer, inner)
        elif stage == 1:
            smooth, update, outer, inner, far_next, far_prev = result
            third = arrived_sides = exchanged_by_pairs(outer, inner)
        else:
            (smooth,) = result
    return call(
        functools.partial(coarse_kernel, subs=lax.axis_size("sub")),
        sds((3, points), F32),
        (
            place,
            base,
            coarse_couple,
            *first,
            *second,
            *third,
            far_after,
            far_before,
            agg,
            smooth,
        ),
        scratch=[
            VMEM((2, 2 * FAR + 1, 3, coarse_groups, LANES), F32),
            VMEM((2 * FAR - 1, 4, coarse_groups, LANES), F32),
            VMEM((2 * FAR + 1, 3, coarse_groups, LANES), F32),
        ],
        us=2.0,
    )


def solution(mesh):
    placed = (
        P(None, ("dom", "sub")),
        P(None, None, None, ("dom", "sub")),
        P(None, ("dom", "sub")),
        P(("dom", "sub"), None, None),
        P(None, None, ("dom", "sub")),
        P(("dom", "sub")),
        P(None, None, "sub"),
        P(None, "sub"),
    )
    return jax.shard_map(
        body, mesh=mesh, in_specs=placed, out_specs=P(None, ("dom", "sub")), check_vma=False
    )
```

```python
import functools

import jax
import jax.numpy as jnp
from jax import lax
from jax.experimental import pallas as pl
from jax.experimental.pallas import tpu as pltpu
from jax.sharding import PartitionSpec as P

SWEEPS = 3
STEPS = 5
FAR = 4
LOW_EIG = 0.3
HIGH_EIG = 2.2
CENTER = (HIGH_EIG + LOW_EIG) / 2.0
HALF = (HIGH_EIG - LOW_EIG) / 2.0
LANES = 128
PACK = 16
LAYERS = 10
HALO_LAYERS = 3
F32 = jnp.float32
BF16 = jnp.bfloat16
VMEM = pltpu.VMEM


def gather(rows, index, axis):
    numbers = lax.GatherDimensionNumbers(
        offset_dims=(),
        collapsed_slice_dims=(axis,),
        start_index_map=(axis,),
        operand_batching_dims=(1 - axis,),
        start_indices_batching_dims=(1 - axis,),
    )
    return lax.gather(
        rows,
        index[..., None],
        numbers,
        (1, 1),
        mode=lax.GatherScatterMode.PROMISE_IN_BOUNDS,
    )


def lane_gather(rows, index):
    return gather(rows, index, 1)


def row_gather(rows, index):
    return gather(rows, index, 0)


def sorting_network(count):
    pairs = []
    span = 1
    while span < count:
        gap = span
        while gap >= 1:
            for j in range(gap % span, count - gap, 2 * gap):
                for i in range(min(gap, count - j - gap)):
                    if (i + j) // (2 * span) == (i + j + gap) // (2 * span):
                        pairs.append((i + j, i + j + gap))
            gap //= 2
        span *= 2
    return pairs


def sort_planes(planes):
    planes = list(planes)
    for i, j in sorting_network(len(planes)):
        planes[i], planes[j] = (
            jnp.minimum(planes[i], planes[j]),
            jnp.maximum(planes[i], planes[j]),
        )
    return planes


def call(kernel, out, inputs, scratch=(), us=1.0, spaces={}, limit=16):
    return pl.pallas_call(
        kernel,
        out_shape=out,
        in_specs=[
            pl.BlockSpec(memory_space=spaces.get(i, VMEM)) for i in range(len(inputs))
        ],
        out_specs=jax.tree.map(
            lambda _: pl.BlockSpec(memory_space=VMEM), out
        ),
        scratch_shapes=list(scratch),
        cost_estimate=pl.CostEstimate(
            flops=int(us * 1.0e9), transcendentals=0, bytes_accessed=int(us * 1.0e6)
        ),
        compiler_params=pltpu.CompilerParams(vmem_limit_bytes=limit * 1024 * 1024),
    )(*inputs)


def rows_of(ref, lead, group):
    return ref[lead + (slice(group * LANES, (group + 1) * LANES),)]


def restrict_kernel(*refs):
    sources = refs[:2]
    dense_residual, rhs = refs[2:4]
    residual, aggregate, semaphores = refs[4:]
    copies = [
        pltpu.make_async_copy(source, target, semaphores.at[i])
        for i, (source, target) in enumerate(zip(sources, (residual, aggregate)))
    ]
    for copy in copies:
        copy.start()
    copies[0].wait()
    for g in range(dense_residual.shape[1]):
        for e in range(3):
            dense_residual[e, g : g + 1, :] = residual[
                e : e + 1, g * LANES : (g + 1) * LANES
            ]
    copies[1].wait()
    restrict(dense_residual, aggregate, rhs)


def first_kernel(dense_residual, dinv, couple, dense_dinv, smooth, message):
    groups = smooth.shape[1]
    coarse_groups = message.shape[1]
    for g in range(groups):
        lanes = slice(g * LANES, (g + 1) * LANES)
        for e in range(3):
            for c in range(3):
                dense_dinv[c, e, g : g + 1, :] = dinv[c, e : e + 1, lanes]
    for g in range(coarse_groups):
        lanes = slice(g * LANES, (g + 1) * LANES)
        for k in range(4):
            message[3 + k, g : g + 1, :] = couple[k : k + 1, lanes].astype(BF16)
    for c in range(3):
        total = dense_dinv[c, 0] * dense_residual[0]
        for e in range(1, 3):
            total = total + dense_dinv[c, e] * dense_residual[e]
        total = total * (1.0 / CENTER)
        smooth[c] = total
        message[c] = total.astype(BF16)


def restrict(residual, aggregate, out):
    groups = residual.shape[1]
    bins = out.shape[1]
    agg = aggregate[...] & (bins * LANES - 1)
    low = agg & (LANES - 1)
    high = agg >> 7
    batch = 8
    row16 = lax.broadcasted_iota(jnp.int32, (PACK, LANES), 0).astype(jnp.int16)
    one, zero = jnp.ones((PACK, LANES), BF16), jnp.zeros((PACK, LANES), BF16)

    def wide(row, kind):
        return jnp.broadcast_to(row, (PACK, LANES)).astype(kind)

    total = jnp.zeros((6 * bins, LANES), F32)
    for block in range(groups // batch):
        onehot, spread = [], []
        for g in range(block * batch, (block + 1) * batch):
            lane = wide(low[g : g + 1], jnp.int16)
            line = wide(high[g : g + 1], jnp.int16)
            onehot.append(
                jnp.concatenate(
                    [
                        jnp.where(lane == row16 + jnp.int16(first), one, zero)
                        for first in range(0, LANES, PACK)
                    ],
                    axis=0,
                )
            )
            chosen = [line == row16 + jnp.int16(first) for first in range(0, bins, PACK)]
            column = []
            for c in range(3):
                value = residual[c, g : g + 1, :]
                upper = value.astype(BF16).astype(F32)
                for part in (upper, value - upper):
                    part = wide(part, BF16)
                    column += [jnp.where(mask, part, zero) for mask in chosen]
            spread.append(jnp.concatenate(column, axis=0))
        total = total + lax.dot_general(
            jnp.concatenate(spread, axis=1),
            jnp.concatenate(onehot, axis=1),
            (((1,), (1,)), ((), ())),
            preferred_element_type=F32,
        )
    for c in range(3):
        first = 2 * c * bins
        out[c] = total[first : first + bins] + total[first + bins : first + 2 * bins]


def spread_max(values):
    top = jnp.max(jnp.max(values, axis=1, keepdims=True), axis=0, keepdims=True)
    return jnp.broadcast_to(top, values.shape)


def prepare_kernel(
    col, picks, start, halo_start, spot, rank, most, columns, halo_columns, flip
):
    bonds_of = col.shape[0]
    groups = col.shape[1] // LANES
    stride = bonds_of + 1

    def eight_tiles(block, carry):
        best, halo_best = carry

        def lanes_of(t):
            return pl.ds(pl.multiple_of((block * 8 + t) * LANES, LANES), LANES)

        for t in range(8):
            flip[pl.ds(t * stride, bonds_of), :] = col[:, lanes_of(t)]
        keys = []
        for k in range(bonds_of):
            c = flip[pl.ds(k, 8, stride=stride), :]
            keys.append(((c >> 8) << 13) | (k << 8) | (c & 255))
        keys = sort_planes(keys)
        pairs = [key >> 13 for key in keys]
        ranks = [jnp.zeros((8, LANES), jnp.int32)]
        for k in range(1, bonds_of):
            ranks.append(jnp.where(pairs[k] == pairs[k - 1], ranks[k - 1] + 1, 0))
        back = []
        here = jnp.zeros((8, LANES), jnp.int32)
        for k in range(bonds_of):
            local = pairs[k] < PACK
            here = jnp.maximum(here, jnp.where(local, ranks[k], 0))
            halo_best = jnp.maximum(halo_best, jnp.where(local, 0, ranks[k]))
            code = jnp.where(
                local,
                (ranks[k] << 4) | pairs[k],
                ((ranks[k] >> 2) << 4) | ((ranks[k] & 3) << 2) | ((pairs[k] - PACK) + (32 << 4)),
            )
            back.append((((keys[k] >> 8) & 31) << 10) | code)
            flip[pl.ds(k, 8, stride=stride), :] = keys[k]
        row = lax.broadcasted_iota(jnp.int32, (PACK, LANES), 0)
        for t in range(8):
            halves = [flip[pl.ds(t * stride + h * PACK, PACK), :] for h in range(2)]
            for h in range(2):
                picks[h * PACK : (h + 1) * PACK, lanes_of(t)] = (halves[h] & 255).astype(jnp.int16)
            first, second = [(x >> 13).astype(jnp.int16) for x in halves]
            for target, pair, extra in (
                (start, row.astype(jnp.int16), None),
                (halo_start, (PACK + (row & 3)).astype(jnp.int16), (row >> 2).astype(jnp.int16)),
            ):
                place = jnp.zeros((PACK, LANES), jnp.int16)
                for step in (16, 8, 4, 2, 1, 1):
                    probe = place + jnp.int16(step - 1)
                    inner = probe & jnp.int16(PACK - 1)
                    value = jnp.where(
                        probe < PACK, row_gather(first, inner), row_gather(second, inner)
                    )
                    place = jnp.where(value < pair, place + jnp.int16(step), place)
                place = place if extra is None else place + extra
                target[:, lanes_of(t)] = place
                chosen = [(x & 255).astype(jnp.int16) for x in halves]
                if extra is None:
                    for m in range(LAYERS):
                        columns[m * PACK : (m + 1) * PACK, lanes_of(t)] = picked(
                            place + jnp.int16(m), chosen
                        )
                else:
                    for v in range(HALO_LAYERS):
                        halo_columns[v * PACK : (v + 1) * PACK, lanes_of(t)] = picked(
                            place + jnp.int16(4 * v), chosen
                        )
        back = sort_planes(back)
        for k in range(bonds_of):
            flip[pl.ds(k, 8, stride=stride), :] = back[k] & 1023
        for t in range(8):
            for h in range(2):
                code = flip[pl.ds(t * stride + h * PACK, PACK), :]
                rows = slice(h * PACK, (h + 1) * PACK)
                spot[rows, lanes_of(t)] = (code & 15).astype(jnp.int16)
                rank[rows, lanes_of(t)] = (code >> 4).astype(jnp.int16)
        most[pl.ds(pl.multiple_of(block * 8, 8), 8), :] = spread_max(here)
        return jnp.maximum(best, here), halo_best

    zero = jnp.zeros((8, LANES), jnp.int32)
    best, halo_best = lax.fori_loop(0, groups // 8, eight_tiles, (zero, zero))
    most[groups : groups + 8, :] = spread_max(best)
    most[groups + 8 :, :] = spread_max(halo_best) >> 2


def picked(place, picks):
    inner = place & jnp.int16(PACK - 1)
    return jnp.where(place < PACK, row_gather(picks[0], inner), row_gather(picks[1], inner))


def layer(column, even, odd):
    lane = column & jnp.int16(LANES - 1)
    second = column >= LANES
    return [
        jnp.where(second, lane_gather(odd[e], lane), lane_gather(even[e], lane))
        for e in range(3)
    ]


def put_back(values, number, spots, ranks, out):
    for h in range(2):
        hit = ranks[h] == number
        for e in range(3):
            out[h][e] = jnp.where(hit, row_gather(values[e], spots[h]), out[h][e])


def halves_of(ref, lanes):
    return [ref[h * PACK : (h + 1) * PACK, lanes] for h in range(2)]


def tiles_per_step(tiles):
    return max(n for n in range(1, 17) if tiles % n == 0)


def splat(number):
    return jnp.full((PACK, LANES), number, jnp.int32).astype(jnp.int16)


def local_kernel(
    smooth, picks, start, spot, rank, most, columns, out, *, first, tiles, unroll
):
    even = [smooth[e, pl.ds(0, PACK, stride=2), :].astype(BF16) for e in range(3)]
    odd = [smooth[e, pl.ds(1, PACK, stride=2), :].astype(BF16) for e in range(3)]

    def some_tiles(t, carry):
        for u in range(unroll):
            source = pl.ds(pl.multiple_of((first + t * unroll + u) * LANES, LANES), LANES)
            target = pl.ds(pl.multiple_of((t * unroll + u) * LANES, LANES), LANES)
            spots, ranks = halves_of(spot, source), halves_of(rank, source)
            found = [[jnp.zeros((PACK, LANES), BF16)] * 3 for h in range(2)]
            for m in range(LAYERS):
                values = layer(columns[m * PACK : (m + 1) * PACK, source], even, odd)
                put_back(values, jnp.int16(m), spots, ranks, found)
            for h in range(2):
                for e in range(3):
                    out[e, h * PACK : (h + 1) * PACK, target] = found[h][e]
        return carry

    lax.fori_loop(0, tiles // unroll, some_tiles, 0)

    @pl.when(most[smooth.shape[1], 0] >= LAYERS)
    def _():
        def eight_tiles(block, carry):
            def more(m, inner):
                number = splat(m)
                for t in range(8):
                    tile = block * 8 + t
                    source = pl.ds(pl.multiple_of((first + tile) * LANES, LANES), LANES)
                    target = pl.ds(pl.multiple_of(tile * LANES, LANES), LANES)
                    found = [
                        [out[e, h * PACK : (h + 1) * PACK, target] for e in range(3)]
                        for h in range(2)
                    ]
                    column = picked(start[:, source] + number, halves_of(picks, source))
                    values = layer(column, even, odd)
                    put_back(
                        values, number, halves_of(spot, source), halves_of(rank, source), found
                    )
                    for h in range(2):
                        for e in range(3):
                            out[e, h * PACK : (h + 1) * PACK, target] = found[h][e]
                return inner

            lax.fori_loop(LAYERS, most[first + block * 8, 0] + 1, more, 0)
            return carry

        lax.fori_loop(0, tiles // 8, eight_tiles, 0)


def dense_solve(matrix, vector):
    solved = []
    for c in range(3):
        total = matrix[c, 0] * vector[0]
        for e in range(1, 3):
            total = total + matrix[c, e] * vector[e]
        solved.append(total)
    return solved


def sideways(x):
    lines = x.shape[0]
    lane = lax.broadcasted_iota(jnp.int32, x.shape, 1)
    right = pltpu.roll(x, 1, 1)
    right = jnp.where(lane == 0, pltpu.roll(right, 1, 0), right)
    left = pltpu.roll(x, LANES - 1, 1)
    left = jnp.where(lane == LANES - 1, pltpu.roll(left, lines - 1, 0), left)
    return right, left


def inside_masks(shape):
    lane = lax.broadcasted_iota(jnp.int32, shape, 1)
    line = lax.broadcasted_iota(jnp.int32, shape, 0)
    return (
        jnp.logical_or(lane > 0, line > 0),
        jnp.logical_or(lane < LANES - 1, line < shape[0] - 1),
    )


def halo_kernel(*refs, stage, sizes, scale_old, scale_new, subs):
    (place, most, picks, halo_start, halo_columns, spot, rank, ghost) = refs[:8]
    (outer, inner, residual, dinv, smooth, update, bonds) = refs[8:15]
    pieces = len(sizes)
    local_found = refs[15 : 15 + pieces]
    refs = refs[15 + pieces :]
    if stage == 0:
        rhs, arrived, coarse_dinv = refs[:3]
        new_smooth, new_update, base, out_outer, out_inner = refs[3:8]
        refs = refs[8:]
    elif stage == 1:
        first_outer, first_inner, base, couple_own = refs[:4]
        new_smooth, new_update, out_outer, out_inner, far_next, far_prev = refs[4:10]
        refs = refs[10:]
    else:
        (new_smooth,) = refs[:1]
        refs = refs[1:]
    applied, other, partial = refs
    groups = smooth.shape[1]
    if stage == 0:
        vector = [rhs[e] + arrived[e] for e in range(3)]
        coarse_groups = base.shape[1]
        for c in range(3):
            for g in range(coarse_groups):
                lanes = slice(g * LANES, (g + 1) * LANES)
                total = coarse_dinv[c, 0:1, lanes] * vector[0][g : g + 1]
                for e in range(1, 3):
                    total = total + coarse_dinv[c, e : e + 1, lanes] * vector[e][g : g + 1]
                base[c, g : g + 1, :] = total
        for c in range(3):
            row = base[c].astype(BF16)
            out_outer[3 + c] = row
            out_inner[3 + c] = row
        out_outer[6:10] = inner[3:7]
        out_inner[6:10] = outer[3:7]
    elif stage == 1:
        out_outer[3:6] = inner[3:6]
        out_inner[3:6] = outer[3:6]
        me = jnp.concatenate([place[...]] * (base.shape[1] // 8), axis=0)
        even = (me & 1) == 0
        links = [couple_own[3 + k].astype(F32) for k in range(4)]
        links[0] = jnp.where(me > 0, links[0], 0.0)
        links[1] = jnp.where(me < subs - 1, links[1], 0.0)
        for k, mask in zip((2, 3), inside_masks(me.shape)):
            links[k] = jnp.where(mask, links[k], 0.0)
        for c in range(3):
            own = base[c]
            outer_row, inner_row = outer[3 + c].astype(F32), inner[3 + c].astype(F32)
            below = jnp.where(even, outer_row, inner_row)
            above = jnp.where(even, inner_row, outer_row)
            right, left = sideways(own)
            iterate = own + (
                links[0] * below + links[1] * above + links[2] * right + links[3] * left
            )
            for message, beyond in ((far_next, above), (far_prev, below)):
                message[c] = own.astype(BF16)
                message[3 + c] = iterate.astype(BF16)
                message[6 + c] = beyond.astype(BF16)
        for k in range(4):
            outer_row = first_outer[3 + k].astype(F32)
            inner_row = first_inner[3 + k].astype(F32)
            far_next[9 + k] = jnp.where(even, inner_row, outer_row).astype(BF16)
            far_prev[9 + k] = jnp.where(even, outer_row, inner_row).astype(BF16)
    wanted = ghost[...]
    half = wanted.shape[0] // 2
    low = wanted & (LANES - 1)
    high = wanted >> 7
    upper = jnp.where(lax.broadcasted_iota(jnp.int32, wanted.shape, 0) < half, 1, 0)
    from_outer = (upper ^ (place[...] & 1)) == 1
    found = [jnp.zeros(wanted.shape, F32)] * 3
    for e in range(3):
        applied[e] = outer[e].astype(F32)
        other[e] = inner[e].astype(F32)
    for g in range(groups):
        chosen = high == g
        for e in range(3):
            rows = jnp.where(
                from_outer,
                jnp.broadcast_to(applied[e, g : g + 1, :], wanted.shape),
                jnp.broadcast_to(other[e, g : g + 1, :], wanted.shape),
            )
            found[e] = jnp.where(chosen, lane_gather(rows, low), found[e])
    pair = (lax.broadcasted_iota(jnp.int32, wanted.shape, 0) & 3) * 2

    def four_times(rows):
        return jnp.concatenate([rows, rows], axis=0).astype(BF16)

    even = [four_times(row_gather(found[e], pair)) for e in range(3)]
    odd = [four_times(row_gather(found[e], pair + 1)) for e in range(3)]

    def apply_tile(tile, values):
        here = pl.ds(pl.multiple_of(tile * LANES, LANES), LANES)
        totals = []
        for c in range(3):
            total = jnp.zeros((PACK, LANES), F32)
            for h in range(2):
                for e in range(3):
                    block = bonds[c, e, h * PACK : (h + 1) * PACK, here].astype(F32)
                    total = total + block * values[h][e].astype(F32)
            totals.append(total[:8] + total[8:])
        return totals

    for piece, part in enumerate(local_found):
        first = sum(sizes[:piece])
        unroll = tiles_per_step(sizes[piece])

        def some_tiles(t, carry, part=part, first=first, unroll=unroll):
            for u in range(unroll):
                there = pl.ds(pl.multiple_of((t * unroll + u) * LANES, LANES), LANES)
                tile = first + t * unroll + u
                here = pl.ds(pl.multiple_of(tile * LANES, LANES), LANES)
                spots, ranks = halves_of(spot, here), halves_of(rank, here)
                values = [
                    [part[e, h * PACK : (h + 1) * PACK, there] for e in range(3)]
                    for h in range(2)
                ]
                for v in range(HALO_LAYERS):
                    row = layer(halo_columns[v * PACK : (v + 1) * PACK, here], even, odd)
                    put_back(row, jnp.int16(32 + v), spots, ranks, values)
                totals = apply_tile(tile, values)
                for c in range(3):
                    partial[c, pl.ds(pl.multiple_of(tile * 8, 8), 8), :] = totals[c]
            return carry

        lax.fori_loop(0, sizes[piece] // unroll, some_tiles, 0)

    last_layer = most[groups + 8, 0]

    @pl.when(last_layer >= HALO_LAYERS)
    def _():
        def one_tile(tile, carry):
            here = pl.ds(pl.multiple_of(tile * LANES, LANES), LANES)

            def more(v, flat):
                values = [list(flat[:3]), list(flat[3:])]
                column = picked(halo_start[:, here] + splat(4 * v), halves_of(picks, here))
                row = layer(column, even, odd)
                put_back(row, splat(32 + v), halves_of(spot, here), halves_of(rank, here), values)
                return tuple(values[0] + values[1])

            empty = (jnp.zeros((PACK, LANES), BF16),) * 6
            flat = lax.fori_loop(HALO_LAYERS, last_layer + 1, more, empty)
            totals = apply_tile(tile, [flat[:3], flat[3:]])
            for c in range(3):
                rows = pl.ds(pl.multiple_of(tile * 8, 8), 8)
                partial[c, rows, :] = partial[c, rows, :] + totals[c]
            return carry

        lax.fori_loop(0, groups, one_tile, 0)

    remainder = []
    for e in range(3):
        total = partial[e, pl.ds(0, groups, stride=8), :]
        for row in range(1, 8):
            total = total + partial[e, pl.ds(row, groups, stride=8), :]
        remainder.append(residual[e] - smooth[e] - total)
    solved = dense_solve(dinv, remainder)
    for c in range(3):
        change = scale_old * update[c] + scale_new * solved[c]
        total = smooth[c] + change
        new_smooth[c] = total
        if stage < SWEEPS - 1:
            new_update[c] = change
            out_outer[c] = total.astype(BF16)
            out_inner[c] = total.astype(BF16)


def coarse_kernel(*refs, subs):
    (place, base, own_couple) = refs[:3]
    first, second, third = refs[3:5], refs[5:7], refs[7:9]
    far_after, far_before, aggregate, smooth = refs[9:13]
    out, field, links, kept = refs[13:]
    groups = base.shape[1]
    me = jnp.concatenate([place[...]] * (groups // 8), axis=0)
    even = (me & 1) == 0

    def valid(row):
        if row < 0:
            return jnp.where(me + row >= 0, 1.0, 0.0)
        return jnp.where(me + row < subs, 1.0, 0.0)

    def from_after(pair, start):
        return lambda i: jnp.where(
            even, pair[0][start + i].astype(F32), pair[1][start + i].astype(F32)
        )

    def from_before(pair, start):
        return from_after((pair[1], pair[0]), start)

    def plain(ref, start):
        return lambda i: ref[start + i].astype(F32)

    base_rows = {
        -4: plain(far_after, 0),
        -3: plain(far_after, 6),
        -2: from_after(third, 3),
        -1: from_after(second, 3),
        1: from_before(second, 3),
        2: from_before(third, 3),
        3: plain(far_before, 6),
        4: plain(far_before, 0),
    }
    link_rows = {
        -3: plain(far_after, 9),
        -2: from_after(second, 6),
        -1: from_after(first, 3),
        1: from_before(first, 3),
        2: from_before(second, 6),
        3: plain(far_before, 9),
    }
    for g in range(groups):
        for k in range(4):
            links[FAR - 1, k, g : g + 1, :] = own_couple[
                k : k + 1, g * LANES : (g + 1) * LANES
            ]
    for row, read in link_rows.items():
        for k in range(4):
            links[row + FAR - 1, k] = read(k) * valid(row)
    for k, mask in zip((2, 3), inside_masks(me.shape)):
        for row in range(2 * FAR - 1):
            links[row, k] = jnp.where(mask, links[row, k], 0.0)
    for c in range(3):
        field[0, FAR, c] = base[c]
        for row, read in base_rows.items():
            field[0, row + FAR, c] = read(c) * valid(row)
        field[1, 0, c] = far_after[3 + c].astype(F32) * valid(-FAR)
        field[1, 2 * FAR, c] = far_before[3 + c].astype(F32) * valid(FAR)
        for row in range(2 * FAR + 1):
            kept[row, c] = field[0, row, c]
    for step in range(STEPS):
        old, new = step % 2, (step + 1) % 2
        reach = min(STEPS - 1 - step, FAR - 1)
        for row in range(-reach, reach + 1):
            spot = row + FAR
            weights = [links[spot - 1, k] for k in range(4)]
            for c in range(3):
                right, left = sideways(field[old, spot, c])
                field[new, spot, c] = kept[spot, c] + (
                    weights[0] * field[old, spot - 1, c]
                    + weights[1] * field[old, spot + 1, c]
                    + weights[2] * right
                    + weights[3] * left
                )
    final = STEPS % 2
    agg = aggregate[...] & (groups * LANES - 1)
    for block in range(agg.shape[0] // 8):
        index = agg[block * 8 : (block + 1) * 8]
        low = index & (LANES - 1)
        high = index >> 7
        found = [jnp.zeros((8, LANES), F32)] * 3
        for g in range(groups):
            chosen = high == g
            for c in range(3):
                rows = jnp.broadcast_to(field[final, FAR, c, g : g + 1, :], (8, LANES))
                found[c] = jnp.where(chosen, lane_gather(rows, low), found[c])
        for c in range(3):
            result = smooth[c, block * 8 : (block + 1) * 8, :] + found[c]
            for r in range(8):
                lanes = slice((block * 8 + r) * LANES, (block * 8 + r + 1) * LANES)
                out[c : c + 1, lanes] = result[r : r + 1]


def shifted(value, steps):
    count = lax.axis_size("sub")
    return lax.ppermute(value, "sub", [(i, (i + steps) % count) for i in range(count)])


def across_chips(value):
    count = lax.axis_size("sub")
    pairs = [(i, (i + 1) % count) for i in range(1, count, 2)]
    return lax.ppermute(value, "sub", pairs + [(j, i) for i, j in pairs])


def within_chip(value):
    count = lax.axis_size("sub")
    pairs = [(i, i + 1) for i in range(0, count, 2)]
    return lax.ppermute(value, "sub", pairs + [(j, i) for i, j in pairs])


def exchanged_by_pairs(outer, inner):
    return across_chips(outer), within_chip(inner)


def local_pass(smooth, lists, first, tiles, us=None):
    unroll = tiles_per_step(tiles)
    return call(
        functools.partial(local_kernel, first=first, tiles=tiles, unroll=unroll),
        jax.ShapeDtypeStruct((3, lists[0].shape[0], tiles * LANES), BF16),
        (smooth, *lists),
        us=us or 0.12 * tiles,
    )


def body(
    fine_residual, bonds, bond_col, ghost_points, fine_dinv, aggregate, coarse_dinv, coarse_couple
):
    points = fine_residual.shape[1]
    groups = points // LANES
    bonds_of = bond_col.shape[0]
    per_group = coarse_dinv.shape[2]
    coarse_groups = per_group // LANES
    assert per_group & (per_group - 1) == 0
    sub = lax.axis_index("sub")
    doms = lax.axis_size("dom")
    ghost = ghost_points.reshape(-1, LANES)
    agg = aggregate.reshape(groups, LANES)
    relaid = bonds.transpose(1, 2, 0, 3)
    sds = jax.ShapeDtypeStruct
    field = sds((3, groups, LANES), F32)
    coarse_field = sds((3, coarse_groups, LANES), F32)

    def message(rows):
        return sds((rows, groups, LANES), BF16)

    residual, rhs = call(
        restrict_kernel,
        (field, coarse_field),
        tuple(pltpu.with_memory_space_constraint(x, pltpu.HBM) for x in (fine_residual, agg)),
        scratch=[
            VMEM(fine_residual.shape, F32),
            VMEM(agg.shape, jnp.int32),
            pltpu.SemaphoreType.DMA((2,)),
        ],
        us=1.6,
        spaces={0: pltpu.HBM, 1: pltpu.HBM},
    )
    dinv, smooth, packed = call(
        first_kernel,
        (sds((3, 3, groups, LANES), F32), field, message(7)),
        (residual, fine_dinv, coarse_couple),
        us=0.8,
    )
    update = smooth
    own_packed = packed
    place = jnp.full((8, LANES), sub, jnp.int32)
    def exchanged(value, step):
        return lax.ppermute(value, "dom", [(i, i ^ step) for i in range(doms)])

    assert doms == 8
    arrived = exchanged(rhs, 1)
    later_col, rhs = lax.optimization_barrier((bond_col, rhs))

    def shorts(rows):
        return sds((rows, points), jnp.int16)

    picks, start, halo_start, spot, rank, most, columns, halo_columns = call(
        prepare_kernel,
        (
            shorts(bonds_of),
            shorts(PACK),
            shorts(PACK),
            shorts(bonds_of),
            shorts(bonds_of),
            sds((groups + 16, LANES), jnp.int32),
            shorts(LAYERS * PACK),
            shorts(HALO_LAYERS * PACK),
        ),
        (later_col,),
        scratch=[VMEM((8 * (bonds_of + 2), LANES), jnp.int32)],
        us=2.5,
    )
    start, rhs = lax.optimization_barrier((start, rhs))
    rhs = rhs + arrived
    packed, start, rhs = lax.optimization_barrier((packed, start, rhs))
    arrived = exchanged(rhs, 2)
    first_outer = across_chips(packed)
    early = local_pass(smooth, (picks, start, spot, rank, most, columns), 0, 8)
    rhs, early = lax.optimization_barrier((rhs, early))
    rhs = rhs + arrived
    packed_inner, start, rhs = lax.optimization_barrier((packed, start, rhs))
    arrived = exchanged(rhs, 6)
    first = arrived_sides = (first_outer, within_chip(packed_inner))

    factor = HALF / CENTER
    for stage in range(SWEEPS):
        factor_new = 1.0 / (2.0 * CENTER / HALF - factor)
        lists = (picks, start, spot, rank, most, columns)
        if stage == 0:
            sizes = (8, groups - 8)
            found = [early, local_pass(smooth, lists, *sizes)]
        elif stage == 1:
            sizes = (groups,)
            found = [local_pass(smooth, lists, 0, groups)]
        else:
            sizes = (groups // 2,) * 2
            found = [local_pass(smooth, lists, 0, sizes[0], us=0.2)]
            far_next, far_prev, start, found[0] = lax.optimization_barrier(
                (far_next, far_prev, start, found[0])
            )
            far_after = shifted(far_next, 4)
            far_before = shifted(far_prev, -4)
            lists = (picks, start, spot, rank, most, columns)
            found.append(local_pass(smooth, lists, *sizes, us=0.2))
        inputs = [place, most, picks, halo_start, halo_columns, spot, rank, ghost]
        inputs += arrived_sides
        inputs += [residual, dinv, smooth, update, relaid, *found]
        if stage == 0:
            inputs += [rhs, arrived, coarse_dinv]
            outs = (field, field, coarse_field, message(10), message(10))
        elif stage == 1:
            inputs += [*first, base, own_packed]
            outs = (field, field, message(6), message(6), message(13), message(13))
        else:
            outs = (field,)
        result = call(
            functools.partial(
                halo_kernel,
                stage=stage,
                sizes=sizes,
                scale_old=factor_new * factor,
                scale_new=2.0 * factor_new / HALF,
                subs=lax.axis_size("sub"),
            ),
            outs,
            inputs,
            scratch=[VMEM((3, groups, LANES), F32)] * 2 + [VMEM((3, 8 * groups, LANES), F32)],
            us=2.5,
        )
        factor = factor_new
        if stage == 0:
            smooth, update, base, outer, inner = result
            second = arrived_sides = exchanged_by_pairs(outer, inner)
        elif stage == 1:
            smooth, update, outer, inner, far_next, far_prev = result
            third = arrived_sides = exchanged_by_pairs(outer, inner)
        else:
            (smooth,) = result
    return call(
        functools.partial(coarse_kernel, subs=lax.axis_size("sub")),
        sds((3, points), F32),
        (
            place,
            base,
            coarse_couple,
            *first,
            *second,
            *third,
            far_after,
            far_before,
            agg,
            smooth,
        ),
        scratch=[
            VMEM((2, 2 * FAR + 1, 3, coarse_groups, LANES), F32),
            VMEM((2 * FAR - 1, 4, coarse_groups, LANES), F32),
            VMEM((2 * FAR + 1, 3, coarse_groups, LANES), F32),
        ],
        us=2.0,
    )


def solution(mesh):
    placed = (
        P(None, ("dom", "sub")),
        P(None, None, None, ("dom", "sub")),
        P(None, ("dom", "sub")),
        P(("dom", "sub"), None, None),
        P(None, None, ("dom", "sub")),
        P(("dom", "sub")),
        P(None, None, "sub"),
        P(None, "sub"),
    )
    return jax.shard_map(
        body, mesh=mesh, in_specs=placed, out_specs=P(None, ("dom", "sub")), check_vma=False
    )
```
